256 devices in a mesh: cells: 32 (over x_lo, z, core), orb: 8 (over x_hi, y).
Axes of the slice: x: 4 (x_hi: 2, x_lo: 2; x = x_hi * 2 + x_lo), y: 4, z: 8, core: 2. Of those that a mesh axis runs over, the one named last changes fastest.
Arguments:
- orbitals: float32 [69312, 1024], P('cells', 'orb'), may hold values from -6 to 6
- occupations: float32 [1024], P('orb'), may hold values from 0.4 to 2.5
- external: float32 [69312], P('cells'), may hold values from -3 to 3
- core_density: float32 [69312], P('cells'), may hold values from 1 to 300
- cell_scale: float32 [288], P('cells'), may hold values from 0.5 to 2
- stiffness: float32 [343, 343], replicated, may hold values from -1 to 7, as said below
- touched_atom: int32 [192], replicated, may hold values from 0 to 63, as said below
- touched_cells: int32 [192, 1], P('cells'), may hold values from 0 to 8
- projectors: float32 [192, 1, 18, 343], P('cells'), may hold values from -1.2 to 1.2
- coupling: float32 [64, 18, 18], replicated, may hold values from -3 to 3, as said below
- atom_owner: int32 [64, 1], replicated, may hold values from 0 to 31; in each aligned block of 64 rows (0 to 63, 64 to 127, ...) at most 5 rows name the same one
Outputs:
- final_orbitals: float32 [69312, 1024], P('cells', 'orb')
- rayleigh: float32 [1024], P('orb')
- owned_projections: float32 [160, 18, 1024], P('cells', None, 'orb')
The draws below stay inside these ranges and needn't reach their ends.
Inputs may be any that keep to these rules, and one draw needn't show every extreme that they name: `stiffness`: symmetric. `coupling`: each atom's matrix is symmetric. `touched_atom`: the 6 atoms of one device are distinct, and atom a's home index of cells, a // 2, lies within 2 of the device along the periodic cells axis. `touched_cells`: the cells in one row are distinct. `atom_owner`: no owner has more than 5 atoms, and some owner has exactly 5.
All inputs are finite; a program needn't handle non-finite values.
Results may differ from the reference program's by a relative error of at most 0.00011.
Values sent between devices are 32-bit elements; how exact they have to be, the bound alone decides.
A program may use at most 128 MiB of HBM per device.

```python
import math
import jax
import jax.numpy as jnp
import numpy as np
from jax import lax

DEG = 6
EDGE = 7
CELL_NODES = 343
SIDE = 3
CELL_DEV = 9
CELLS = 288
PLANE = 361
NODES = 69312
ORB = 1024
PROJ = 18
ATOM_DEV = 2
ATOMS = 64
REACH = 2
TOUCH_DEV = 6
PATCH_AT = 1
OWN_CAP = 5
ITERS = 1
N_CELLS = 32


def draw_stiffness(key, part):
    first = jax.random.fold_in(key, 11)
    second = jax.random.fold_in(key, 12)
    noise = jax.random.normal(first, (CELL_NODES, CELL_NODES), jnp.float32)
    symmetric = (noise + noise.T) / jnp.sqrt(2.0 * CELL_NODES)
    diagonal = jax.random.uniform(second, (CELL_NODES,), jnp.float32, 2.5, 4.0)
    return symmetric + jnp.diag(diagonal)


def draw_coupling(key, part):
    first = jax.random.fold_in(key, 21)
    noise = jax.random.normal(first, (ATOMS, PROJ, PROJ), jnp.float32)
    return (noise + jnp.swapaxes(noise, 1, 2)) / jnp.sqrt(2.0 * PROJ)


def draw_occupations(key, part):
    first = jax.random.fold_in(key, 31)
    position = jnp.arange(ORB, dtype=jnp.float32) / (ORB - 1)
    jitter = jnp.exp(jax.random.uniform(first, (ORB,), jnp.float32, -0.18, 0.18))
    return (2.0 - 1.4 * position) * jitter


def draw_touched_atom(key, part):
    first = jax.random.fold_in(key, 41)
    candidates = (2 * REACH + 1) * ATOM_DEV

    def one_device(device):
        order = jax.random.permutation(jax.random.fold_in(first, device), candidates)
        chosen = order[:TOUCH_DEV]
        home = (device + chosen // ATOM_DEV - REACH) % N_CELLS
        return (home * ATOM_DEV + chosen % ATOM_DEV).astype(jnp.int32)
    return jax.vmap(one_device)(jnp.arange(N_CELLS, dtype=jnp.int32)).reshape(-1)


def steps_of(own_key, shape, shards, least, top_value):
    loudness, own = 1.0, jax.random.fold_in(own_key, 6)
    for dim, parts in shards:
        steps = jnp.exp(jax.random.uniform(jax.random.fold_in(own, dim), (parts,), jnp.float32, least / len(shards), top_value / len(shards)))
        loudness = loudness * jnp.repeat(steps, shape[dim] // parts).reshape([-1 if axis == dim else 1 for axis in range(len(shape))])
    return loudness


def distinct(rng, rows, amount, top, lift):
    sequence = jax.random.permutation(jax.random.fold_in(rng, 1), amount)
    pull = sequence
    for power in range(3):
        pull = pull * pull // amount
    pull = pull * lift // amount
    tickets = jax.random.randint(jax.random.fold_in(rng, 2), (rows, amount), 0, 4096) + pull
    holders = jax.random.permutation(jax.random.fold_in(rng, 3), rows)[jnp.arange(amount) % rows]
    tickets = jnp.where(jnp.arange(rows)[:, None] == holders[None, :], 1 << 14, tickets)
    merit = tickets * amount + jnp.arange(amount)
    return lax.top_k(merit.astype(jnp.int32), top)[1].astype(jnp.int32)


def deal_out(stream_key, own, number, rows, count, top, most, slope):
    sequence = jax.random.permutation(stream_key, count)
    packed, common = shares(count, rows * top, most, slope, True), shares(count, rows * top, most, slope, False)
    places = jnp.arange(count)

    def named(tallies, turn):
        used = int((tallies > 0).sum())
        fixed = max(1, used // 4)
        moved = fixed + (places - fixed + turn * (used - fixed)) % max(1, count - fixed)
        return jnp.zeros((count,), jnp.int32).at[sequence[jnp.where(places < fixed, places, moved)]].set(jnp.asarray(tallies, jnp.int32))

    tallies = jnp.where(number % 4 == 0, named(packed, number // 4), named(common, number - number // 4 - 1))
    mixed = jax.random.permutation(jax.random.fold_in(own, 3), count)
    source_of, taker = mixed[0:count // 2 * 2:2], mixed[1:count // 2 * 2:2]
    slack = jnp.minimum(tallies[source_of] - 1, most - tallies[taker]) // 2
    slack = jnp.where((source_of == sequence[0]) | (taker == sequence[0]) | (tallies[taker] == 0), 0, jnp.maximum(slack, 0))
    moved = jax.random.randint(jax.random.fold_in(own, 4), (count // 2,), 0, 1 << 20) % (slack + 1)
    tallies = tallies.at[source_of].add(-moved).at[taker].add(moved)
    members = jnp.searchsorted(jnp.cumsum(tallies), jnp.arange(rows * top), side="right").astype(jnp.int32)
    table = members.reshape(top, rows).T
    table = table[jax.random.permutation(jax.random.fold_in(own, 1), rows)]
    turn = jax.random.randint(jax.random.fold_in(own, 2), (rows, 1), 0, top)
    return jnp.take_along_axis(table, (jnp.arange(top)[None, :] + turn) % top, axis=1)


def shares(count, total, limit, skew, full):
    portions = [(1 << 20) // math.isqrt(grade ** skew) + 1 for grade in range(1, count + 1)]
    largest = limit if full else min(limit, max(-(-total // count), total * portions[0] // sum(portions)))
    least = 1 if total - largest >= count - 1 else 0
    counts, surplus = [largest] + [least] * (count - 1), total - largest - least * (count - 1)
    while surplus > 0:
        free = [i for i in range(1, count) if counts[i] < largest] or [i for i in range(1, count) if counts[i] < limit]
        mass, remaining = sum([portions[i] for i in free]), surplus
        for i in free:
            addition = min(limit - counts[i], max(1, remaining * portions[i] // mass), surplus)
            counts[i] = counts[i] + addition
            surplus = surplus - addition
    return np.array(counts)


def bell_draw(key, dims, scale, most, pieces=(), kind=jnp.bfloat16):
    array = scale * jax.random.normal(key, dims, jnp.float32)
    if pieces:
        array = array * steps_of(key, dims, pieces, -0.22, 0.18)
    return jnp.clip(array, -most, most).astype(kind)


def setup_inputs(seed: int = 0) -> dict:
    seeds = jax.random.split(jax.random.key(seed), 12)
    orbitals = bell_draw(seeds[0], (NODES, ORB), 1.0, 6.0, ((0, 32), (1, 8)), jnp.float32)
    occupations = draw_occupations(jax.random.fold_in(seeds[11], 71), 0)
    external = jnp.clip(jax.random.uniform(seeds[2], (NODES,), jnp.float32, -3.0, 3.0) * steps_of(seeds[2], (NODES,), ((0, 32),), -0.4, 0.0), -3.0, 3.0)
    core_density = jnp.clip(jnp.exp(math.log(300.0) - 5.7037825 * jax.random.uniform(seeds[3], (NODES,), jnp.float32) ** steps_of(seeds[3], (NODES,), ((0, 32),), -0.2, 0.2)), 1.0, 300.0)
    cell_scale = jnp.clip(jnp.exp(math.log(2.0) - 1.3862944 * jax.random.uniform(seeds[4], (CELLS,), jnp.float32) ** steps_of(seeds[4], (CELLS,), ((0, 32),), -0.2, 0.2)), 0.5, 2.0)
    stiffness = draw_stiffness(jax.random.fold_in(seeds[11], 71), 0)
    touched_atom = draw_touched_atom(jax.random.fold_in(seeds[11], 71), 0)
    touched_cells = distinct(seeds[7], (N_CELLS * TOUCH_DEV), CELL_DEV, PATCH_AT, 0)
    projectors = bell_draw(seeds[8], (N_CELLS * TOUCH_DEV, PATCH_AT, PROJ, CELL_NODES), 0.2, 1.2, ((0, 32),), jnp.float32)
    coupling = draw_coupling(jax.random.fold_in(seeds[11], 71), 0)
    atom_owner_keys = jax.random.split(jax.random.fold_in(seeds[10], 1), ATOMS // ATOMS)
    atom_owner_turns = jax.random.permutation(jax.random.fold_in(seeds[10], 3), ATOMS // ATOMS)
    atom_owner = jax.vmap(lambda own, number: deal_out(jax.random.fold_in(seeds[10], 2), own, number, ATOMS, N_CELLS, 1, OWN_CAP, 2))(atom_owner_keys, atom_owner_turns).reshape((ATOMS, 1))
    return dict(orbitals=orbitals, occupations=occupations, external=external, core_density=core_density, cell_scale=cell_scale, stiffness=stiffness, touched_atom=touched_atom, touched_cells=touched_cells, projectors=projectors, coupling=coupling, atom_owner=atom_owner)


highest = lax.Precision.HIGHEST
step_size = 0.1
exchange_coef = (3.0 / math.pi) ** (1.0 / 3.0)
tiny = 1e-06

def cut_cells(grid, upper_layer):
    layers = grid.shape[0]
    extended = jnp.concatenate([grid, upper_layer[None]], axis=0)
    slabs = jnp.stack([extended[offset:offset + layers:DEG] for offset in range(EDGE)], axis=1)
    blocks = [slabs[:, :, DEG * row_cell:DEG * row_cell + EDGE, DEG * col_cell:DEG * col_cell + EDGE] for row_cell in range(SIDE) for col_cell in range(SIDE)]
    return jnp.stack(blocks, axis=1).reshape(-1, CELL_NODES, grid.shape[-1])

def add_cells(values, layers):
    width = values.shape[-1]
    side_nodes = SIDE * DEG + 1
    blocks = values.reshape(-1, SIDE, SIDE, EDGE, EDGE, EDGE, width)
    slabs = jnp.zeros((blocks.shape[0], EDGE, side_nodes, side_nodes, width), values.dtype)
    for row_cell in range(SIDE):
        for col_cell in range(SIDE):
            slabs = slabs.at[:, :, DEG * row_cell:DEG * row_cell + EDGE, DEG * col_cell:DEG * col_cell + EDGE].add(blocks[:, row_cell, col_cell])
    lower = slabs[:, :DEG].reshape(layers, side_nodes, side_nodes, width)
    return (lower, slabs[:, DEG])

def reference(orbitals, occupations, external, core_density, cell_scale, stiffness, touched_atom, touched_cells, projectors, coupling, atom_owner):
    layers = NODES // PLANE
    side_nodes = SIDE * DEG + 1
    owner = atom_owner[:, 0]
    atom_index = jnp.arange(ATOMS, dtype=jnp.int32)
    earlier = (owner[None, :] == owner[:, None]) & (atom_index[None, :] < atom_index[:, None])
    owner_rank = jnp.sum(earlier.astype(jnp.int32), axis=1)
    own_slot = owner * OWN_CAP + owner_rank
    cell_hot = (touched_cells[:, :, None] == jnp.arange(CELL_DEV, dtype=jnp.int32)[None, None, :]).astype(jnp.float32)
    spread = jnp.einsum('tqc,tqpn->tpcn', cell_hot, projectors, precision=highest)
    spread = spread.reshape(N_CELLS, TOUCH_DEV, PROJ, CELL_DEV * CELL_NODES)
    current = orbitals
    for iteration in range(ITERS):
        density = jnp.dot(current * current, occupations, precision=highest)
        potential = external - exchange_coef * jnp.cbrt(density + core_density)
        grid = current.reshape(layers, side_nodes, side_nodes, ORB)
        cells = cut_cells(grid, grid[0])
        local = cell_scale[:, None, None] * jnp.einsum('mn,cnr->cmr', stiffness, cells, precision=highest)
        grouped = cells.reshape(N_CELLS, CELL_DEV * CELL_NODES, ORB)
        contrib = jnp.einsum('dtpk,dkr->dtpr', spread, grouped, precision=highest).reshape(N_CELLS * TOUCH_DEV, PROJ, ORB)
        atom_sums = jax.ops.segment_sum(contrib, touched_atom, num_segments=ATOMS)
        applied = jnp.einsum('apq,aqr->apr', coupling, atom_sums, precision=highest)
        returned = applied[touched_atom].reshape(N_CELLS, TOUCH_DEV, PROJ, ORB)
        nonlocal_term = jnp.einsum('dtpk,dtpr->dkr', spread, returned, precision=highest).reshape(CELLS, CELL_NODES, ORB)
        lower, upper = add_cells(local + nonlocal_term, layers)
        lower = lower.at[::DEG].add(jnp.roll(upper, 1, axis=0))
        image = lower.reshape(NODES, ORB) + potential[:, None] * current
        rayleigh = jnp.sum(current * image, axis=0) / (jnp.sum(current * current, axis=0) + tiny)
        trial = current - step_size * (image - rayleigh[None, :] * current)
        margin = jnp.dot(trial.T, trial, precision=highest) / NODES
        factor = jnp.linalg.cholesky(margin)
        current = lax.linalg.triangular_solve(factor, trial, left_side=False, lower=True, transpose_a=True)
    owned = jnp.zeros((N_CELLS * OWN_CAP, PROJ, ORB), jnp.float32).at[own_slot].set(atom_sums)
    return (current, rayleigh, owned)
```

```python
import functools
import math

import jax
import jax.numpy as jnp
from jax import lax
from jax.experimental import pallas as pl
from jax.experimental.pallas import tpu as pltpu
from jax.sharding import Mesh
from jax.sharding import PartitionSpec as P

DEG = 6
EDGE = 7
CELL_NODES = 343
SIDE = 3
THICK = 1
CELL_DEV = 9
ORB = 1024
TOUCH_DEV = 6
OWN_CAP = 5
CELLS = ("xl", "z", "core")
ORBS = ("xh", "y")


highest = lax.Precision.HIGHEST
step_size = 0.1
exchange_coef = (3.0 / math.pi) ** (1.0 / 3.0)
tiny = 1e-06


def from_everyone(value, axis):
    length = lax.axis_size(axis)
    return lax.all_to_all(
        jnp.broadcast_to(value[None], (length, *value.shape)), axis, 0, 0, tiled=True
    )


def over_copies(value, axis):
    return from_everyone(value, axis).sum(axis=0)


def passed_along(value, axis, steps):
    count = lax.axis_size(axis)
    pairs = [(source, (source + steps) % count) for source in range(count)]
    return lax.ppermute(value, axis, pairs)


def in_order(parts, dim):
    lengths = list(parts.shape[1:])
    lengths[dim] *= parts.shape[0]
    return jnp.moveaxis(parts, 0, dim).reshape(lengths)


def gather_axes(value, axes, dim):
    far, near = axes
    parts = from_everyone(from_everyone(value, far), near)
    return in_order(parts.swapaxes(0, 1).reshape(-1, *value.shape), dim)


def packed_total(arrays, axis):
    ends = [0]
    for a in arrays:
        ends.append(ends[-1] + a.size)
    so_far = over_copies(jnp.concatenate([a.ravel() for a in arrays]), axis)
    return tuple((so_far[b:e].reshape(a.shape) for a, b, e in zip(arrays, ends, ends[1:])))


def cut_cells(grid, upper_layer):
    layers = grid.shape[0]
    extended = jnp.concatenate([grid, upper_layer[None]], axis=0)
    slabs = jnp.stack([extended[offset : offset + layers : DEG] for offset in range(EDGE)], axis=1)
    blocks = [
        slabs[:, :, DEG * row_cell : DEG * row_cell + EDGE, DEG * col_cell : DEG * col_cell + EDGE]
        for row_cell in range(SIDE)
        for col_cell in range(SIDE)
    ]
    return jnp.stack(blocks, axis=1).reshape(-1, CELL_NODES, grid.shape[-1])


def add_cells(values, layers):
    width = values.shape[-1]
    side_nodes = SIDE * DEG + 1
    blocks = values.reshape(-1, SIDE, SIDE, EDGE, EDGE, EDGE, width)
    slabs = jnp.zeros((blocks.shape[0], EDGE, side_nodes, side_nodes, width), values.dtype)
    for row_cell in range(SIDE):
        for col_cell in range(SIDE):
            slabs = slabs.at[
                :, :, DEG * row_cell : DEG * row_cell + EDGE, DEG * col_cell : DEG * col_cell + EDGE
            ].add(blocks[:, row_cell, col_cell])
    lower = slabs[:, :DEG].reshape(layers, side_nodes, side_nodes, width)
    return (lower, slabs[:, DEG])


ROWS = 272
HALF = 18
PIECE = 288
SLOT = 18
MESH_ID = pl.DeviceIdType.MESH
WHOLE = pl.BlockSpec(memory_space=pltpu.VMEM)


def split(x):
    high = x.astype(jnp.bfloat16)
    low = (x - high.astype(jnp.float32)).astype(jnp.bfloat16)
    return high, low


def orb_peer(index):
    return {"xh": index // 4, "y": index % 4}


def site_peer(index):
    return {"xl": index // 8, "z": index % 8}


def my_orb():
    return lax.axis_index("xh") * 4 + lax.axis_index("y")


def my_site():
    return lax.axis_index("xl") * 8 + lax.axis_index("z")


def greet(peers):
    barrier = pltpu.get_barrier_semaphore()
    for peer in peers:
        pl.semaphore_signal(barrier, inc=1, device_id=peer, device_id_type=MESH_ID)
    pl.semaphore_wait(barrier, len(peers))


def remote(src, dst, send, recv, peer):
    return pltpu.make_async_remote_copy(
        src_ref=src, dst_ref=dst, send_sem=send, recv_sem=recv,
        device_id=peer, device_id_type=MESH_ID,
    )


def rows_out_kernel(t_ref, out_ref, send, recv):
    me = my_orb()
    greet([orb_peer((me + r) % 8) for r in range(1, 8)])
    copies = []
    for r in (6, 2, 5, 3, 7, 1, 4):
        peer = (me + r) % 8
        copy = remote(t_ref.at[peer], out_ref.at[me], send.at[r], recv.at[r], orb_peer(peer))
        copy.start()
        copies.append(copy)
    out_ref[me] = t_ref[me]
    for copy in copies:
        copy.wait()


def exchange_rows(value, collective_id):
    return pl.pallas_call(
        rows_out_kernel,
        out_shape=jax.ShapeDtypeStruct((8, ROWS, 128), jnp.float32),
        in_specs=[WHOLE],
        out_specs=WHOLE,
        scratch_shapes=[pltpu.SemaphoreType.DMA((8,)), pltpu.SemaphoreType.DMA((8,))],
        compiler_params=pltpu.CompilerParams(collective_id=collective_id, has_side_effects=True),
    )(value)


def gram_kernel(x_ref, out_ref, left_ref, right_ref):
    for j in range(8):
        high, low = split(x_ref[j])
        lanes = pl.ds(128 * j, 128)
        left_ref[0:ROWS, lanes] = high
        left_ref[ROWS:2 * ROWS, lanes] = low
        left_ref[2 * ROWS:3 * ROWS, lanes] = high
        right_ref[0:ROWS, lanes] = high
        right_ref[ROWS:2 * ROWS, lanes] = high
        right_ref[2 * ROWS:3 * ROWS, lanes] = low
    for i in range(8):
        product = lax.dot_general(
            left_ref[:, pl.ds(128 * i, 128)], right_ref[:, pl.ds(0, 128 * (i + 1))],
            (((0,), (0,)), ((), ())), preferred_element_type=jnp.float32,
        )
        for j in range(i + 1):
            out_ref[i * (i + 1) // 2 + j] = product[:, 128 * j:128 * (j + 1)]


def gram(rows):
    return pl.pallas_call(
        gram_kernel,
        out_shape=jax.ShapeDtypeStruct((36, 128, 128), jnp.float32),
        in_specs=[WHOLE],
        out_specs=WHOLE,
        scratch_shapes=[pltpu.VMEM((3 * ROWS, 1024), jnp.bfloat16)] * 2,
    )(rows)


def total_kernel(
    m_ref, out_ref, pair_ref, mine_ref, orb_ref, sum_ref, cut_ref, site_ref, done_ref,
    pair_send, pair_recv, orb_send, orb_recv, site_send, site_recv,
    back_send, back_recv, home_send, home_recv, last_send, last_recv,
):
    core = lax.axis_index("core")
    me = my_orb()
    here = my_site()
    partner = {"core": 1 - core}
    order = (6, 2, 5, 3, 7, 1, 4)
    greet(
        [partner]
        + [orb_peer((me + r) % 8) for r in range(1, 8)]
        + [site_peer((here + r) % 16) for r in range(1, 16)]
    )
    pending = []
    arrivals = {}
    for r in order + (0,):
        piece = (me + r) % 8
        copy = remote(
            m_ref.at[1 - core, piece], pair_ref.at[piece], pair_send.at[r], pair_recv.at[r], partner
        )
        copy.start()
        arrivals[r] = copy
        pending.append(copy)
    firsts = []
    for r in order + (0,):
        piece = (me + r) % 8
        arrivals[r].wait_recv()
        mine_ref[piece] = m_ref[core, piece] + pair_ref[piece]
        if r:
            copy = remote(mine_ref.at[piece], orb_ref.at[r], orb_send.at[r], orb_recv.at[r], orb_peer(piece))
            copy.start()
            firsts.append(copy)
    total = mine_ref[me]
    for copy, r in zip(firsts, order):
        copy.wait_recv()
        total = total + orb_ref[r]
    sum_ref[...] = total
    for i in range(16):
        cut_ref[i] = sum_ref[SLOT * i:SLOT * (i + 1), :]
    seconds = []
    for r in range(1, 16):
        peer = (here + r) % 16
        copy = remote(cut_ref.at[peer], site_ref.at[r], site_send.at[r], site_recv.at[r], site_peer(peer))
        copy.start()
        seconds.append(copy)
    slot = cut_ref[here]
    for r, copy in enumerate(seconds, 1):
        copy.wait_recv()
        slot = slot + site_ref[r]
    done_ref[here] = slot
    thirds = []
    for r in range(1, 16):
        peer = (here + r) % 16
        copy = remote(done_ref.at[here], done_ref.at[here], back_send.at[r], back_recv.at[r], site_peer(peer))
        copy.start()
        thirds.append(copy)
    for copy in seconds:
        copy.wait_send()
    for copy in thirds:
        copy.wait_recv()
    for i in range(16):
        sum_ref[SLOT * i:SLOT * (i + 1), :] = done_ref[i]
    fourths = []
    for r in order:
        peer = (me + r) % 8
        copy = remote(sum_ref, out_ref.at[core, me], home_send.at[r], home_recv.at[r], orb_peer(peer))
        copy.start()
        fourths.append(copy)
    lasts = [remote(sum_ref, out_ref.at[core, me], last_send.at[0], last_recv.at[0], partner)]
    lasts[0].start()
    out_ref[core, me] = sum_ref[...]
    for copy, r in zip(fourths, order):
        source = (me + 8 - r) % 8
        copy.wait_recv()
        place = out_ref.at[core, source]
        forward = remote(place, place, last_send.at[r], last_recv.at[r], partner)
        forward.start()
        lasts.append(forward)
    for copy in pending + firsts + thirds + fourths + lasts:
        copy.wait_send()
    for copy in lasts:
        copy.wait_recv()


def total_blocks(blocks, collective_id):
    pieces = blocks.reshape(2, 8, PIECE, 128)
    eight = pltpu.SemaphoreType.DMA((8,))
    sixteen = pltpu.SemaphoreType.DMA((16,))
    total = pl.pallas_call(
        total_kernel,
        out_shape=jax.ShapeDtypeStruct(pieces.shape, jnp.float32),
        in_specs=[WHOLE],
        out_specs=WHOLE,
        scratch_shapes=[
            pltpu.VMEM((8, PIECE, 128), jnp.float32),
            pltpu.VMEM((8, PIECE, 128), jnp.float32),
            pltpu.VMEM((8, PIECE, 128), jnp.float32),
            pltpu.VMEM((PIECE, 128), jnp.float32),
            pltpu.VMEM((16, SLOT, 128), jnp.float32),
            pltpu.VMEM((16, SLOT, 128), jnp.float32),
            pltpu.VMEM((16, SLOT, 128), jnp.float32),
            eight, eight, eight, eight, sixteen, sixteen,
            sixteen, sixteen, eight, eight, eight, eight,
        ],
        compiler_params=pltpu.CompilerParams(collective_id=collective_id, has_side_effects=True),
    )(pieces)
    return total.reshape(36, 128, 128)


def product(x, y):
    xh, xl = split(x)
    yh, yl = split(y)
    right = jnp.concatenate([yh, yl], axis=1)
    both = jnp.dot(
        jnp.concatenate([xh, xl], axis=1), jnp.concatenate([right, right], axis=0),
        preferred_element_type=jnp.float32,
    )
    return both[:, :128] + both[:, 128:]


def twice(y):
    yh, yl = split(y)
    return jnp.concatenate(
        [jnp.concatenate([yh, yh], axis=1), jnp.concatenate([yl, yl], axis=1)], axis=0
    )


def against(pair, right):
    both = lax.dot_general(pair, right, (((1,), (1,)), ((), ())), preferred_element_type=jnp.float32)
    return both[:, :128] + both[:, 128:]


def pair_of(x):
    return jnp.concatenate(split(x), axis=1)


def solve_kernel(scale, m_ref, t_ref, out_ref, panel_ref, left_ref, inv_ref, work_ref, unit_ref):
    row = lax.broadcasted_iota(jnp.int32, (128, 128), 0)
    col = lax.broadcasted_iota(jnp.int32, (128, 128), 1)
    eye = (row == col).astype(jnp.float32)
    half = (row > col).astype(jnp.float32) + 0.5 * eye
    down, across = [], []
    for k in range(8):
        diagonal = m_ref[k * (k + 1) // 2 + k] * eye
        down.append(lax.rsqrt(jnp.sum(diagonal, axis=1, keepdims=True) * scale))
        across.append(lax.rsqrt(jnp.sum(diagonal, axis=0, keepdims=True) * scale))
    for j in range(8):
        for i in range(j, 8):
            block = m_ref[i * (i + 1) // 2 + j] * scale
            panel_ref[j, 128 * i:128 * (i + 1), :] = block * down[i] * across[j]
        panel_ref[j, 1024:1024 + ROWS, :] = t_ref[j] * across[j]
    bottom = 1024 + ROWS
    for k in range(8):
        block = panel_ref[k, 128 * k:128 * (k + 1), :]
        x = eye - half * (block - eye)
        for step in range(2):
            error = against(pair_of(product(x, block)), twice(x)) - eye
            x = x - product(half * error, x)
        inv_ref[...] = x
        left = jnp.sum(jnp.sum(error * error, axis=0, keepdims=True), axis=1, keepdims=True)[0, 0]

        @pl.when(jnp.logical_not(left < 1e-6))
        def _():
            work_ref[...] = panel_ref[k, 128 * k:128 * (k + 1), :]
            unit_ref[...] = eye

            def eliminate(j, carry):
                lane = (col == j).astype(jnp.float32)
                mine = work_ref[pl.ds(j, 1), :]
                unit = unit_ref[pl.ds(j, 1), :]
                pivot = jnp.sum(jnp.where(col[0:1] == j, mine, 0.0), axis=1, keepdims=True)
                whole = work_ref[...]
                column = jnp.sum(jnp.where(col == j, whole, 0.0), axis=1, keepdims=True)
                factor = jnp.where(row > j, column / pivot, 0.0)
                work_ref[...] = whole - factor * mine
                unit_ref[...] = unit_ref[...] - factor * unit
                inv_ref[pl.ds(j, 1), :] = unit * lax.rsqrt(pivot)
                return carry

            lax.fori_loop(0, 128, eliminate, 0)

        right = twice(inv_ref[...])
        starts = list(range(128 * (k + 1), 1024, 128)) + [1024, 1024 + ROWS // 2]
        for start in starts:
            size = 128 if start < 1024 else ROWS // 2
            value = against(pair_of(panel_ref[k, start:start + size, :]), right)
            if start < 1024:
                left_ref[start:start + size, :] = pair_of(value)
            else:
                out_ref[k, start - 1024:start - 1024 + size, :] = value
                if k < 7:
                    left_ref[start:start + size, :] = pair_of(value)
        for j in range(k + 1, 8):
            pair = left_ref[128 * j:128 * (j + 1), :]
            high, low = pair[:, :128], pair[:, 128:]
            right = jnp.concatenate(
                [jnp.concatenate([high, high], axis=1), jnp.concatenate([low, low], axis=1)], axis=0
            )
            for start in list(range(128 * j, 1024, 128)) + [1024, 1024 + ROWS // 2]:
                size = 128 if start < 1024 else ROWS // 2
                panel_ref[j, start:start + size, :] = panel_ref[j, start:start + size, :] - against(
                    left_ref[start:start + size, :], right
                )


def solve_rows(blocks, rows, scale):
    return pl.pallas_call(
        functools.partial(solve_kernel, scale),
        out_shape=jax.ShapeDtypeStruct((8, ROWS, 128), jnp.float32),
        in_specs=[WHOLE, WHOLE],
        out_specs=WHOLE,
        scratch_shapes=[
            pltpu.VMEM((8, 1024 + ROWS, 128), jnp.float32),
            pltpu.VMEM((1024 + ROWS, 256), jnp.bfloat16),
            pltpu.VMEM((128, 128), jnp.float32),
            pltpu.VMEM((128, 128), jnp.float32),
            pltpu.VMEM((128, 128), jnp.float32),
        ],
    )(blocks, rows)


def orthonormal(trial, total_nodes):
    padded = jnp.pad(trial, ((0, 8 * ROWS - trial.shape[0]), (0, 0)))
    rows = exchange_rows(padded.reshape(8, ROWS, 128), 1)
    blocks = total_blocks(gram(rows), 2)
    solved = solve_rows(blocks, rows, 1.0 / total_nodes)
    back = exchange_rows(solved, 3)
    return back.reshape(8 * ROWS, 128)[: trial.shape[0]]


def per_device(
    orbitals,
    occupations,
    external,
    core_density,
    cell_scale,
    stiffness,
    touched_atom,
    touched_cells,
    projectors,
    coupling,
    atom_owner,
):
    n_cells = lax.axis_size(CELLS)
    node_dev, width = orbitals.shape
    total_nodes = node_dev * n_cells
    layers = THICK * DEG
    side_nodes = SIDE * DEG + 1
    here = lax.axis_index(CELLS)
    proj_count = projectors.shape[2]
    atom_count = atom_owner.shape[0]
    owner = atom_owner[:, 0]
    atom_index = jnp.arange(atom_count, dtype=jnp.int32)
    earlier = (owner[None, :] == owner[:, None]) & (atom_index[None, :] < atom_index[:, None])
    owner_rank = jnp.sum(earlier.astype(jnp.int32), axis=1)
    own_slot = owner * OWN_CAP + owner_rank
    slot_all = jnp.sum(
        jnp.where(touched_atom[:, None] == atom_index[None, :], own_slot[None, :], 0), axis=1
    )
    my_slots = here * OWN_CAP + jnp.arange(OWN_CAP, dtype=jnp.int32)
    owned_hot = (slot_all[None, :] == my_slots[:, None]).astype(jnp.float32)
    flat_coupling = coupling.reshape(atom_count, proj_count * proj_count)
    mine = lax.dynamic_slice_in_dim(touched_atom, here * TOUCH_DEV, TOUCH_DEV)
    pair_hot = (mine[:, None] == touched_atom[None, :]).astype(jnp.float32)
    mine_pick = (mine[:, None] == atom_index[None, :]).astype(jnp.float32)
    mine_coupling = jnp.dot(mine_pick, flat_coupling, precision=highest).reshape(
        TOUCH_DEV, proj_count, proj_count
    )
    cell_hot = (
        touched_cells[:, :, None] == jnp.arange(CELL_DEV, dtype=jnp.int32)[None, None, :]
    ).astype(jnp.float32)
    spread = jnp.einsum("tqc,tqpn->tpcn", cell_hot, projectors, precision=highest).reshape(
        TOUCH_DEV * proj_count, CELL_DEV * CELL_NODES
    )
    current = orbitals
    partial_density = jnp.dot(current * current, occupations, precision=highest)
    density = over_copies(partial_density, ORBS)
    potential = external - exchange_coef * jnp.cbrt(density + core_density)
    grid = current.reshape(layers, side_nodes, side_nodes, width)
    upper_layer = passed_along(grid[0], CELLS, -1)
    cells = cut_cells(grid, upper_layer)
    local = cell_scale[:, None, None] * jnp.einsum(
        "mn,cnr->cmr", stiffness, cells, precision=highest
    )
    contrib = jnp.dot(
        spread, cells.reshape(CELL_DEV * CELL_NODES, width), precision=highest
    ).reshape(TOUCH_DEV, proj_count, width)
    piece = gather_axes(contrib, (("xl", "z"), "core"), 0)
    owned = jnp.einsum("kt,tpr->kpr", owned_hot, piece, precision=highest)
    touched_sums = jnp.einsum("kt,tpr->kpr", pair_hot, piece, precision=highest)
    returned = jnp.einsum("tpq,tqr->tpr", mine_coupling, touched_sums, precision=highest)
    nonlocal_term = jnp.einsum(
        "kn,kr->nr", spread, returned.reshape(TOUCH_DEV * proj_count, width), precision=highest
    ).reshape(CELL_DEV, CELL_NODES, width)
    lower, upper = add_cells(local + nonlocal_term, layers)
    lower = lower.at[DEG::DEG].add(upper[:-1])
    carried = passed_along(upper[-1], CELLS, 1)
    lower = lower.at[0].add(carried)
    image = lower.reshape(node_dev, width) + potential[:, None] * current
    numerator, denominator = packed_total(
        (jnp.sum(current * image, axis=0), jnp.sum(current * current, axis=0)), CELLS
    )
    rayleigh = numerator / (denominator + tiny)
    trial = current - step_size * (image - rayleigh[None, :] * current)
    current = orthonormal(trial, total_nodes)
    return (current, rayleigh, owned)


def solution(mesh):
    finer = Mesh(mesh.devices.reshape(2, 8, 2, 2, 4), ("xl", "z", "core", "xh", "y"))
    return jax.shard_map(
        per_device,
        mesh=finer,
        in_specs=(
            P(CELLS, ORBS),
            P(ORBS),
            P(CELLS),
            P(CELLS),
            P(CELLS),
            P(),
            P(),
            P(CELLS, None),
            P(CELLS, None, None, None),
            P(),
            P(),
        ),
        out_specs=(P(CELLS, ORBS), P(ORBS), P(CELLS, None, ORBS)),
        check_vma=False,
    )
```

```python
import functools
import math

import jax
import jax.numpy as jnp
from jax import lax
from jax.experimental import pallas as pl
from jax.experimental.pallas import tpu as pltpu
from jax.sharding import Mesh
from jax.sharding import PartitionSpec as P

DEG = 6
EDGE = 7
CELL_NODES = 343
SIDE = 3
PROJ = 18
ATOM_DEV = 2
REACH = 2
TOUCH_DEV = 6
OWN_CAP = 5
CELLS = ("xl", "z", "core")
ORBS = ("xh", "y")

highest = lax.Precision.HIGHEST
step_size = 0.1
exchange_coef = (3.0 / math.pi) ** (1.0 / 3.0)
tiny = 1e-06


ROWS = 272
PIECE = 288
SLOT = 18
MESH_ID = pl.DeviceIdType.MESH
WHOLE = pl.BlockSpec(memory_space=pltpu.VMEM)


def split(x):
    high = x.astype(jnp.bfloat16)
    low = (x - high.astype(jnp.float32)).astype(jnp.bfloat16)
    return high, low


def orb_peer(index):
    return {"xh": index // 4, "y": index % 4}


def site_peer(index):
    return {"xl": index // 8, "z": index % 8}


def my_orb():
    return lax.axis_index("xh") * 4 + lax.axis_index("y")


def my_site():
    return lax.axis_index("xl") * 8 + lax.axis_index("z")


def greet(peers):
    barrier = pltpu.get_barrier_semaphore()
    for peer in peers:
        pl.semaphore_signal(barrier, inc=1, device_id=peer, device_id_type=MESH_ID)
    pl.semaphore_wait(barrier, len(peers))


def remote(src, dst, send, recv, peer):
    return pltpu.make_async_remote_copy(
        src_ref=src, dst_ref=dst, send_sem=send, recv_sem=recv,
        device_id=peer, device_id_type=MESH_ID,
    )


def rows_out_kernel(t_ref, out_ref, send, recv):
    me = my_orb()
    greet([orb_peer((me + r) % 8) for r in range(1, 8)])
    copies = []
    for r in (6, 2, 5, 3, 7, 1, 4):
        peer = (me + r) % 8
        copy = remote(t_ref.at[peer], out_ref.at[me], send.at[r], recv.at[r], orb_peer(peer))
        copy.start()
        copies.append(copy)
    out_ref[me] = t_ref[me]
    for copy in copies:
        copy.wait()


def exchange_rows(value, collective_id):
    return pl.pallas_call(
        rows_out_kernel,
        out_shape=jax.ShapeDtypeStruct((8, ROWS, 128), jnp.float32),
        in_specs=[WHOLE],
        out_specs=WHOLE,
        scratch_shapes=[pltpu.SemaphoreType.DMA((8,)), pltpu.SemaphoreType.DMA((8,))],
        compiler_params=pltpu.CompilerParams(collective_id=collective_id, has_side_effects=True),
    )(value)


def gram_kernel(x_ref, out_ref, left_ref, right_ref):
    for j in range(8):
        high, low = split(x_ref[j])
        lanes = pl.ds(128 * j, 128)
        left_ref[0:ROWS, lanes] = high
        left_ref[ROWS:2 * ROWS, lanes] = low
        left_ref[2 * ROWS:3 * ROWS, lanes] = high
        right_ref[0:ROWS, lanes] = high
        right_ref[ROWS:2 * ROWS, lanes] = high
        right_ref[2 * ROWS:3 * ROWS, lanes] = low
    for i in range(8):
        product = lax.dot_general(
            left_ref[:, pl.ds(128 * i, 128)], right_ref[:, pl.ds(0, 128 * (i + 1))],
            (((0,), (0,)), ((), ())), preferred_element_type=jnp.float32,
        )
        for j in range(i + 1):
            out_ref[i * (i + 1) // 2 + j] = product[:, 128 * j:128 * (j + 1)]


def gram(rows):
    return pl.pallas_call(
        gram_kernel,
        out_shape=jax.ShapeDtypeStruct((36, 128, 128), jnp.float32),
        in_specs=[WHOLE],
        out_specs=WHOLE,
        scratch_shapes=[pltpu.VMEM((3 * ROWS, 1024), jnp.bfloat16)] * 2,
    )(rows)


def total_kernel(
    m_ref, out_ref, pair_ref, mine_ref, orb_ref, sum_ref, cut_ref, site_ref, done_ref,
    pair_send, pair_recv, orb_send, orb_recv, site_send, site_recv,
    back_send, back_recv, home_send, home_recv, last_send, last_recv,
):
    core = lax.axis_index("core")
    me = my_orb()
    here = my_site()
    partner = {"core": 1 - core}
    order = (6, 2, 5, 3, 7, 1, 4)
    greet(
        [partner]
        + [orb_peer((me + r) % 8) for r in range(1, 8)]
        + [site_peer((here + r) % 16) for r in range(1, 16)]
    )
    pending = []
    arrivals = {}
    for r in order + (0,):
        piece = (me + r) % 8
        copy = remote(
            m_ref.at[1 - core, piece], pair_ref.at[piece], pair_send.at[r], pair_recv.at[r], partner
        )
        copy.start()
        arrivals[r] = copy
        pending.append(copy)
    firsts = []
    for r in order + (0,):
        piece = (me + r) % 8
        arrivals[r].wait_recv()
        mine_ref[piece] = m_ref[core, piece] + pair_ref[piece]
        if r:
            copy = remote(mine_ref.at[piece], orb_ref.at[r], orb_send.at[r], orb_recv.at[r], orb_peer(piece))
            copy.start()
            firsts.append(copy)
    total = mine_ref[me]
    for copy, r in zip(firsts, order):
        copy.wait_recv()
        total = total + orb_ref[r]
    sum_ref[...] = total
    for i in range(16):
        cut_ref[i] = sum_ref[SLOT * i:SLOT * (i + 1), :]
    seconds = []
    for r in range(1, 16):
        peer = (here + r) % 16
        copy = remote(cut_ref.at[peer], site_ref.at[r], site_send.at[r], site_recv.at[r], site_peer(peer))
        copy.start()
        seconds.append(copy)
    slot = cut_ref[here]
    for r, copy in enumerate(seconds, 1):
        copy.wait_recv()
        slot = slot + site_ref[r]
    done_ref[here] = slot
    thirds = []
    for r in range(1, 16):
        peer = (here + r) % 16
        copy = remote(done_ref.at[here], done_ref.at[here], back_send.at[r], back_recv.at[r], site_peer(peer))
        copy.start()
        thirds.append(copy)
    for copy in seconds:
        copy.wait_send()
    for copy in thirds:
        copy.wait_recv()
    for i in range(16):
        sum_ref[SLOT * i:SLOT * (i + 1), :] = done_ref[i]
    fourths = []
    for r in order:
        peer = (me + r) % 8
        copy = remote(sum_ref, out_ref.at[core, me], home_send.at[r], home_recv.at[r], orb_peer(peer))
        copy.start()
        fourths.append(copy)
    lasts = [remote(sum_ref, out_ref.at[core, me], last_send.at[0], last_recv.at[0], partner)]
    lasts[0].start()
    out_ref[core, me] = sum_ref[...]
    for copy, r in zip(fourths, order):
        source = (me + 8 - r) % 8
        copy.wait_recv()
        place = out_ref.at[core, source]
        forward = remote(place, place, last_send.at[r], last_recv.at[r], partner)
        forward.start()
        lasts.append(forward)
    for copy in pending + firsts + thirds + fourths + lasts:
        copy.wait_send()
    for copy in lasts:
        copy.wait_recv()


def total_blocks(blocks, collective_id):
    pieces = blocks.reshape(2, 8, PIECE, 128)
    eight = pltpu.SemaphoreType.DMA((8,))
    sixteen = pltpu.SemaphoreType.DMA((16,))
    total = pl.pallas_call(
        total_kernel,
        out_shape=jax.ShapeDtypeStruct(pieces.shape, jnp.float32),
        in_specs=[WHOLE],
        out_specs=WHOLE,
        scratch_shapes=[
            pltpu.VMEM((8, PIECE, 128), jnp.float32),
            pltpu.VMEM((8, PIECE, 128), jnp.float32),
            pltpu.VMEM((8, PIECE, 128), jnp.float32),
            pltpu.VMEM((PIECE, 128), jnp.float32),
            pltpu.VMEM((16, SLOT, 128), jnp.float32),
            pltpu.VMEM((16, SLOT, 128), jnp.float32),
            pltpu.VMEM((16, SLOT, 128), jnp.float32),
            eight, eight, eight, eight, sixteen, sixteen,
            sixteen, sixteen, eight, eight, eight, eight,
        ],
        compiler_params=pltpu.CompilerParams(collective_id=collective_id, has_side_effects=True),
    )(pieces)
    return total.reshape(36, 128, 128)


def product(x, y):
    xh, xl = split(x)
    yh, yl = split(y)
    right = jnp.concatenate([yh, yl], axis=1)
    both = jnp.dot(
        jnp.concatenate([xh, xl], axis=1), jnp.concatenate([right, right], axis=0),
        preferred_element_type=jnp.float32,
    )
    return both[:, :128] + both[:, 128:]


def twice(y):
    yh, yl = split(y)
    return jnp.concatenate(
        [jnp.concatenate([yh, yh], axis=1), jnp.concatenate([yl, yl], axis=1)], axis=0
    )


def against(pair, right):
    both = lax.dot_general(pair, right, (((1,), (1,)), ((), ())), preferred_element_type=jnp.float32)
    return both[:, :128] + both[:, 128:]


def pair_of(x):
    return jnp.concatenate(split(x), axis=1)


def solve_kernel(scale, m_ref, t_ref, out_ref, panel_ref, left_ref, inv_ref, work_ref, unit_ref):
    row = lax.broadcasted_iota(jnp.int32, (128, 128), 0)
    col = lax.broadcasted_iota(jnp.int32, (128, 128), 1)
    eye = (row == col).astype(jnp.float32)
    half = (row > col).astype(jnp.float32) + 0.5 * eye
    down, across = [], []
    for k in range(8):
        diagonal = m_ref[k * (k + 1) // 2 + k] * eye
        down.append(lax.rsqrt(jnp.sum(diagonal, axis=1, keepdims=True) * scale))
        across.append(lax.rsqrt(jnp.sum(diagonal, axis=0, keepdims=True) * scale))
    for j in range(8):
        for i in range(j, 8):
            block = m_ref[i * (i + 1) // 2 + j] * scale
            panel_ref[j, 128 * i:128 * (i + 1), :] = block * down[i] * across[j]
        panel_ref[j, 1024:1024 + ROWS, :] = t_ref[j] * across[j]
    bottom = 1024 + ROWS
    for k in range(8):
        block = panel_ref[k, 128 * k:128 * (k + 1), :]
        x = eye - half * (block - eye)
        for step in range(2):
            error = against(pair_of(product(x, block)), twice(x)) - eye
            x = x - product(half * error, x)
        inv_ref[...] = x

        def unfinished(state):
            return (state[0] < 12) & jnp.logical_not(state[1] < 3e-5)

        def improve(state):
            x = inv_ref[...]
            block = panel_ref[k, 128 * k:128 * (k + 1), :]
            error = against(pair_of(product(x, block)), twice(x)) - eye
            inv_ref[...] = x - product(half * error, x)
            return state[0] + 1, jnp.sum(error * error)

        left = lax.while_loop(unfinished, improve, (0, jnp.sum(error * error)))[1]

        @pl.when(jnp.logical_not(left < 3e-5))
        def _():
            work_ref[...] = panel_ref[k, 128 * k:128 * (k + 1), :]
            unit_ref[...] = eye

            def eliminate(j, carry):
                lane = (col == j).astype(jnp.float32)
                mine = work_ref[pl.ds(j, 1), :]
                unit = unit_ref[pl.ds(j, 1), :]
                pivot = jnp.sum(jnp.where(col[0:1] == j, mine, 0.0), axis=1, keepdims=True)
                whole = work_ref[...]
                column = jnp.sum(jnp.where(col == j, whole, 0.0), axis=1, keepdims=True)
                factor = jnp.where(row > j, column / pivot, 0.0)
                work_ref[...] = whole - factor * mine
                unit_ref[...] = unit_ref[...] - factor * unit
                inv_ref[pl.ds(j, 1), :] = unit * lax.rsqrt(pivot)
                return carry

            lax.fori_loop(0, 128, eliminate, 0)

        right = twice(inv_ref[...])
        starts = list(range(128 * (k + 1), 1024, 128)) + [1024, 1024 + ROWS // 2]
        for start in starts:
            size = 128 if start < 1024 else ROWS // 2
            value = against(pair_of(panel_ref[k, start:start + size, :]), right)
            if start < 1024:
                left_ref[start:start + size, :] = pair_of(value)
            else:
                out_ref[k, start - 1024:start - 1024 + size, :] = value
                if k < 7:
                    left_ref[start:start + size, :] = pair_of(value)
        for j in range(k + 1, 8):
            pair = left_ref[128 * j:128 * (j + 1), :]
            high, low = pair[:, :128], pair[:, 128:]
            right = jnp.concatenate(
                [jnp.concatenate([high, high], axis=1), jnp.concatenate([low, low], axis=1)], axis=0
            )
            for start in list(range(128 * j, 1024, 128)) + [1024, 1024 + ROWS // 2]:
                size = 128 if start < 1024 else ROWS // 2
                panel_ref[j, start:start + size, :] = panel_ref[j, start:start + size, :] - against(
                    left_ref[start:start + size, :], right
                )


def solve_rows(blocks, rows, scale):
    return pl.pallas_call(
        functools.partial(solve_kernel, scale),
        out_shape=jax.ShapeDtypeStruct((8, ROWS, 128), jnp.float32),
        in_specs=[WHOLE, WHOLE],
        out_specs=WHOLE,
        scratch_shapes=[
            pltpu.VMEM((8, 1024 + ROWS, 128), jnp.float32),
            pltpu.VMEM((1024 + ROWS, 256), jnp.bfloat16),
            pltpu.VMEM((128, 128), jnp.float32),
            pltpu.VMEM((128, 128), jnp.float32),
            pltpu.VMEM((128, 128), jnp.float32),
        ],
    )(blocks, rows)


WINDOW = 2 * REACH + 1
TILE = 8
LINES = SIDE * DEG + 1
PLANE = LINES * LINES
HALO = 368
PADDED = EDGE * EDGE * TILE


def cell_peer(index):
    return {"xl": index // 16, "z": (index // 2) % 8, "core": index % 2}


def thrice(left, right, dims):
    lh, ll = left
    rh, rl = right
    dot = functools.partial(
        lax.dot_general, dimension_numbers=(dims, ((), ())), preferred_element_type=jnp.float32
    )
    return dot(lh, rh) + dot(ll, rh) + dot(lh, rl)


def cube_root(x):
    root = jnp.exp(jnp.log(x) * (1.0 / 3.0))
    for _ in range(2):
        root = root - (root * root * root - x) / (3.0 * root * root)
    return root


def trial_kernel(
    scale_ref, hot_ref,
    c_ref, occ_ref, ext_ref, core_ref, stiff_ref, proj_ref, coup_ref,
    rows_ref, ray_ref, sums_ref,
    halo_ref, tile_ref, value_ref, image_ref, top_ref, under_ref, proj24_ref,
    give_ref, take_ref, used_ref, window_ref, dens_ref, ray_all_ref, pot_ref,
    halo_sem, dens_send, dens_recv, give_send, give_recv, used_send, used_recv,
    top_sem, ray_send, ray_recv, rows_send, rows_recv, sums_send, sums_recv,
):
    nodes = c_ref.shape[0]
    here = lax.axis_index("xl") * 16 + lax.axis_index("z") * 2 + lax.axis_index("core")
    me = my_orb()
    barrier = pltpu.get_barrier_semaphore()
    peers = [cell_peer((here + r) % 32) for r in range(1, 32)]
    peers += [orb_peer((me + r) % 8) for r in range(1, 8)]
    for peer in peers:
        pl.semaphore_signal(barrier, inc=1, device_id=peer, device_id_type=MESH_ID)
    sends = []

    current = c_ref[...]
    square = current * current
    occ = occ_ref[...]
    density = thrice(split(jnp.broadcast_to(occ, (TILE, 128))), split(square), ((1,), (1,)))
    dens_ref[0] = density[0:1, :]

    node = lax.broadcasted_iota(jnp.int32, (CELL_NODES, PADDED), 0)
    place = lax.broadcasted_iota(jnp.int32, (CELL_NODES, PADDED), 1)
    inside = (place & 7) < EDGE
    match = node == EDGE * (place >> 3) + (place & 7)
    spot = jnp.where(inside & match, 1.0, 0.0).astype(jnp.bfloat16)
    dot = functools.partial(lax.dot_general, preferred_element_type=jnp.float32)

    def both_sides(part):
        wide = dot(part, spot, (((1,), (0,)), ((), ()))).astype(jnp.bfloat16)
        return dot(spot, wide, (((0,), (0,)), ((), ()))).astype(jnp.bfloat16)

    stiff = tuple(both_sides(part) for part in split(stiff_ref[...]))
    proj24_ref[...] = jnp.zeros_like(proj24_ref)
    for t in range(TOUCH_DEV):
        proj24_ref[24 * t:24 * t + PROJ, :] = proj_ref[t, 0]
    parts = split(proj24_ref[...])
    proj_rows = tuple(dot(p, spot, (((1,), (0,)), ((), ()))).astype(jnp.bfloat16) for p in parts)
    proj_cols = tuple(dot(spot, p, (((0,), (1,)), ((), ()))).astype(jnp.bfloat16) for p in parts)

    pl.semaphore_wait(barrier, len(peers))
    halo = remote(
        c_ref.at[pl.ds(0, HALO)], halo_ref, halo_sem.at[0], halo_sem.at[1], cell_peer((here + 31) % 32)
    )
    halo.start()
    dens_copies = []
    for r in range(1, 8):
        peer = (me + r) % 8
        copy = remote(dens_ref.at[0], dens_ref.at[r], dens_send.at[r], dens_recv.at[r], orb_peer(peer))
        copy.start()
        dens_copies.append(copy)

    for a in range(DEG):
        for y in range(LINES):
            for s in range(SIDE):
                start = PLANE * a + LINES * y + DEG * s
                if start + TILE > nodes:
                    piece = jnp.concatenate(
                        [c_ref[start:nodes, :], jnp.zeros((start + TILE - nodes, 128), jnp.float32)], axis=0
                    )
                else:
                    piece = c_ref[start:start + TILE, :]
                tile_ref[s, a, TILE * y:TILE * (y + 1), :] = piece
    halo.wait_recv()
    for y in range(LINES):
        for s in range(SIDE):
            start = LINES * y + DEG * s
            tile_ref[s, DEG, TILE * y:TILE * (y + 1), :] = halo_ref[start:start + TILE, :]

    def cell_values(r):
        span = slice(DEG * TILE * r, DEG * TILE * r + EDGE * TILE)
        return [
            jnp.concatenate([tile_ref[s, a, span, :] for a in range(EDGE)], axis=0)
            for s in range(SIDE)
        ]

    contrib = [jnp.zeros((24, 128), jnp.float32) for _ in range(TOUCH_DEV)]
    for r in range(SIDE):
        wide = thrice(proj_rows, split(jnp.concatenate(cell_values(r), axis=1)), ((1,), (0,)))
        for t in range(TOUCH_DEV):
            for s in range(SIDE):
                part = wide[24 * t:24 * t + 24, 128 * s:128 * (s + 1)]
                contrib[t] = contrib[t] + hot_ref[t, 10 + SIDE * r + s] * part
    for k in range(WINDOW):
        for m in range(ATOM_DEV):
            total = hot_ref[0, ATOM_DEV * k + m] * contrib[0]
            for t in range(1, TOUCH_DEV):
                total = total + hot_ref[t, ATOM_DEV * k + m] * contrib[t]
            give_ref[k, m] = total[:PROJ]
    gives = {}
    for k in (0, 4, 1, 3):
        copy = remote(
            give_ref.at[k], take_ref.at[k], give_send.at[k], give_recv.at[k],
            cell_peer((here + k + 32 - REACH) % 32),
        )
        copy.start()
        gives[k] = copy

    value_ref[...] = jnp.zeros_like(value_ref)

    def add_value(r, wide):
        for s in range(SIDE):
            for a in range(EDGE):
                span = slice(DEG * TILE * r, DEG * TILE * r + EDGE * TILE)
                value_ref[s, a, span, :] = (
                    value_ref[s, a, span, :]
                    + wide[EDGE * TILE * a:EDGE * TILE * (a + 1), 128 * s:128 * (s + 1)]
                )

    for r in range(SIDE):
        wide = jnp.concatenate(
            [value * scale_ref[SIDE * r + s] for s, value in enumerate(cell_values(r))], axis=1
        )
        add_value(r, thrice(stiff, split(wide), ((1,), (0,))))

    for k in (0, 4, 1, 3):
        gives[k].wait_recv()
    useds = {}
    for m in range(ATOM_DEV):
        total = give_ref[REACH, m]
        for k in (0, 1, 3, 4):
            total = total + take_ref[k, m]
        sums_ref[here, m] = total
        used_ref[m] = thrice(split(coup_ref[2 * here + m]), split(total), ((1,), (0,)))
        window_ref[REACH, m] = used_ref[m]
    for q in (0, 4, 1, 3):
        copy = remote(
            used_ref, window_ref.at[4 - q], used_send.at[4 - q], used_recv.at[4 - q],
            cell_peer((here + q + 32 - REACH) % 32),
        )
        copy.start()
        useds[4 - q] = copy

    for copy in dens_copies:
        copy.wait_recv()
    density = dens_ref[0]
    for r in range(1, 8):
        density = density + dens_ref[r]
    potential = ext_ref[...] - exchange_coef * cube_root(density + core_ref[...])
    pot_ref[...] = dot(
        jnp.broadcast_to(potential, (TILE, nodes)),
        (lax.broadcasted_iota(jnp.int32, (TILE, 128), 0) == 0).astype(jnp.float32),
        (((0,), (0,)), ((), ())), precision=highest,
    )

    for k in (0, 4, 1, 3):
        useds[k].wait_recv()
    back = []
    for t in range(TOUCH_DEV):
        total = jnp.zeros((PROJ, 128), jnp.float32)
        for k in range(WINDOW):
            for m in range(ATOM_DEV):
                total = total + hot_ref[t, ATOM_DEV * k + m] * window_ref[k, m]
        back.append(jnp.concatenate([total, jnp.zeros((24 - PROJ, 128), jnp.float32)], axis=0))
    for r in range(SIDE):
        wide = jnp.concatenate(
            [
                jnp.concatenate(
                    [
                        hot_ref[t, 10 + SIDE * r + s] * back[t]
                        for t in range(TOUCH_DEV)
                    ],
                    axis=0,
                )
                for s in range(SIDE)
            ],
            axis=1,
        )
        add_value(r, thrice(proj_cols, split(wide), ((1,), (0,))))

    top_ref[...] = jnp.zeros_like(top_ref)
    for y in range(LINES):
        for s in range(SIDE):
            start = LINES * y + DEG * s
            top_ref[start:start + TILE, :] = (
                top_ref[start:start + TILE, :] + value_ref[s, DEG, TILE * y:TILE * (y + 1), :]
            )
    top = remote(top_ref, under_ref, top_sem.at[0], top_sem.at[1], cell_peer((here + 1) % 32))
    top.start()

    current = c_ref[...]
    square = current * current
    numerator = jnp.sum(pot_ref[...] * square, axis=0, keepdims=True)
    for s in range(SIDE):
        for a in range(EDGE):
            numerator = numerator + jnp.sum(tile_ref[s, a] * value_ref[s, a], axis=0, keepdims=True)
    ray_all_ref[here, 0:1, :] = numerator
    ray_all_ref[here, 1:2, :] = jnp.sum(square, axis=0, keepdims=True)
    rays = []
    for r in range(1, 32):
        copy = remote(
            ray_all_ref.at[here], ray_all_ref.at[here], ray_send.at[r], ray_recv.at[r],
            cell_peer((here + r) % 32),
        )
        copy.start()
        rays.append(copy)

    image_ref[...] = jnp.zeros_like(image_ref)
    image_ref[0:nodes, :] = pot_ref[...] * current
    for a in range(DEG):
        for y in range(LINES):
            for s in range(SIDE):
                start = PLANE * a + LINES * y + DEG * s
                image_ref[start:start + TILE, :] = (
                    image_ref[start:start + TILE, :] + value_ref[s, a, TILE * y:TILE * (y + 1), :]
                )
    top.wait_recv()
    image_ref[0:PLANE, :] = image_ref[0:PLANE, :] + under_ref[0:PLANE, :]
    for copy in rays:
        copy.wait_recv()
    total = jnp.sum(ray_all_ref[...], axis=0)
    rayleigh = total[0:1, :] / (total[1:2, :] + tiny)
    ray_ref[...] = rayleigh
    image_ref[0:nodes, :] = current - step_size * (image_ref[0:nodes, :] - rayleigh * current)

    rows = []
    for r in (6, 2, 5, 3, 7, 1, 4):
        peer = (me + r) % 8
        first = pl.multiple_of(peer * ROWS, TILE)
        copy = remote(
            image_ref.at[pl.ds(first, ROWS)], rows_ref.at[me], rows_send.at[r], rows_recv.at[r],
            orb_peer(peer),
        )
        copy.start()
        rows.append(copy)
    sums = []
    for r in range(1, 32):
        copy = remote(
            sums_ref.at[here], sums_ref.at[here], sums_send.at[r], sums_recv.at[r],
            cell_peer((here + r) % 32),
        )
        copy.start()
        sums.append(copy)
    rows_ref[me] = image_ref[pl.ds(pl.multiple_of(me * ROWS, TILE), ROWS), :]
    for copy in rows + sums:
        copy.wait_recv()
    everything = [halo, top] + dens_copies + list(gives.values()) + list(useds.values()) + rays
    for copy in everything + rows + sums:
        copy.wait_send()


def trial_rows(
    orbitals, occupations, external, core_density, cell_scale, stiffness,
    touched_atom, touched_cells, projectors, coupling, collective_id,
):
    nodes = orbitals.shape[0]
    here = lax.axis_index(CELLS)
    mine = lax.dynamic_slice_in_dim(touched_atom, here * TOUCH_DEV, TOUCH_DEV)[:, None]
    column = jnp.arange(10 + 9, dtype=jnp.int32)[None, :]
    near = (mine - 2 * here + 2 * REACH + 64) % 64
    hot = (jnp.where(column < 10, near, touched_cells + 10) == column).astype(jnp.float32)
    scalars = pl.BlockSpec(memory_space=pltpu.SMEM)
    dma = lambda n: pltpu.SemaphoreType.DMA((n,))
    vmem = lambda *shape: pltpu.VMEM(shape, jnp.float32)
    return pl.pallas_call(
        trial_kernel,
        out_shape=(
            jax.ShapeDtypeStruct((8, ROWS, 128), jnp.float32),
            jax.ShapeDtypeStruct((1, 128), jnp.float32),
            jax.ShapeDtypeStruct((32, ATOM_DEV, PROJ, 128), jnp.float32),
        ),
        in_specs=[scalars] * 2 + [WHOLE] * 7,
        out_specs=(WHOLE,) * 3,
        scratch_shapes=[
            vmem(HALO, 128),
            vmem(SIDE, EDGE, LINES * TILE, 128),
            vmem(SIDE, EDGE, LINES * TILE, 128),
            vmem(8 * ROWS, 128),
            vmem(HALO, 128),
            vmem(HALO, 128),
            vmem(24 * TOUCH_DEV, CELL_NODES),
            vmem(WINDOW, ATOM_DEV, PROJ, 128),
            vmem(WINDOW, ATOM_DEV, PROJ, 128),
            vmem(ATOM_DEV, PROJ, 128),
            vmem(WINDOW, ATOM_DEV, PROJ, 128),
            vmem(8, 1, nodes),
            vmem(32, 2, 128),
            vmem(nodes, 128),
            dma(2), dma(8), dma(8), dma(5), dma(5), dma(5), dma(5),
            dma(2), dma(32), dma(32), dma(8), dma(8), dma(32), dma(32),
        ],
        compiler_params=pltpu.CompilerParams(
            collective_id=collective_id, has_side_effects=True, vmem_limit_bytes=48 * 1024 * 1024
        ),
    )(
        cell_scale, hot, orbitals, occupations.reshape(1, -1),
        external.reshape(1, -1), core_density.reshape(1, -1), stiffness, projectors, coupling,
    )


def owned_kernel(owner_ref, sums_ref, out_ref):
    here = lax.axis_index("xl") * 16 + lax.axis_index("z") * 2 + lax.axis_index("core")
    out_ref[...] = jnp.zeros_like(out_ref)

    def place(atom, count):
        held = owner_ref[atom, 0] == here

        @pl.when(held)
        def _():
            out_ref[jnp.minimum(count, OWN_CAP - 1)] = sums_ref[atom // ATOM_DEV, atom % ATOM_DEV]

        return count + jnp.where(held, 1, 0)

    lax.fori_loop(0, owner_ref.shape[0], place, 0)


def owned_rows(sums, atom_owner):
    return pl.pallas_call(
        owned_kernel,
        out_shape=jax.ShapeDtypeStruct((OWN_CAP, PROJ, 128), jnp.float32),
        in_specs=[pl.BlockSpec(memory_space=pltpu.SMEM), WHOLE],
        out_specs=WHOLE,
    )(atom_owner, sums)


def per_device(
    orbitals,
    occupations,
    external,
    core_density,
    cell_scale,
    stiffness,
    touched_atom,
    touched_cells,
    projectors,
    coupling,
    atom_owner,
):
    nodes = orbitals.shape[0]
    rows, rayleigh, sums = trial_rows(
        orbitals, occupations, external, core_density, cell_scale, stiffness,
        touched_atom, touched_cells, projectors, coupling, 1,
    )
    blocks = total_blocks(gram(rows), 2)
    solved = solve_rows(blocks, rows, 1.0 / (nodes * 32))
    back = exchange_rows(solved, 3)
    current = back.reshape(8 * ROWS, 128)[:nodes]
    return (current, rayleigh.reshape(-1), owned_rows(sums, atom_owner))


def solution(mesh):
    finer = Mesh(mesh.devices.reshape(2, 8, 2, 2, 4), ("xl", "z", "core", "xh", "y"))
    return jax.shard_map(
        per_device,
        mesh=finer,
        in_specs=(
            P(CELLS, ORBS),
            P(ORBS),
            P(CELLS),
            P(CELLS),
            P(CELLS),
            P(),
            P(),
            P(CELLS, None),
            P(CELLS, None, None, None),
            P(),
            P(),
        ),
        out_specs=(P(CELLS, ORBS), P(ORBS), P(CELLS, None, ORBS)),
        check_vma=False,
    )
```

```python
import functools
import math

import jax
import jax.numpy as jnp
from jax import lax
from jax.experimental import pallas as pl
from jax.experimental.pallas import tpu as pltpu
from jax.sharding import Mesh
from jax.sharding import PartitionSpec as P

DEG = 6
EDGE = 7
CELL_NODES = 343
SIDE = 3
PROJ = 18
ATOM_DEV = 2
REACH = 2
TOUCH_DEV = 6
OWN_CAP = 5
CELLS = ("xl", "z", "core")
ORBS = ("xh", "y")

highest = lax.Precision.HIGHEST
step_size = 0.1
exchange_coef = (3.0 / math.pi) ** (1.0 / 3.0)
tiny = 1e-06


ROWS = 272
PIECE = 288
SLOT = 18
MESH_ID = pl.DeviceIdType.MESH
WHOLE = pl.BlockSpec(memory_space=pltpu.VMEM)


def split(x):
    high = x.astype(jnp.bfloat16)
    low = (x - high.astype(jnp.float32)).astype(jnp.bfloat16)
    return high, low


def orb_peer(index):
    return {"xh": index // 4, "y": index % 4}


def site_peer(index):
    return {"xl": index // 8, "z": index % 8}


def my_orb():
    return lax.axis_index("xh") * 4 + lax.axis_index("y")


def my_site():
    return lax.axis_index("xl") * 8 + lax.axis_index("z")


def greet(peers):
    barrier = pltpu.get_barrier_semaphore()
    for peer in peers:
        pl.semaphore_signal(barrier, inc=1, device_id=peer, device_id_type=MESH_ID)
    pl.semaphore_wait(barrier, len(peers))


def remote(src, dst, send, recv, peer):
    return pltpu.make_async_remote_copy(
        src_ref=src, dst_ref=dst, send_sem=send, recv_sem=recv,
        device_id=peer, device_id_type=MESH_ID,
    )


def rows_back_kernel(t_ref, out_ref, full_ref, send, recv, own):
    me = my_orb()
    greet([orb_peer((me + r) % 8) for r in range(1, 8)])
    mine = pl.ds(pl.multiple_of(me * ROWS, 8), ROWS)
    copies = []
    for r in (6, 2, 5, 3, 7, 1, 4):
        peer = (me + r) % 8
        copy = remote(t_ref.at[peer], full_ref.at[mine], send.at[r], recv.at[r], orb_peer(peer))
        copy.start()
        copies.append(copy)
    local = pltpu.make_async_copy(t_ref.at[me], full_ref.at[mine], own)
    local.start()
    local.wait()
    for copy in copies:
        copy.wait()
    out_ref[...] = full_ref[0:out_ref.shape[0], :]


def rows_back(value, nodes, collective_id):
    return pl.pallas_call(
        rows_back_kernel,
        out_shape=jax.ShapeDtypeStruct((nodes, 128), jnp.float32),
        in_specs=[pl.BlockSpec(memory_space=pltpu.HBM)],
        out_specs=WHOLE,
        scratch_shapes=[
            pltpu.VMEM((8 * ROWS, 128), jnp.float32),
            pltpu.SemaphoreType.DMA((8,)), pltpu.SemaphoreType.DMA((8,)), pltpu.SemaphoreType.DMA,
        ],
        compiler_params=pltpu.CompilerParams(
            collective_id=collective_id, has_side_effects=True, vmem_limit_bytes=62 * 1024 * 1024
        ),
    )(value)


def gram(x_ref, out_ref, left_ref, right_ref):
    for j in range(8):
        high, low = split(x_ref[j])
        lanes = pl.ds(128 * j, 128)
        left_ref[0:ROWS, lanes] = high
        left_ref[ROWS:2 * ROWS, lanes] = low
        left_ref[2 * ROWS:3 * ROWS, lanes] = high
        right_ref[0:ROWS, lanes] = high
        right_ref[ROWS:2 * ROWS, lanes] = high
        right_ref[2 * ROWS:3 * ROWS, lanes] = low
    for i in range(8):
        product = lax.dot_general(
            left_ref[:, pl.ds(128 * i, 128)], right_ref[:, pl.ds(0, 128 * (i + 1))],
            (((0,), (0,)), ((), ())), preferred_element_type=jnp.float32,
        )
        for j in range(i + 1):
            block = i * (i + 1) // 2 + j
            out_ref[128 * block:128 * (block + 1), :] = product[:, 128 * j:128 * (j + 1)]


def total_over_all(
    m_ref, out_ref, pair_ref, mine_ref, orb_ref, sum_ref, cut_ref, site_ref, done_ref,
    pair_send, pair_recv, orb_send, orb_recv, site_send, site_recv,
    back_send, back_recv, home_send, home_recv, last_send, last_recv,
):
    core = lax.axis_index("core")
    me = my_orb()
    here = my_site()
    partner = {"core": 1 - core}
    order = (6, 2, 5, 3, 7, 1, 4)

    def part(half, piece):
        return pl.ds(pl.multiple_of((8 * half + piece) * PIECE, 8), PIECE)

    pending = []
    arrivals = {}
    for r in order + (0,):
        piece = (me + r) % 8
        copy = remote(
            m_ref.at[part(1 - core, piece)], pair_ref.at[piece], pair_send.at[r], pair_recv.at[r], partner
        )
        copy.start()
        arrivals[r] = copy
        pending.append(copy)
    firsts = []
    for r in order + (0,):
        piece = (me + r) % 8
        arrivals[r].wait_recv()
        mine_ref[piece] = m_ref[part(core, piece), :] + pair_ref[piece]
        if r:
            copy = remote(mine_ref.at[piece], orb_ref.at[r], orb_send.at[r], orb_recv.at[r], orb_peer(piece))
            copy.start()
            firsts.append(copy)
    total = mine_ref[me]
    for copy, r in zip(firsts, order):
        copy.wait_recv()
        total = total + orb_ref[r]
    sum_ref[...] = total
    for i in range(16):
        cut_ref[i] = sum_ref[SLOT * i:SLOT * (i + 1), :]
    seconds = []
    for r in range(1, 16):
        peer = (here + r) % 16
        copy = remote(cut_ref.at[peer], site_ref.at[r], site_send.at[r], site_recv.at[r], site_peer(peer))
        copy.start()
        seconds.append(copy)
    slot = cut_ref[here]
    for r, copy in enumerate(seconds, 1):
        copy.wait_recv()
        slot = slot + site_ref[r]
    done_ref[here] = slot
    thirds = []
    for r in range(1, 16):
        peer = (here + r) % 16
        copy = remote(done_ref.at[here], done_ref.at[here], back_send.at[r], back_recv.at[r], site_peer(peer))
        copy.start()
        thirds.append(copy)
    for copy in thirds:
        copy.wait_recv()
    for i in range(16):
        sum_ref[SLOT * i:SLOT * (i + 1), :] = done_ref[i]
    fourths = []
    for r in order:
        peer = (me + r) % 8
        copy = remote(sum_ref, out_ref.at[core, me], home_send.at[r], home_recv.at[r], orb_peer(peer))
        copy.start()
        fourths.append(copy)
    lasts = [remote(sum_ref, out_ref.at[core, me], last_send.at[0], last_recv.at[0], partner)]
    lasts[0].start()
    out_ref[core, me] = sum_ref[...]
    for copy, r in zip(fourths, order):
        source = (me + 8 - r) % 8
        copy.wait_recv()
        place = out_ref.at[core, source]
        forward = remote(place, place, last_send.at[r], last_recv.at[r], partner)
        forward.start()
        lasts.append(forward)
    for copy in lasts:
        copy.wait_recv()
    return pending + firsts + seconds + thirds + fourths + lasts


def product(x, y):
    xh, xl = split(x)
    yh, yl = split(y)
    right = jnp.concatenate([yh, yl], axis=1)
    both = jnp.dot(
        jnp.concatenate([xh, xl], axis=1), jnp.concatenate([right, right], axis=0),
        preferred_element_type=jnp.float32,
    )
    return both[:, :128] + both[:, 128:]


def twice(y):
    yh, yl = split(y)
    return jnp.concatenate(
        [jnp.concatenate([yh, yh], axis=1), jnp.concatenate([yl, yl], axis=1)], axis=0
    )


def against(pair, right):
    both = lax.dot_general(pair, right, (((1,), (1,)), ((), ())), preferred_element_type=jnp.float32)
    return both[:, :128] + both[:, 128:]


def pair_of(x):
    return jnp.concatenate(split(x), axis=1)


def place_owned(owner_ref, sums_ref, owned_ref):
    here = lax.axis_index("xl") * 16 + lax.axis_index("z") * 2 + lax.axis_index("core")
    owned_ref[...] = jnp.zeros_like(owned_ref)

    def place(atom, count):
        held = owner_ref[atom] == here

        @pl.when(held)
        def _():
            owned_ref[jnp.minimum(count, OWN_CAP - 1)] = sums_ref[atom // ATOM_DEV, atom % ATOM_DEV]

        return count + jnp.where(held, 1, 0)

    lax.fori_loop(0, owner_ref.shape[0], place, 0)


def solve_kernel(
    scale, owner_ref, m_ref, t_ref, sums_ref, ray_ref, out_ref, owned_ref, rayleigh_ref,
    panel_ref, left_ref, inv_ref, work_ref, unit_ref,
):
    rayleigh_ref[...] = ray_ref[...]
    place_owned(owner_ref, sums_ref, owned_ref)
    row = lax.broadcasted_iota(jnp.int32, (128, 128), 0)
    col = lax.broadcasted_iota(jnp.int32, (128, 128), 1)
    eye = (row == col).astype(jnp.float32)
    half = (row > col).astype(jnp.float32) + 0.5 * eye
    down, across = [], []
    for k in range(8):
        diagonal = m_ref[k * (k + 1) // 2 + k] * eye
        down.append(lax.rsqrt(jnp.sum(diagonal, axis=1, keepdims=True) * scale))
        across.append(lax.rsqrt(jnp.sum(diagonal, axis=0, keepdims=True) * scale))
    for j in range(8):
        for i in range(j, 8):
            block = m_ref[i * (i + 1) // 2 + j] * scale
            panel_ref[j, 128 * i:128 * (i + 1), :] = block * down[i] * across[j]
        panel_ref[j, 1024:1024 + ROWS, :] = t_ref[j] * across[j]
    bottom = 1024 + ROWS
    for k in range(8):
        block = panel_ref[k, 128 * k:128 * (k + 1), :]
        x = eye - half * (block - eye)
        for step in range(2):
            error = against(pair_of(product(x, block)), twice(x)) - eye
            x = x - product(half * error, x)
        inv_ref[...] = x

        def unfinished(state):
            return (state[0] < 12) & jnp.logical_not(state[1] < 3e-5)

        def improve(state):
            x = inv_ref[...]
            block = panel_ref[k, 128 * k:128 * (k + 1), :]
            error = against(pair_of(product(x, block)), twice(x)) - eye
            inv_ref[...] = x - product(half * error, x)
            return state[0] + 1, jnp.sum(error * error)

        left = lax.while_loop(unfinished, improve, (0, jnp.sum(error * error)))[1]

        @pl.when(jnp.logical_not(left < 3e-5))
        def _():
            work_ref[...] = panel_ref[k, 128 * k:128 * (k + 1), :]
            unit_ref[...] = eye

            def eliminate(j, carry):
                lane = (col == j).astype(jnp.float32)
                mine = work_ref[pl.ds(j, 1), :]
                unit = unit_ref[pl.ds(j, 1), :]
                pivot = jnp.sum(jnp.where(col[0:1] == j, mine, 0.0), axis=1, keepdims=True)
                whole = work_ref[...]
                column = jnp.sum(jnp.where(col == j, whole, 0.0), axis=1, keepdims=True)
                factor = jnp.where(row > j, column / pivot, 0.0)
                work_ref[...] = whole - factor * mine
                unit_ref[...] = unit_ref[...] - factor * unit
                inv_ref[pl.ds(j, 1), :] = unit * lax.rsqrt(pivot)
                return carry

            lax.fori_loop(0, 128, eliminate, 0)

        right = twice(inv_ref[...])
        starts = list(range(128 * (k + 1), 1024, 128)) + [1024, 1024 + ROWS // 2]
        for start in starts:
            size = 128 if start < 1024 else ROWS // 2
            value = against(pair_of(panel_ref[k, start:start + size, :]), right)
            if start < 1024:
                left_ref[start:start + size, :] = pair_of(value)
            else:
                out_ref[k, start - 1024:start - 1024 + size, :] = value
                if k < 7:
                    left_ref[start:start + size, :] = pair_of(value)
        for j in range(k + 1, 8):
            pair = left_ref[128 * j:128 * (j + 1), :]
            high, low = pair[:, :128], pair[:, 128:]
            right = jnp.concatenate(
                [jnp.concatenate([high, high], axis=1), jnp.concatenate([low, low], axis=1)], axis=0
            )
            for start in list(range(128 * j, 1024, 128)) + [1024, 1024 + ROWS // 2]:
                size = 128 if start < 1024 else ROWS // 2
                panel_ref[j, start:start + size, :] = panel_ref[j, start:start + size, :] - against(
                    left_ref[start:start + size, :], right
                )


def solve_rows(blocks, rows, scale, atom_owner, sums, rayleigh):
    return pl.pallas_call(
        functools.partial(solve_kernel, scale),
        out_shape=(
            jax.ShapeDtypeStruct((8, ROWS, 128), jnp.float32),
            jax.ShapeDtypeStruct((OWN_CAP, PROJ, 128), jnp.float32),
            jax.ShapeDtypeStruct((1, 128), jnp.float32),
        ),
        in_specs=[pl.BlockSpec(memory_space=pltpu.SMEM)] + [WHOLE] * 4,
        out_specs=(WHOLE,) * 3,
        scratch_shapes=[
            pltpu.VMEM((8, 1024 + ROWS, 128), jnp.float32),
            pltpu.VMEM((1024 + ROWS, 256), jnp.bfloat16),
            pltpu.VMEM((128, 128), jnp.float32),
            pltpu.VMEM((128, 128), jnp.float32),
            pltpu.VMEM((128, 128), jnp.float32),
        ],
        compiler_params=pltpu.CompilerParams(vmem_limit_bytes=62 * 1024 * 1024),
    )(atom_owner, blocks, rows, sums, rayleigh)


WINDOW = 2 * REACH + 1
TILE = 8
LINES = SIDE * DEG + 1
PLANE = LINES * LINES
HALO = 368
PADDED = EDGE * EDGE * TILE


def cell_peer(index):
    return {"xl": index // 16, "z": (index // 2) % 8, "core": index % 2}


def thrice(left, right, dims):
    lh, ll = left
    rh, rl = right
    dot = functools.partial(
        lax.dot_general, dimension_numbers=(dims, ((), ())), preferred_element_type=jnp.float32
    )
    return dot(lh, rh) + dot(ll, rh) + dot(lh, rl)


def cube_root(x):
    root = jnp.exp(jnp.log(x) * (1.0 / 3.0))
    for _ in range(2):
        root = root - (root * root * root - x) / (3.0 * root * root)
    return root


def trial_kernel(
    scale_ref, hot_ref,
    c_in, occ_in, ext_in, core_in, stiff_in, proj_in, coup_in,
    rows_ref, ray_ref, sums_ref, total_ref,
    c_ref, occ_ref, ext_ref, core_ref, stiff_ref, proj_ref, coup_ref, pick_ref, load_sem,
    halo_ref, tile_ref, value_ref, image_ref, top_ref, under_ref, proj24_ref,
    give_ref, take_ref, used_ref, window_ref, dens_ref, ray_all_ref, pot_ref,
    halo_sem, dens_send, dens_recv, give_send, give_recv, used_send, used_recv,
    top_sem, ray_send, ray_recv, rows_send, rows_recv, sums_send, sums_recv,
    gram_ref, left_ref, right_ref, *total_scratch,
):
    nodes = c_ref.shape[0]
    here = lax.axis_index("xl") * 16 + lax.axis_index("z") * 2 + lax.axis_index("core")
    me = my_orb()
    barrier = pltpu.get_barrier_semaphore()
    peers = [cell_peer((here + r) % 32) for r in range(1, 32)]
    peers += [orb_peer((me + r) % 8) for r in range(1, 8)]
    for peer in peers:
        pl.semaphore_signal(barrier, inc=1, device_id=peer, device_id_type=MESH_ID)
    loads = [
        pltpu.make_async_copy(source, target, load_sem.at[i])
        for i, (source, target) in enumerate(
            (
                (stiff_in, stiff_ref), (proj_in, proj_ref), (coup_in, coup_ref), (c_in, c_ref),
                (occ_in, occ_ref), (ext_in, ext_ref), (core_in, core_ref),
            )
        )
    ]
    for load in loads:
        load.start()
    node = lax.broadcasted_iota(jnp.int32, (CELL_NODES, PADDED), 0)
    place = lax.broadcasted_iota(jnp.int32, (CELL_NODES, PADDED), 1)
    inside = (place & 7) < EDGE
    match = node == EDGE * (place >> 3) + (place & 7)
    spot = jnp.where(inside & match, 1.0, 0.0).astype(jnp.bfloat16)
    dot = functools.partial(lax.dot_general, preferred_element_type=jnp.float32)

    def both_sides(part):
        wide = dot(part, spot, (((1,), (0,)), ((), ()))).astype(jnp.bfloat16)
        return dot(spot, wide, (((0,), (0,)), ((), ()))).astype(jnp.bfloat16)

    loads[0].wait()
    stiff = tuple(both_sides(part) for part in split(stiff_ref[...]))
    loads[1].wait()
    proj24_ref[...] = jnp.zeros_like(proj24_ref)
    for t in range(TOUCH_DEV):
        proj24_ref[24 * t:24 * t + PROJ, :] = proj_ref[t, :, 0, :]
    parts = split(proj24_ref[...])
    proj_rows = tuple(dot(p, spot, (((1,), (0,)), ((), ()))).astype(jnp.bfloat16) for p in parts)
    proj_cols = tuple(dot(spot, p, (((0,), (1,)), ((), ()))).astype(jnp.bfloat16) for p in parts)

    loads[2].wait()
    lane = lax.broadcasted_iota(jnp.int32, (PROJ, 64), 1)
    for m in range(ATOM_DEV):
        for p in range(PROJ):
            column = jnp.sum(jnp.where(lane == 2 * here + m, coup_ref[p], 0.0), axis=1, keepdims=True)
            pick_ref[m, p] = jnp.broadcast_to(column, (PROJ, 128))
    for load in loads[3:]:
        load.wait()
    current = c_ref[...]
    square = current * current
    density = thrice(split(jnp.broadcast_to(occ_ref[...].reshape(1, 128), (TILE, 128))), split(square), ((1,), (1,)))
    dens_ref[0] = density[0:1, :]

    pl.semaphore_wait(barrier, len(peers))
    halo = remote(
        c_ref.at[pl.ds(0, HALO)], halo_ref, halo_sem.at[0], halo_sem.at[1], cell_peer((here + 31) % 32)
    )
    halo.start()
    dens_copies = []
    for r in range(1, 8):
        peer = (me + r) % 8
        copy = remote(dens_ref.at[0], dens_ref.at[r], dens_send.at[r], dens_recv.at[r], orb_peer(peer))
        copy.start()
        dens_copies.append(copy)

    for a in range(DEG):
        for y in range(LINES):
            for s in range(SIDE):
                start = PLANE * a + LINES * y + DEG * s
                if start + TILE > nodes:
                    piece = jnp.concatenate(
                        [c_ref[start:nodes, :], jnp.zeros((start + TILE - nodes, 128), jnp.float32)], axis=0
                    )
                else:
                    piece = c_ref[start:start + TILE, :]
                tile_ref[s, a, TILE * y:TILE * (y + 1), :] = piece
    halo.wait_recv()
    for y in range(LINES):
        for s in range(SIDE):
            start = LINES * y + DEG * s
            tile_ref[s, DEG, TILE * y:TILE * (y + 1), :] = halo_ref[start:start + TILE, :]

    def cell_values(r):
        span = slice(DEG * TILE * r, DEG * TILE * r + EDGE * TILE)
        return [
            jnp.concatenate([tile_ref[s, a, span, :] for a in range(EDGE)], axis=0)
            for s in range(SIDE)
        ]

    contrib = [jnp.zeros((24, 128), jnp.float32) for _ in range(TOUCH_DEV)]
    for r in range(SIDE):
        wide = thrice(proj_rows, split(jnp.concatenate(cell_values(r), axis=1)), ((1,), (0,)))
        for t in range(TOUCH_DEV):
            for s in range(SIDE):
                part = wide[24 * t:24 * t + 24, 128 * s:128 * (s + 1)]
                contrib[t] = contrib[t] + hot_ref[10 + SIDE * r + s, t] * part
    for k in range(WINDOW):
        for m in range(ATOM_DEV):
            total = hot_ref[ATOM_DEV * k + m, 0] * contrib[0]
            for t in range(1, TOUCH_DEV):
                total = total + hot_ref[ATOM_DEV * k + m, t] * contrib[t]
            give_ref[k, m] = total[:PROJ]
    gives = {}
    for k in (0, 4, 1, 3):
        copy = remote(
            give_ref.at[k], take_ref.at[k], give_send.at[k], give_recv.at[k],
            cell_peer((here + k + 32 - REACH) % 32),
        )
        copy.start()
        gives[k] = copy

    value_ref[...] = jnp.zeros_like(value_ref)

    def add_value(r, wide):
        for s in range(SIDE):
            for a in range(EDGE):
                span = slice(DEG * TILE * r, DEG * TILE * r + EDGE * TILE)
                value_ref[s, a, span, :] = (
                    value_ref[s, a, span, :]
                    + wide[EDGE * TILE * a:EDGE * TILE * (a + 1), 128 * s:128 * (s + 1)]
                )

    for r in range(SIDE):
        wide = jnp.concatenate(
            [value * scale_ref[SIDE * r + s] for s, value in enumerate(cell_values(r))], axis=1
        )
        add_value(r, thrice(stiff, split(wide), ((1,), (0,))))

    for k in (0, 4, 1, 3):
        gives[k].wait_recv()
    useds = {}
    for m in range(ATOM_DEV):
        total = give_ref[REACH, m]
        for k in (0, 1, 3, 4):
            total = total + take_ref[k, m]
        sums_ref[here, m] = total
        for p in range(PROJ):
            used_ref[m, p:p + 1, :] = jnp.sum(pick_ref[m, p] * total, axis=0, keepdims=True)
        window_ref[REACH, m] = used_ref[m]
    for q in (0, 4, 1, 3):
        copy = remote(
            used_ref, window_ref.at[4 - q], used_send.at[4 - q], used_recv.at[4 - q],
            cell_peer((here + q + 32 - REACH) % 32),
        )
        copy.start()
        useds[4 - q] = copy

    for copy in dens_copies:
        copy.wait_recv()
    density = dens_ref[0]
    for r in range(1, 8):
        density = density + dens_ref[r]
    potential = ext_ref[...].reshape(1, nodes) - exchange_coef * cube_root(
        density + core_ref[...].reshape(1, nodes)
    )
    pot_ref[...] = dot(
        jnp.broadcast_to(potential, (TILE, nodes)),
        (lax.broadcasted_iota(jnp.int32, (TILE, 128), 0) == 0).astype(jnp.float32),
        (((0,), (0,)), ((), ())), precision=highest,
    )

    for k in (0, 4, 1, 3):
        useds[k].wait_recv()
    back = []
    for t in range(TOUCH_DEV):
        total = jnp.zeros((PROJ, 128), jnp.float32)
        for k in range(WINDOW):
            for m in range(ATOM_DEV):
                total = total + hot_ref[ATOM_DEV * k + m, t] * window_ref[k, m]
        back.append(jnp.concatenate([total, jnp.zeros((24 - PROJ, 128), jnp.float32)], axis=0))
    for r in range(SIDE):
        wide = jnp.concatenate(
            [
                jnp.concatenate(
                    [
                        hot_ref[10 + SIDE * r + s, t] * back[t]
                        for t in range(TOUCH_DEV)
                    ],
                    axis=0,
                )
                for s in range(SIDE)
            ],
            axis=1,
        )
        add_value(r, thrice(proj_cols, split(wide), ((1,), (0,))))

    top_ref[...] = jnp.zeros_like(top_ref)
    for y in range(LINES):
        for s in range(SIDE):
            start = LINES * y + DEG * s
            top_ref[start:start + TILE, :] = (
                top_ref[start:start + TILE, :] + value_ref[s, DEG, TILE * y:TILE * (y + 1), :]
            )
    top = remote(top_ref, under_ref, top_sem.at[0], top_sem.at[1], cell_peer((here + 1) % 32))
    top.start()

    current = c_ref[...]
    square = current * current
    numerator = jnp.sum(pot_ref[...] * square, axis=0, keepdims=True)
    for s in range(SIDE):
        for a in range(EDGE):
            numerator = numerator + jnp.sum(tile_ref[s, a] * value_ref[s, a], axis=0, keepdims=True)
    ray_all_ref[here, 0:1, :] = numerator
    ray_all_ref[here, 1:2, :] = jnp.sum(square, axis=0, keepdims=True)
    rays = []
    for r in range(1, 32):
        copy = remote(
            ray_all_ref.at[here], ray_all_ref.at[here], ray_send.at[r], ray_recv.at[r],
            cell_peer((here + r) % 32),
        )
        copy.start()
        rays.append(copy)

    image_ref[...] = jnp.zeros_like(image_ref)
    image_ref[0:nodes, :] = pot_ref[...] * current
    for a in range(DEG):
        for y in range(LINES):
            for s in range(SIDE):
                start = PLANE * a + LINES * y + DEG * s
                image_ref[start:start + TILE, :] = (
                    image_ref[start:start + TILE, :] + value_ref[s, a, TILE * y:TILE * (y + 1), :]
                )
    top.wait_recv()
    image_ref[0:PLANE, :] = image_ref[0:PLANE, :] + under_ref[0:PLANE, :]
    for copy in rays:
        copy.wait_recv()
    total = jnp.sum(ray_all_ref[...], axis=0)
    rayleigh = total[0:1, :] / (total[1:2, :] + tiny)
    ray_ref[...] = rayleigh
    image_ref[0:nodes, :] = current - step_size * (image_ref[0:nodes, :] - rayleigh * current)

    rows = []
    for r in (6, 2, 5, 3, 7, 1, 4):
        peer = (me + r) % 8
        first = pl.multiple_of(peer * ROWS, TILE)
        copy = remote(
            image_ref.at[pl.ds(first, ROWS)], rows_ref.at[me], rows_send.at[r], rows_recv.at[r],
            orb_peer(peer),
        )
        copy.start()
        rows.append(copy)
    sums = []
    for r in range(1, 32):
        copy = remote(
            sums_ref.at[here], sums_ref.at[here], sums_send.at[r], sums_recv.at[r],
            cell_peer((here + r) % 32),
        )
        copy.start()
        sums.append(copy)
    rows_ref[me] = image_ref[pl.ds(pl.multiple_of(me * ROWS, TILE), ROWS), :]
    for copy in rows:
        copy.wait_recv()
    gram(rows_ref, gram_ref, left_ref, right_ref)
    everything = total_over_all(gram_ref, total_ref, *total_scratch)
    for copy in sums:
        copy.wait_recv()
    everything += [halo, top] + dens_copies + list(gives.values()) + list(useds.values()) + rays
    for copy in everything + rows + sums:
        copy.wait_send()


def trial_rows(
    orbitals, occupations, external, core_density, cell_scale, stiffness,
    touched_atom, touched_cells, projectors, coupling, collective_id,
):
    nodes = orbitals.shape[0]
    here = lax.axis_index(CELLS)
    mine = lax.dynamic_slice_in_dim(touched_atom, here * TOUCH_DEV, TOUCH_DEV)[None, :]
    line = lax.broadcasted_iota(jnp.int32, (10 + 9, TOUCH_DEV), 0)
    near = mine - 2 * here + 2 * REACH
    near = jnp.where(near < 0, near + 64, jnp.where(near >= 64, near - 64, near))
    cells = touched_cells.reshape(1, -1) + 10
    hot = jnp.where(jnp.where(line < 10, near, cells) == line, 1.0, 0.0)
    scalars = pl.BlockSpec(memory_space=pltpu.SMEM)
    dma = lambda n: pltpu.SemaphoreType.DMA((n,))
    vmem = lambda *shape: pltpu.VMEM(shape, jnp.float32)
    return pl.pallas_call(
        trial_kernel,
        out_shape=(
            jax.ShapeDtypeStruct((8, ROWS, 128), jnp.float32),
            jax.ShapeDtypeStruct((1, 128), jnp.float32),
            jax.ShapeDtypeStruct((32, ATOM_DEV, PROJ, 128), jnp.float32),
            jax.ShapeDtypeStruct((2, 8, PIECE, 128), jnp.float32),
        ),
        in_specs=[scalars] * 2 + [pl.BlockSpec(memory_space=pltpu.HBM)] * 7,
        out_specs=(WHOLE,) * 4,
        scratch_shapes=[
            vmem(nodes, 128), vmem(128), vmem(nodes), vmem(nodes), vmem(CELL_NODES, CELL_NODES),
            vmem(TOUCH_DEV, PROJ, 1, CELL_NODES), vmem(PROJ, PROJ, 64), vmem(ATOM_DEV, PROJ, PROJ, 128),
            dma(7),
            vmem(HALO, 128),
            vmem(SIDE, EDGE, LINES * TILE, 128),
            vmem(SIDE, EDGE, LINES * TILE, 128),
            vmem(8 * ROWS, 128),
            vmem(HALO, 128),
            vmem(HALO, 128),
            vmem(24 * TOUCH_DEV, CELL_NODES),
            vmem(WINDOW, ATOM_DEV, PROJ, 128),
            vmem(WINDOW, ATOM_DEV, PROJ, 128),
            vmem(ATOM_DEV, PROJ, 128),
            vmem(WINDOW, ATOM_DEV, PROJ, 128),
            vmem(8, 1, nodes),
            vmem(32, 2, 128),
            vmem(nodes, 128),
            dma(2), dma(8), dma(8), dma(5), dma(5), dma(5), dma(5),
            dma(2), dma(32), dma(32), dma(8), dma(8), dma(32), dma(32),
            vmem(16 * PIECE, 128),
            pltpu.VMEM((3 * ROWS, 1024), jnp.bfloat16),
            pltpu.VMEM((3 * ROWS, 1024), jnp.bfloat16),
            vmem(8, PIECE, 128), vmem(8, PIECE, 128), vmem(8, PIECE, 128), vmem(PIECE, 128),
            vmem(16, SLOT, 128), vmem(16, SLOT, 128), vmem(16, SLOT, 128),
            dma(8), dma(8), dma(8), dma(8), dma(16), dma(16),
            dma(16), dma(16), dma(8), dma(8), dma(8), dma(8),
        ],
        compiler_params=pltpu.CompilerParams(
            collective_id=collective_id, has_side_effects=True, vmem_limit_bytes=62 * 1024 * 1024
        ),
    )(
        cell_scale, hot, orbitals, occupations,
        external, core_density, stiffness, projectors.transpose(0, 2, 1, 3), coupling.transpose(1, 2, 0),
    )


def per_device(
    orbitals,
    occupations,
    external,
    core_density,
    cell_scale,
    stiffness,
    touched_atom,
    touched_cells,
    projectors,
    coupling,
    atom_owner,
):
    nodes = orbitals.shape[0]
    rows, rayleigh, sums, blocks = trial_rows(
        orbitals, occupations, external, core_density, cell_scale, stiffness,
        touched_atom, touched_cells, projectors, coupling, 1,
    )
    solved, owned, rayleigh = solve_rows(
        blocks.reshape(36, 128, 128), rows, 1.0 / (nodes * 32), atom_owner.reshape(-1), sums, rayleigh
    )
    return (rows_back(solved, nodes, 2), rayleigh.reshape(-1), owned)


def solution(mesh):
    finer = Mesh(mesh.devices.reshape(2, 8, 2, 2, 4), ("xl", "z", "core", "xh", "y"))
    return jax.shard_map(
        per_device,
        mesh=finer,
        in_specs=(
            P(CELLS, ORBS),
            P(ORBS),
            P(CELLS),
            P(CELLS),
            P(CELLS),
            P(),
            P(),
            P(CELLS, None),
            P(CELLS, None, None, None),
            P(),
            P(),
        ),
        out_specs=(P(CELLS, ORBS), P(ORBS), P(CELLS, None, ORBS)),
        check_vma=False,
    )
```

```python
import functools
import math

import jax
import jax.numpy as jnp
from jax import lax
from jax.experimental import pallas as pl
from jax.experimental.pallas import tpu as pltpu
from jax.sharding import Mesh
from jax.sharding import PartitionSpec as P

DEG = 6
EDGE = 7
CELL_NODES = 343
SIDE = 3
PROJ = 18
ATOM_DEV = 2
REACH = 2
TOUCH_DEV = 6
OWN_CAP = 5
CELLS = ("xl", "z", "core")
ORBS = ("xh", "y")

highest = lax.Precision.HIGHEST
step_size = 0.1
exchange_coef = (3.0 / math.pi) ** (1.0 / 3.0)
tiny = 1e-06


ROWS = 272
EDGE_ROWS = 48
BODY_ROWS = 224
FORTH = 1536
ORB_PIECE, ORB_SLOT = 192, 12
SITE_PIECE, SITE_SLOT = 48, 6
MESH_ID = pl.DeviceIdType.MESH
WHOLE = pl.BlockSpec(memory_space=pltpu.VMEM)


def split(x):
    high = x.astype(jnp.bfloat16)
    low = (x - high.astype(jnp.float32)).astype(jnp.bfloat16)
    return high, low


def orb_peer(index):
    return {"xh": index // 4, "y": index % 4}


def site_peer(index):
    return {"xl": index // 8, "z": index % 8}


def my_orb():
    return lax.axis_index("xh") * 4 + lax.axis_index("y")


def my_site():
    return lax.axis_index("xl") * 8 + lax.axis_index("z")


def greet(peers):
    barrier = pltpu.get_barrier_semaphore()
    for peer in peers:
        pl.semaphore_signal(barrier, inc=1, device_id=peer, device_id_type=MESH_ID)
    pl.semaphore_wait(barrier, len(peers))


def remote(src, dst, send, recv, peer):
    return pltpu.make_async_remote_copy(
        src_ref=src, dst_ref=dst, send_sem=send, recv_sem=recv,
        device_id=peer, device_id_type=MESH_ID,
    )


def rows_back_kernel(t_ref, out_ref, full_ref, edge_sem, body_sem, own):
    me = my_orb()
    greet([orb_peer((me + r) % 8) for r in range(1, 8)])
    edge = pl.ds(pl.multiple_of(EDGE_ROWS * me, 8), EDGE_ROWS)
    body = pl.ds(pl.multiple_of(8 * EDGE_ROWS + BODY_ROWS * me, 8), BODY_ROWS)
    copies = []
    for r in (6, 2, 5, 3, 7, 1, 4):
        peer = (me + r) % 8
        for source, target, sems in (
            (pl.ds(EDGE_ROWS, BODY_ROWS), body, body_sem), (pl.ds(0, EDGE_ROWS), edge, edge_sem)
        ):
            copy = remote(
                t_ref.at[peer, source], full_ref.at[target], sems.at[0, r], sems.at[1, r], orb_peer(peer)
            )
            copy.start()
            copies.append(copy)
    locals_ = [
        pltpu.make_async_copy(t_ref.at[me, pl.ds(EDGE_ROWS, BODY_ROWS)], full_ref.at[body], own.at[0]),
        pltpu.make_async_copy(t_ref.at[me, pl.ds(0, EDGE_ROWS)], full_ref.at[edge], own.at[1]),
    ]
    for copy in locals_:
        copy.start()
    for copy in locals_ + copies:
        copy.wait()
    out_ref[...] = full_ref[0:out_ref.shape[0], :]


def rows_back(value, nodes, collective_id):
    return pl.pallas_call(
        rows_back_kernel,
        out_shape=jax.ShapeDtypeStruct((nodes, 128), jnp.float32),
        in_specs=[pl.BlockSpec(memory_space=pltpu.HBM)],
        out_specs=WHOLE,
        scratch_shapes=[
            pltpu.VMEM((8 * ROWS, 128), jnp.float32),
            pltpu.SemaphoreType.DMA((2, 8)), pltpu.SemaphoreType.DMA((2, 8)), pltpu.SemaphoreType.DMA((2,)),
        ],
        compiler_params=pltpu.CompilerParams(
            collective_id=collective_id, has_side_effects=True, vmem_limit_bytes=58 * 1024 * 1024
        ),
    )(value)


def gram(x_ref, out_ref, left_ref, right_ref):
    for j in range(8):
        high, low = split(x_ref[j])
        lanes = pl.ds(128 * j, 128)
        left_ref[0:ROWS, lanes] = high
        left_ref[ROWS:2 * ROWS, lanes] = low
        left_ref[2 * ROWS:3 * ROWS, lanes] = high
        right_ref[0:ROWS, lanes] = high
        right_ref[ROWS:2 * ROWS, lanes] = high
        right_ref[2 * ROWS:3 * ROWS, lanes] = low
    for i in range(8):
        product = lax.dot_general(
            left_ref[:, pl.ds(128 * i, 128)], right_ref[:, pl.ds(0, 128 * (i + 1))],
            (((0,), (0,)), ((), ())), preferred_element_type=jnp.float32,
        )
        for j in range(i + 1):
            block = i * (i + 1) // 2 + j
            out_ref[128 * block:128 * (block + 1), :] = product[:, 128 * j:128 * (j + 1)]


def total_over_all(
    m_ref, out_ref, pair_ref, mine_ref,
    orb_ref, sum_ref, cut_ref, site_ref, done_ref,
    orb2_ref, sum2_ref, cut2_ref, site2_ref, done2_ref,
    pair_sem, orb_sem, site_sem, back_sem, home_sem, last_sem,
    orb2_sem, site2_sem, back2_sem, home2_sem, last2_sem,
):
    core = lax.axis_index("core")
    me = my_orb()
    here = my_site()
    partner = {"core": 1 - core}
    order = (6, 2, 5, 3, 7, 1, 4)
    sites = (4, 12, 5, 3, 13, 11, 6, 2, 14, 10, 7, 1, 15, 9, 8)
    half = m_ref.shape[0] // 2
    every = []

    def rows(start, size, base=0):
        return pl.ds(pl.multiple_of(base + start, 8), size)

    def go(source, target, sems, index, peer):
        copy = remote(source, target, sems.at[0, index], sems.at[1, index], peer)
        copy.start()
        every.append(copy)
        return copy

    mine_base = core * half
    other_base = (1 - core) * half
    first = go(
        m_ref.at[rows(FORTH, half - FORTH, other_base)], pair_ref.at[pl.ds(FORTH, half - FORTH)],
        pair_sem, 8, partner,
    )
    arrivals = {}
    for r in order + (0,):
        start = ORB_PIECE * ((me + r) % 8)
        arrivals[r] = go(
            m_ref.at[rows(start, ORB_PIECE, other_base)], pair_ref.at[rows(start, ORB_PIECE)],
            pair_sem, r, partner,
        )
    first.wait_recv()
    mine_ref[FORTH:half, :] = m_ref[rows(FORTH, half - FORTH, mine_base), :] + pair_ref[FORTH:half, :]
    spread2 = {}
    for r in sites:
        peer = (here + r) % 16
        spread2[r] = go(
            mine_ref.at[rows(SITE_PIECE * peer, SITE_PIECE, FORTH)], site2_ref.at[r], site2_sem, r,
            site_peer(peer),
        )
    spread1 = {}
    for r in order + (0,):
        peer = (me + r) % 8
        start = ORB_PIECE * peer
        arrivals[r].wait_recv()
        mine_ref[rows(start, ORB_PIECE), :] = (
            m_ref[rows(start, ORB_PIECE, mine_base), :] + pair_ref[rows(start, ORB_PIECE), :]
        )
        if r:
            spread1[r] = go(
                mine_ref.at[rows(start, ORB_PIECE)], orb_ref.at[r], orb_sem, r, orb_peer(peer)
            )
    total = mine_ref[rows(SITE_PIECE * here, SITE_PIECE, FORTH), :]
    for r in sites:
        spread2[r].wait_recv()
        total = total + site2_ref[r]
    sum2_ref[...] = total
    for i in range(8):
        cut2_ref[i] = sum2_ref[SITE_SLOT * i:SITE_SLOT * (i + 1), :]
    inner2 = {}
    for r in order:
        peer = (me + r) % 8
        inner2[r] = go(cut2_ref.at[peer], orb2_ref.at[r], orb2_sem, r, orb_peer(peer))
    total = mine_ref[rows(ORB_PIECE * me, ORB_PIECE), :]
    for r in order:
        spread1[r].wait_recv()
        total = total + orb_ref[r]
    sum_ref[...] = total
    for i in range(16):
        cut_ref[i] = sum_ref[ORB_SLOT * i:ORB_SLOT * (i + 1), :]
    inner1 = {}
    for r in sites:
        peer = (here + r) % 16
        inner1[r] = go(cut_ref.at[peer], site_ref.at[r], site_sem, r, site_peer(peer))
    slot = cut2_ref[me]
    for r in order:
        inner2[r].wait_recv()
        slot = slot + orb2_ref[r]
    done2_ref[me] = slot
    outer2 = [
        go(done2_ref.at[me], done2_ref.at[me], back2_sem, r, orb_peer((me + r) % 8)) for r in order
    ]
    slot = cut_ref[here]
    for r in sites:
        inner1[r].wait_recv()
        slot = slot + site_ref[r]
    done_ref[here] = slot
    outer1 = [
        go(done_ref.at[here], done_ref.at[here], back_sem, r, site_peer((here + r) % 16)) for r in sites
    ]
    for copy in outer2:
        copy.wait_recv()
    for i in range(8):
        sum2_ref[SITE_SLOT * i:SITE_SLOT * (i + 1), :] = done2_ref[i]
    place2 = out_ref.at[rows(SITE_PIECE * here, SITE_PIECE, mine_base + FORTH)]
    homes2 = [
        (r, go(sum2_ref, place2, home2_sem, r, site_peer((here + r) % 16))) for r in sites
    ]
    lasts = [go(sum2_ref, place2, last2_sem, 0, partner)]
    out_ref[rows(SITE_PIECE * here, SITE_PIECE, mine_base + FORTH), :] = sum2_ref[...]
    for copy in outer1:
        copy.wait_recv()
    for i in range(16):
        sum_ref[ORB_SLOT * i:ORB_SLOT * (i + 1), :] = done_ref[i]
    place = out_ref.at[rows(ORB_PIECE * me, ORB_PIECE, mine_base)]
    homes1 = [(r, go(sum_ref, place, home_sem, r, orb_peer((me + r) % 8))) for r in order]
    lasts.append(go(sum_ref, place, last_sem, 0, partner))
    out_ref[rows(ORB_PIECE * me, ORB_PIECE, mine_base), :] = sum_ref[...]
    for r, copy in homes1:
        copy.wait_recv()
        place = out_ref.at[rows(ORB_PIECE * ((me + 8 - r) % 8), ORB_PIECE, mine_base)]
        lasts.append(go(place, place, last_sem, r, partner))
    for r, copy in homes2:
        copy.wait_recv()
        place = out_ref.at[rows(SITE_PIECE * ((here + 16 - r) % 16), SITE_PIECE, mine_base + FORTH)]
        lasts.append(go(place, place, last2_sem, r, partner))
    for copy in lasts:
        copy.wait_recv()
    return every


def product(x, y):
    xh, xl = split(x)
    yh, yl = split(y)
    right = jnp.concatenate([yh, yl], axis=1)
    both = jnp.dot(
        jnp.concatenate([xh, xl], axis=1), jnp.concatenate([right, right], axis=0),
        preferred_element_type=jnp.float32,
    )
    return both[:, :128] + both[:, 128:]


def twice(y):
    yh, yl = split(y)
    return jnp.concatenate(
        [jnp.concatenate([yh, yh], axis=1), jnp.concatenate([yl, yl], axis=1)], axis=0
    )


def against(pair, right):
    both = lax.dot_general(pair, right, (((1,), (1,)), ((), ())), preferred_element_type=jnp.float32)
    return both[:, :128] + both[:, 128:]


def pair_of(x):
    return jnp.concatenate(split(x), axis=1)


def place_owned(owner_ref, sums_ref, owned_ref):
    here = lax.axis_index("xl") * 16 + lax.axis_index("z") * 2 + lax.axis_index("core")
    owned_ref[...] = jnp.zeros_like(owned_ref)

    def place(atom, count):
        held = owner_ref[atom] == here

        @pl.when(held)
        def _():
            owned_ref[jnp.minimum(count, OWN_CAP - 1)] = sums_ref[atom // ATOM_DEV, atom % ATOM_DEV]

        return count + jnp.where(held, 1, 0)

    lax.fori_loop(0, owner_ref.shape[0], place, 0)


def solve_kernel(
    scale, owner_ref, m_ref, t_ref, sums_ref, ray_ref, out_ref, owned_ref, rayleigh_ref,
    panel_ref, left_ref, inv_ref, work_ref, unit_ref,
):
    rayleigh_ref[...] = ray_ref[...]
    place_owned(owner_ref, sums_ref, owned_ref)
    row = lax.broadcasted_iota(jnp.int32, (128, 128), 0)
    col = lax.broadcasted_iota(jnp.int32, (128, 128), 1)
    eye = (row == col).astype(jnp.float32)
    half = (row > col).astype(jnp.float32) + 0.5 * eye
    down, across = [], []
    for k in range(8):
        diagonal = m_ref[k * (k + 1) // 2 + k] * eye
        down.append(lax.rsqrt(jnp.sum(diagonal, axis=1, keepdims=True) * scale))
        across.append(lax.rsqrt(jnp.sum(diagonal, axis=0, keepdims=True) * scale))
    for j in range(8):
        for i in range(j, 8):
            block = m_ref[i * (i + 1) // 2 + j] * scale
            panel_ref[j, 128 * i:128 * (i + 1), :] = block * down[i] * across[j]
        panel_ref[j, 1024:1024 + ROWS, :] = t_ref[j] * across[j]
    bottom = 1024 + ROWS
    for k in range(8):
        block = panel_ref[k, 128 * k:128 * (k + 1), :]
        x = eye - half * (block - eye)
        for step in range(2):
            error = against(pair_of(product(x, block)), twice(x)) - eye
            x = x - product(half * error, x)
        inv_ref[...] = x

        def unfinished(state):
            return (state[0] < 12) & jnp.logical_not(state[1] < 3e-5)

        def improve(state):
            x = inv_ref[...]
            block = panel_ref[k, 128 * k:128 * (k + 1), :]
            error = against(pair_of(product(x, block)), twice(x)) - eye
            inv_ref[...] = x - product(half * error, x)
            return state[0] + 1, jnp.sum(error * error)

        left = lax.while_loop(unfinished, improve, (0, jnp.sum(error * error)))[1]

        @pl.when(jnp.logical_not(left < 3e-5))
        def _():
            work_ref[...] = panel_ref[k, 128 * k:128 * (k + 1), :]
            unit_ref[...] = eye

            def eliminate(j, carry):
                lane = (col == j).astype(jnp.float32)
                mine = work_ref[pl.ds(j, 1), :]
                unit = unit_ref[pl.ds(j, 1), :]
                pivot = jnp.sum(jnp.where(col[0:1] == j, mine, 0.0), axis=1, keepdims=True)
                whole = work_ref[...]
                column = jnp.sum(jnp.where(col == j, whole, 0.0), axis=1, keepdims=True)
                factor = jnp.where(row > j, column / pivot, 0.0)
                work_ref[...] = whole - factor * mine
                unit_ref[...] = unit_ref[...] - factor * unit
                inv_ref[pl.ds(j, 1), :] = unit * lax.rsqrt(pivot)
                return carry

            lax.fori_loop(0, 128, eliminate, 0)

        right = twice(inv_ref[...])
        starts = list(range(128 * (k + 1), 1024, 128)) + [1024, 1024 + ROWS // 2]
        for start in starts:
            size = 128 if start < 1024 else ROWS // 2
            value = against(pair_of(panel_ref[k, start:start + size, :]), right)
            if start < 1024:
                left_ref[start:start + size, :] = pair_of(value)
            else:
                out_ref[k, start - 1024:start - 1024 + size, :] = value
                if k < 7:
                    left_ref[start:start + size, :] = pair_of(value)
        for j in range(k + 1, 8):
            pair = left_ref[128 * j:128 * (j + 1), :]
            high, low = pair[:, :128], pair[:, 128:]
            right = jnp.concatenate(
                [jnp.concatenate([high, high], axis=1), jnp.concatenate([low, low], axis=1)], axis=0
            )
            for start in list(range(128 * j, 1024, 128)) + [1024, 1024 + ROWS // 2]:
                size = 128 if start < 1024 else ROWS // 2
                panel_ref[j, start:start + size, :] = panel_ref[j, start:start + size, :] - against(
                    left_ref[start:start + size, :], right
                )


def solve_rows(blocks, rows, scale, atom_owner, sums, rayleigh):
    return pl.pallas_call(
        functools.partial(solve_kernel, scale),
        out_shape=(
            jax.ShapeDtypeStruct((8, ROWS, 128), jnp.float32),
            jax.ShapeDtypeStruct((OWN_CAP, PROJ, 128), jnp.float32),
            jax.ShapeDtypeStruct((1, 128), jnp.float32),
        ),
        in_specs=[pl.BlockSpec(memory_space=pltpu.SMEM)] + [WHOLE] * 4,
        out_specs=(WHOLE,) * 3,
        scratch_shapes=[
            pltpu.VMEM((8, 1024 + ROWS, 128), jnp.float32),
            pltpu.VMEM((1024 + ROWS, 256), jnp.bfloat16),
            pltpu.VMEM((128, 128), jnp.float32),
            pltpu.VMEM((128, 128), jnp.float32),
            pltpu.VMEM((128, 128), jnp.float32),
        ],
        compiler_params=pltpu.CompilerParams(vmem_limit_bytes=62 * 1024 * 1024),
    )(atom_owner, blocks, rows, sums, rayleigh)


WINDOW = 2 * REACH + 1
TILE = 8
LINES = SIDE * DEG + 1
PLANE = LINES * LINES
HALO = 368
PADDED = EDGE * EDGE * TILE


def cell_peer(index):
    return {"xl": index // 16, "z": (index // 2) % 8, "core": index % 2}


def thrice(left, right, dims):
    lh, ll = left
    rh, rl = right
    dot = functools.partial(
        lax.dot_general, dimension_numbers=(dims, ((), ())), preferred_element_type=jnp.float32
    )
    return dot(lh, rh) + dot(ll, rh) + dot(lh, rl)


def cube_root(x):
    root = jnp.exp(jnp.log(x) * (1.0 / 3.0))
    for _ in range(2):
        root = root - (root * root * root - x) / (3.0 * root * root)
    return root


def trial_kernel(
    scale_ref, hot_ref,
    c_in, occ_in, ext_in, core_in, stiff_in, proj_in, coup_in,
    rows_ref, ray_ref, sums_ref, total_ref,
    c_ref, occ_ref, ext_ref, core_ref, stiff_ref, proj_ref, coup_ref, pick_ref, load_sem,
    halo_ref, tile_ref, value_ref, image_ref, top_ref, under_ref, proj24_ref,
    give_ref, take_ref, used_ref, window_ref, dens_ref, ray_all_ref, pot_ref,
    halo_sem, dens_send, dens_recv, give_send, give_recv, used_send, used_recv,
    top_sem, ray_send, ray_recv, sums_send, sums_recv,
    pad_ref, now_ref, move_ref, rays_ref, early_sem, body_sem, edge_sem, share_sem,
    gram_ref, left_ref, right_ref, *total_scratch,
):
    nodes = c_ref.shape[0]
    here = lax.axis_index("xl") * 16 + lax.axis_index("z") * 2 + lax.axis_index("core")
    me = my_orb()
    barrier = pltpu.get_barrier_semaphore()
    peers = [cell_peer((here + r) % 32) for r in range(1, 32)]
    peers += [orb_peer((me + r) % 8) for r in range(1, 8)]
    for peer in peers:
        pl.semaphore_signal(barrier, inc=1, device_id=peer, device_id_type=MESH_ID)
    loads = [
        pltpu.make_async_copy(source, target, load_sem.at[i])
        for i, (source, target) in enumerate(
            (
                (stiff_in, stiff_ref), (proj_in, proj_ref), (coup_in, coup_ref), (c_in, c_ref),
                (occ_in, occ_ref), (ext_in, ext_ref), (core_in, core_ref),
            )
        )
    ]
    for load in loads:
        load.start()
    node = lax.broadcasted_iota(jnp.int32, (CELL_NODES, PADDED), 0)
    place = lax.broadcasted_iota(jnp.int32, (CELL_NODES, PADDED), 1)
    inside = (place & 7) < EDGE
    match = node == EDGE * (place >> 3) + (place & 7)
    spot = jnp.where(inside & match, 1.0, 0.0).astype(jnp.bfloat16)
    dot = functools.partial(lax.dot_general, preferred_element_type=jnp.float32)

    def both_sides(part):
        wide = dot(part, spot, (((1,), (0,)), ((), ()))).astype(jnp.bfloat16)
        return dot(spot, wide, (((0,), (0,)), ((), ()))).astype(jnp.bfloat16)

    loads[0].wait()
    stiff = tuple(both_sides(part) for part in split(stiff_ref[...]))
    loads[1].wait()
    proj24_ref[...] = jnp.zeros_like(proj24_ref)
    for t in range(TOUCH_DEV):
        proj24_ref[24 * t:24 * t + PROJ, :] = proj_ref[t, :, 0, :]
    parts = split(proj24_ref[...])
    proj_rows = tuple(dot(p, spot, (((1,), (0,)), ((), ()))).astype(jnp.bfloat16) for p in parts)
    proj_cols = tuple(dot(spot, p, (((0,), (1,)), ((), ()))).astype(jnp.bfloat16) for p in parts)

    loads[2].wait()
    lane = lax.broadcasted_iota(jnp.int32, (PROJ, 64), 1)
    for m in range(ATOM_DEV):
        for p in range(PROJ):
            column = jnp.sum(jnp.where(lane == 2 * here + m, coup_ref[p], 0.0), axis=1, keepdims=True)
            pick_ref[m, p] = jnp.broadcast_to(column, (PROJ, 128))
    for load in loads[3:]:
        load.wait()
    current = c_ref[...]
    square = current * current
    density = thrice(split(jnp.broadcast_to(occ_ref[...].reshape(1, 128), (TILE, 128))), split(square), ((1,), (1,)))
    dens_ref[0] = density[0:1, :]

    pad_ref[0:nodes, :] = current
    pad_ref[nodes:8 * ROWS, :] = jnp.zeros((8 * ROWS - nodes, 128), jnp.float32)
    pl.semaphore_wait(barrier, len(peers))
    halo = remote(
        c_ref.at[pl.ds(0, HALO)], halo_ref, halo_sem.at[0], halo_sem.at[1], cell_peer((here + 31) % 32)
    )
    halo.start()
    dens_copies = []
    for r in range(1, 8):
        peer = (me + r) % 8
        copy = remote(dens_ref.at[0], dens_ref.at[r], dens_send.at[r], dens_recv.at[r], orb_peer(peer))
        copy.start()
        dens_copies.append(copy)

    order = (6, 2, 5, 3, 7, 1, 4)

    def edge(index):
        return pl.ds(pl.multiple_of(EDGE_ROWS * index, 8), EDGE_ROWS)

    def body(index):
        return pl.ds(pl.multiple_of(8 * EDGE_ROWS + BODY_ROWS * index, 8), BODY_ROWS)

    early = []
    for r in order:
        peer = (me + r) % 8
        for source, target, i in (
            (body(peer), pl.ds(EDGE_ROWS, BODY_ROWS), 0), (edge(peer), pl.ds(0, EDGE_ROWS), 2)
        ):
            copy = remote(
                pad_ref.at[source], now_ref.at[me, target], early_sem.at[i, r], early_sem.at[i + 1, r],
                orb_peer(peer),
            )
            copy.start()
            early.append(copy)
    now_ref[me, 0:EDGE_ROWS, :] = pad_ref[edge(me), :]
    now_ref[me, EDGE_ROWS:ROWS, :] = pad_ref[body(me), :]

    for a in range(DEG):
        for y in range(LINES):
            for s in range(SIDE):
                start = PLANE * a + LINES * y + DEG * s
                if start + TILE > nodes:
                    piece = jnp.concatenate(
                        [c_ref[start:nodes, :], jnp.zeros((start + TILE - nodes, 128), jnp.float32)], axis=0
                    )
                else:
                    piece = c_ref[start:start + TILE, :]
                tile_ref[s, a, TILE * y:TILE * (y + 1), :] = piece
    halo.wait_recv()
    for y in range(LINES):
        for s in range(SIDE):
            start = LINES * y + DEG * s
            tile_ref[s, DEG, TILE * y:TILE * (y + 1), :] = halo_ref[start:start + TILE, :]

    def cell_values(r):
        span = slice(DEG * TILE * r, DEG * TILE * r + EDGE * TILE)
        return [
            jnp.concatenate([tile_ref[s, a, span, :] for a in range(EDGE)], axis=0)
            for s in range(SIDE)
        ]

    contrib = [jnp.zeros((24, 128), jnp.float32) for _ in range(TOUCH_DEV)]
    for r in range(SIDE):
        wide = thrice(proj_rows, split(jnp.concatenate(cell_values(r), axis=1)), ((1,), (0,)))
        for t in range(TOUCH_DEV):
            for s in range(SIDE):
                part = wide[24 * t:24 * t + 24, 128 * s:128 * (s + 1)]
                contrib[t] = contrib[t] + hot_ref[10 + SIDE * r + s, t] * part
    for k in range(WINDOW):
        for m in range(ATOM_DEV):
            total = hot_ref[ATOM_DEV * k + m, 0] * contrib[0]
            for t in range(1, TOUCH_DEV):
                total = total + hot_ref[ATOM_DEV * k + m, t] * contrib[t]
            give_ref[k, m] = total[:PROJ]
    gives = {}
    for k in (0, 4, 1, 3):
        copy = remote(
            give_ref.at[k], take_ref.at[k], give_send.at[k], give_recv.at[k],
            cell_peer((here + k + 32 - REACH) % 32),
        )
        copy.start()
        gives[k] = copy

    value_ref[...] = jnp.zeros_like(value_ref)

    def add_value(r, wide):
        for s in range(SIDE):
            for a in range(EDGE):
                span = slice(DEG * TILE * r, DEG * TILE * r + EDGE * TILE)
                value_ref[s, a, span, :] = (
                    value_ref[s, a, span, :]
                    + wide[EDGE * TILE * a:EDGE * TILE * (a + 1), 128 * s:128 * (s + 1)]
                )

    for r in range(SIDE):
        wide = jnp.concatenate(
            [value * scale_ref[SIDE * r + s] for s, value in enumerate(cell_values(r))], axis=1
        )
        add_value(r, thrice(stiff, split(wide), ((1,), (0,))))

    for k in (0, 4, 1, 3):
        gives[k].wait_recv()
    useds = {}
    for m in range(ATOM_DEV):
        total = give_ref[REACH, m]
        for k in (0, 1, 3, 4):
            total = total + take_ref[k, m]
        sums_ref[here, m] = total
        for p in range(PROJ):
            used_ref[m, p:p + 1, :] = jnp.sum(pick_ref[m, p] * total, axis=0, keepdims=True)
        window_ref[REACH, m] = used_ref[m]
    for q in (0, 4, 1, 3):
        copy = remote(
            used_ref, window_ref.at[4 - q], used_send.at[4 - q], used_recv.at[4 - q],
            cell_peer((here + q + 32 - REACH) % 32),
        )
        copy.start()
        useds[4 - q] = copy

    for copy in dens_copies:
        copy.wait_recv()
    density = dens_ref[0]
    for r in range(1, 8):
        density = density + dens_ref[r]
    potential = ext_ref[...].reshape(1, nodes) - exchange_coef * cube_root(
        density + core_ref[...].reshape(1, nodes)
    )
    pot_ref[...] = dot(
        jnp.broadcast_to(potential, (TILE, nodes)),
        (lax.broadcasted_iota(jnp.int32, (TILE, 128), 0) == 0).astype(jnp.float32),
        (((0,), (0,)), ((), ())), precision=highest,
    )

    for k in (0, 4, 1, 3):
        useds[k].wait_recv()
    back = []
    for t in range(TOUCH_DEV):
        total = jnp.zeros((PROJ, 128), jnp.float32)
        for k in range(WINDOW):
            for m in range(ATOM_DEV):
                total = total + hot_ref[ATOM_DEV * k + m, t] * window_ref[k, m]
        back.append(jnp.concatenate([total, jnp.zeros((24 - PROJ, 128), jnp.float32)], axis=0))
    for r in range(SIDE):
        wide = jnp.concatenate(
            [
                jnp.concatenate(
                    [
                        hot_ref[10 + SIDE * r + s, t] * back[t]
                        for t in range(TOUCH_DEV)
                    ],
                    axis=0,
                )
                for s in range(SIDE)
            ],
            axis=1,
        )
        add_value(r, thrice(proj_cols, split(wide), ((1,), (0,))))

    top_ref[...] = jnp.zeros_like(top_ref)
    for y in range(LINES):
        for s in range(SIDE):
            start = LINES * y + DEG * s
            top_ref[start:start + TILE, :] = (
                top_ref[start:start + TILE, :] + value_ref[s, DEG, TILE * y:TILE * (y + 1), :]
            )
    top = remote(top_ref, under_ref, top_sem.at[0], top_sem.at[1], cell_peer((here + 1) % 32))
    top.start()

    current = c_ref[...]
    square = current * current
    numerator = jnp.sum(pot_ref[...] * square, axis=0, keepdims=True)
    for s in range(SIDE):
        for a in range(EDGE):
            numerator = numerator + jnp.sum(tile_ref[s, a] * value_ref[s, a], axis=0, keepdims=True)
    ray_all_ref[here, 0:1, :] = numerator
    ray_all_ref[here, 1:2, :] = jnp.sum(square, axis=0, keepdims=True)
    rays = []
    for r in range(1, 32):
        copy = remote(
            ray_all_ref.at[here], ray_all_ref.at[here], ray_send.at[r], ray_recv.at[r],
            cell_peer((here + r) % 32),
        )
        copy.start()
        rays.append(copy)

    image_ref[...] = jnp.zeros_like(image_ref)
    image_ref[0:nodes, :] = pot_ref[...] * current
    for a in range(DEG):
        for y in range(LINES):
            for s in range(SIDE):
                start = PLANE * a + LINES * y + DEG * s
                image_ref[start:start + TILE, :] = (
                    image_ref[start:start + TILE, :] + value_ref[s, a, TILE * y:TILE * (y + 1), :]
                )
    bodies = []
    for r in order:
        peer = (me + r) % 8
        copy = remote(
            image_ref.at[body(peer)], move_ref.at[me, pl.ds(EDGE_ROWS, BODY_ROWS)],
            body_sem.at[0, r], body_sem.at[1, r], orb_peer(peer),
        )
        copy.start()
        bodies.append(copy)
    move_ref[me, EDGE_ROWS:ROWS, :] = image_ref[body(me), :]
    top.wait_recv()
    image_ref[0:PLANE, :] = image_ref[0:PLANE, :] + under_ref[0:PLANE, :]
    edges = []
    for r in order:
        peer = (me + r) % 8
        copy = remote(
            image_ref.at[edge(peer)], move_ref.at[me, pl.ds(0, EDGE_ROWS)],
            edge_sem.at[0, r], edge_sem.at[1, r], orb_peer(peer),
        )
        copy.start()
        edges.append(copy)
    move_ref[me, 0:EDGE_ROWS, :] = image_ref[edge(me), :]
    for copy in rays:
        copy.wait_recv()
    total = jnp.sum(ray_all_ref[...], axis=0)
    rayleigh = total[0:1, :] / (total[1:2, :] + tiny)
    ray_ref[...] = rayleigh
    rays_ref[me] = rayleigh
    shares = []
    for r in order:
        copy = remote(
            rays_ref.at[me], rays_ref.at[me], share_sem.at[0, r], share_sem.at[1, r],
            orb_peer((me + r) % 8),
        )
        copy.start()
        shares.append(copy)
    sums = []
    for r in range(1, 16):
        copy = remote(
            sums_ref.at[here], sums_ref.at[here], sums_send.at[r], sums_recv.at[r],
            site_peer((my_site() + r) % 16),
        )
        copy.start()
        sums.append(copy)
    for copy in early + shares + bodies + edges:
        copy.wait_recv()
    for j in range(8):
        now = now_ref[j]
        rows_ref[j] = now - step_size * (move_ref[j] - rays_ref[j] * now)
    gram(rows_ref, gram_ref, left_ref, right_ref)
    core = lax.axis_index("core")
    passed = []
    for r in range(16):
        if r:
            sums[r - 1].wait_recv()
        held = sums_ref.at[2 * ((my_site() + 16 - r) % 16) + core]
        copy = remote(held, held, sums_send.at[16 + r], sums_recv.at[16 + r], {"core": 1 - core})
        copy.start()
        passed.append(copy)
    everything = total_over_all(gram_ref, total_ref, *total_scratch)
    for copy in passed:
        copy.wait_recv()
    everything += passed
    everything += [halo, top] + dens_copies + list(gives.values()) + list(useds.values()) + rays
    for copy in everything + early + shares + bodies + edges + sums:
        copy.wait_send()


def trial_rows(
    orbitals, occupations, external, core_density, cell_scale, stiffness,
    touched_atom, touched_cells, projectors, coupling, collective_id,
):
    nodes = orbitals.shape[0]
    here = lax.axis_index(CELLS)
    mine = lax.dynamic_slice_in_dim(touched_atom, here * TOUCH_DEV, TOUCH_DEV)[None, :]
    line = lax.broadcasted_iota(jnp.int32, (10 + 9, TOUCH_DEV), 0)
    near = mine - 2 * here + 2 * REACH
    near = jnp.where(near < 0, near + 64, jnp.where(near >= 64, near - 64, near))
    cells = touched_cells.reshape(1, -1) + 10
    hot = jnp.where(jnp.where(line < 10, near, cells) == line, 1.0, 0.0)
    scalars = pl.BlockSpec(memory_space=pltpu.SMEM)
    dma = lambda *n: pltpu.SemaphoreType.DMA(n)
    vmem = lambda *shape: pltpu.VMEM(shape, jnp.float32)
    return pl.pallas_call(
        trial_kernel,
        out_shape=(
            jax.ShapeDtypeStruct((8, ROWS, 128), jnp.float32),
            jax.ShapeDtypeStruct((1, 128), jnp.float32),
            jax.ShapeDtypeStruct((32, ATOM_DEV, PROJ, 128), jnp.float32),
            jax.ShapeDtypeStruct((36 * 128, 128), jnp.float32),
        ),
        in_specs=[scalars] * 2 + [pl.BlockSpec(memory_space=pltpu.HBM)] * 7,
        out_specs=(WHOLE,) * 4,
        scratch_shapes=[
            vmem(nodes, 128), vmem(128), vmem(nodes), vmem(nodes), vmem(CELL_NODES, CELL_NODES),
            vmem(TOUCH_DEV, PROJ, 1, CELL_NODES), vmem(PROJ, PROJ, 64), vmem(ATOM_DEV, PROJ, PROJ, 128),
            dma(7),
            vmem(HALO, 128),
            vmem(SIDE, EDGE, LINES * TILE, 128),
            vmem(SIDE, EDGE, LINES * TILE, 128),
            vmem(8 * ROWS, 128),
            vmem(HALO, 128),
            vmem(HALO, 128),
            vmem(24 * TOUCH_DEV, CELL_NODES),
            vmem(WINDOW, ATOM_DEV, PROJ, 128),
            vmem(WINDOW, ATOM_DEV, PROJ, 128),
            vmem(ATOM_DEV, PROJ, 128),
            vmem(WINDOW, ATOM_DEV, PROJ, 128),
            vmem(8, 1, nodes),
            vmem(32, 2, 128),
            vmem(nodes, 128),
            dma(2), dma(8), dma(8), dma(5), dma(5), dma(5), dma(5),
            dma(2), dma(32), dma(32), dma(32), dma(32),
            vmem(8 * ROWS, 128), vmem(8, ROWS, 128), vmem(8, ROWS, 128), vmem(8, 1, 128),
            dma(4, 8), dma(2, 8), dma(2, 8), dma(2, 8),
            vmem(36 * 128, 128),
            pltpu.VMEM((3 * ROWS, 1024), jnp.bfloat16),
            pltpu.VMEM((3 * ROWS, 1024), jnp.bfloat16),
            vmem(18 * 128, 128), vmem(18 * 128, 128),
            vmem(8, ORB_PIECE, 128), vmem(ORB_PIECE, 128), vmem(16, ORB_SLOT, 128),
            vmem(16, ORB_SLOT, 128), vmem(16, ORB_SLOT, 128),
            vmem(8, SITE_SLOT, 128), vmem(SITE_PIECE, 128), vmem(8, SITE_SLOT, 128),
            vmem(16, SITE_PIECE, 128), vmem(8, SITE_SLOT, 128),
            dma(2, 9), dma(2, 8), dma(2, 16), dma(2, 16), dma(2, 8), dma(2, 8),
            dma(2, 8), dma(2, 16), dma(2, 8), dma(2, 16), dma(2, 16),
        ],
        compiler_params=pltpu.CompilerParams(
            collective_id=collective_id, has_side_effects=True, vmem_limit_bytes=62 * 1024 * 1024
        ),
    )(
        cell_scale, hot, orbitals, occupations,
        external, core_density, stiffness, projectors.transpose(0, 2, 1, 3), coupling.transpose(1, 2, 0),
    )


def per_device(
    orbitals,
    occupations,
    external,
    core_density,
    cell_scale,
    stiffness,
    touched_atom,
    touched_cells,
    projectors,
    coupling,
    atom_owner,
):
    nodes = orbitals.shape[0]
    rows, rayleigh, sums, blocks = trial_rows(
        orbitals, occupations, external, core_density, cell_scale, stiffness,
        touched_atom, touched_cells, projectors, coupling, 1,
    )
    solved, owned, rayleigh = solve_rows(
        blocks.reshape(36, 128, 128), rows, 1.0 / (nodes * 32), atom_owner.reshape(-1), sums, rayleigh
    )
    return (rows_back(solved, nodes, 2), rayleigh.reshape(-1), owned)


def solution(mesh):
    finer = Mesh(mesh.devices.reshape(2, 8, 2, 2, 4), ("xl", "z", "core", "xh", "y"))
    return jax.shard_map(
        per_device,
        mesh=finer,
        in_specs=(
            P(CELLS, ORBS),
            P(ORBS),
            P(CELLS),
            P(CELLS),
            P(CELLS),
            P(),
            P(),
            P(CELLS, None),
            P(CELLS, None, None, None),
            P(),
            P(),
        ),
        out_specs=(P(CELLS, ORBS), P(ORBS), P(CELLS, None, ORBS)),
        check_vma=False,
    )
```

```python
import functools
import math

import jax
import jax.numpy as jnp
from jax import lax
from jax.experimental import pallas as pl
from jax.experimental.pallas import tpu as pltpu
from jax.sharding import Mesh
from jax.sharding import PartitionSpec as P

DEG = 6
EDGE = 7
CELL_NODES = 343
SIDE = 3
PROJ = 18
ATOM_DEV = 2
REACH = 2
TOUCH_DEV = 6
OWN_CAP = 5
CELLS = ("xl", "z", "core")
ORBS = ("xh", "y")

highest = lax.Precision.HIGHEST
step_size = 0.1
exchange_coef = (3.0 / math.pi) ** (1.0 / 3.0)
tiny = 1e-06


ROWS = 272
EDGE_ROWS = 48
BODY_ROWS = 224
FORTH = 1536
ORB_PIECE, ORB_SLOT = 192, 12
SITE_PIECE, SITE_SLOT = 48, 6
MESH_ID = pl.DeviceIdType.MESH
WHOLE = pl.BlockSpec(memory_space=pltpu.VMEM)


def split(x):
    high = x.astype(jnp.bfloat16)
    low = (x - high.astype(jnp.float32)).astype(jnp.bfloat16)
    return high, low


def orb_peer(index):
    return {"xh": index // 4, "y": index % 4}


def site_peer(index):
    return {"xl": index // 8, "z": index % 8}


def my_orb():
    return lax.axis_index("xh") * 4 + lax.axis_index("y")


def my_site():
    return lax.axis_index("xl") * 8 + lax.axis_index("z")


def greet(peers):
    barrier = pltpu.get_barrier_semaphore()
    for peer in peers:
        pl.semaphore_signal(barrier, inc=1, device_id=peer, device_id_type=MESH_ID)
    pl.semaphore_wait(barrier, len(peers))


def remote(src, dst, send, recv, peer):
    return pltpu.make_async_remote_copy(
        src_ref=src, dst_ref=dst, send_sem=send, recv_sem=recv,
        device_id=peer, device_id_type=MESH_ID,
    )


def rows_back_kernel(t_ref, out_ref, full_ref, edge_sem, body_sem, own):
    me = my_orb()
    greet([orb_peer((me + r) % 8) for r in range(1, 8)])
    edge = pl.ds(pl.multiple_of(EDGE_ROWS * me, 8), EDGE_ROWS)
    body = pl.ds(pl.multiple_of(8 * EDGE_ROWS + BODY_ROWS * me, 8), BODY_ROWS)
    copies = []
    for r in (6, 2, 5, 3, 7, 1, 4):
        peer = (me + r) % 8
        for source, target, sems in (
            (pl.ds(EDGE_ROWS, BODY_ROWS), body, body_sem), (pl.ds(0, EDGE_ROWS), edge, edge_sem)
        ):
            copy = remote(
                t_ref.at[peer, source], full_ref.at[target], sems.at[0, r], sems.at[1, r], orb_peer(peer)
            )
            copy.start()
            copies.append(copy)
    locals_ = [
        pltpu.make_async_copy(t_ref.at[me, pl.ds(EDGE_ROWS, BODY_ROWS)], full_ref.at[body], own.at[0]),
        pltpu.make_async_copy(t_ref.at[me, pl.ds(0, EDGE_ROWS)], full_ref.at[edge], own.at[1]),
    ]
    for copy in locals_:
        copy.start()
    for copy in locals_ + copies:
        copy.wait()
    out_ref[...] = full_ref[0:out_ref.shape[0], :]


def rows_back(value, nodes, collective_id):
    return pl.pallas_call(
        rows_back_kernel,
        out_shape=jax.ShapeDtypeStruct((nodes, 128), jnp.float32),
        in_specs=[pl.BlockSpec(memory_space=pltpu.HBM)],
        out_specs=WHOLE,
        scratch_shapes=[
            pltpu.VMEM((8 * ROWS, 128), jnp.float32),
            pltpu.SemaphoreType.DMA((2, 8)), pltpu.SemaphoreType.DMA((2, 8)), pltpu.SemaphoreType.DMA((2,)),
        ],
        compiler_params=pltpu.CompilerParams(
            collective_id=collective_id, has_side_effects=True, vmem_limit_bytes=58 * 1024 * 1024
        ),
    )(value)


def gram(x_ref, out_ref, left_ref, right_ref):
    for j in range(8):
        high, low = split(x_ref[j])
        lanes = pl.ds(128 * j, 128)
        left_ref[0:ROWS, lanes] = high
        left_ref[ROWS:2 * ROWS, lanes] = low
        left_ref[2 * ROWS:3 * ROWS, lanes] = high
        right_ref[0:ROWS, lanes] = high
        right_ref[ROWS:2 * ROWS, lanes] = high
        right_ref[2 * ROWS:3 * ROWS, lanes] = low
    for i in range(8):
        product = lax.dot_general(
            left_ref[:, pl.ds(128 * i, 128)], right_ref[:, pl.ds(0, 128 * (i + 1))],
            (((0,), (0,)), ((), ())), preferred_element_type=jnp.float32,
        )
        for j in range(i + 1):
            block = i * (i + 1) // 2 + j
            out_ref[128 * block:128 * (block + 1), :] = product[:, 128 * j:128 * (j + 1)]


def total_over_all(
    m_ref, out_ref, pair_ref, mine_ref,
    orb_ref, sum_ref, cut_ref, site_ref, done_ref,
    orb2_ref, sum2_ref, cut2_ref, site2_ref, done2_ref,
    pair_sem, orb_sem, site_sem, back_sem, home_sem, last_sem,
    orb2_sem, site2_sem, back2_sem, home2_sem, last2_sem,
):
    core = lax.axis_index("core")
    me = my_orb()
    here = my_site()
    partner = {"core": 1 - core}
    order = (6, 2, 5, 3, 7, 1, 4)
    sites = (4, 12, 5, 3, 13, 11, 6, 2, 14, 10, 7, 1, 15, 9, 8)
    half = m_ref.shape[0] // 2
    every = []

    def rows(start, size, base=0):
        return pl.ds(pl.multiple_of(base + start, 8), size)

    def go(source, target, sems, index, peer):
        copy = remote(source, target, sems.at[0, index], sems.at[1, index], peer)
        copy.start()
        every.append(copy)
        return copy

    mine_base = core * half
    other_base = (1 - core) * half
    first = go(
        m_ref.at[rows(FORTH, half - FORTH, other_base)], pair_ref.at[pl.ds(FORTH, half - FORTH)],
        pair_sem, 8, partner,
    )
    arrivals = {}
    for r in order + (0,):
        start = ORB_PIECE * ((me + r) % 8)
        arrivals[r] = go(
            m_ref.at[rows(start, ORB_PIECE, other_base)], pair_ref.at[rows(start, ORB_PIECE)],
            pair_sem, r, partner,
        )
    first.wait_recv()
    mine_ref[FORTH:half, :] = m_ref[rows(FORTH, half - FORTH, mine_base), :] + pair_ref[FORTH:half, :]
    spread2 = {}
    for r in sites:
        peer = (here + r) % 16
        spread2[r] = go(
            mine_ref.at[rows(SITE_PIECE * peer, SITE_PIECE, FORTH)], site2_ref.at[r], site2_sem, r,
            site_peer(peer),
        )
    spread1 = {}
    for r in order + (0,):
        peer = (me + r) % 8
        start = ORB_PIECE * peer
        arrivals[r].wait_recv()
        mine_ref[rows(start, ORB_PIECE), :] = (
            m_ref[rows(start, ORB_PIECE, mine_base), :] + pair_ref[rows(start, ORB_PIECE), :]
        )
        if r:
            spread1[r] = go(
                mine_ref.at[rows(start, ORB_PIECE)], orb_ref.at[r], orb_sem, r, orb_peer(peer)
            )
    total = mine_ref[rows(SITE_PIECE * here, SITE_PIECE, FORTH), :]
    for r in sites:
        spread2[r].wait_recv()
        total = total + site2_ref[r]
    sum2_ref[...] = total
    for i in range(8):
        cut2_ref[i] = sum2_ref[SITE_SLOT * i:SITE_SLOT * (i + 1), :]
    inner2 = {}
    for r in order:
        peer = (me + r) % 8
        inner2[r] = go(cut2_ref.at[peer], orb2_ref.at[r], orb2_sem, r, orb_peer(peer))
    total = mine_ref[rows(ORB_PIECE * me, ORB_PIECE), :]
    for r in order:
        spread1[r].wait_recv()
        total = total + orb_ref[r]
    sum_ref[...] = total
    for i in range(16):
        cut_ref[i] = sum_ref[ORB_SLOT * i:ORB_SLOT * (i + 1), :]
    inner1 = {}
    for r in sites:
        peer = (here + r) % 16
        inner1[r] = go(cut_ref.at[peer], site_ref.at[r], site_sem, r, site_peer(peer))
    slot = cut2_ref[me]
    for r in order:
        inner2[r].wait_recv()
        slot = slot + orb2_ref[r]
    done2_ref[me] = slot
    outer2 = [
        go(done2_ref.at[me], done2_ref.at[me], back2_sem, r, orb_peer((me + r) % 8)) for r in order
    ]
    slot = cut_ref[here]
    for r in sites:
        inner1[r].wait_recv()
        slot = slot + site_ref[r]
    done_ref[here] = slot
    outer1 = [
        go(done_ref.at[here], done_ref.at[here], back_sem, r, site_peer((here + r) % 16)) for r in sites
    ]
    for copy in outer2:
        copy.wait_recv()
    for i in range(8):
        sum2_ref[SITE_SLOT * i:SITE_SLOT * (i + 1), :] = done2_ref[i]
    place2 = out_ref.at[rows(SITE_PIECE * here, SITE_PIECE, mine_base + FORTH)]
    homes2 = [
        (r, go(sum2_ref, place2, home2_sem, r, site_peer((here + r) % 16))) for r in sites
    ]
    lasts = [go(sum2_ref, place2, last2_sem, 0, partner)]
    out_ref[rows(SITE_PIECE * here, SITE_PIECE, mine_base + FORTH), :] = sum2_ref[...]
    for copy in outer1:
        copy.wait_recv()
    for i in range(16):
        sum_ref[ORB_SLOT * i:ORB_SLOT * (i + 1), :] = done_ref[i]
    place = out_ref.at[rows(ORB_PIECE * me, ORB_PIECE, mine_base)]
    homes1 = [(r, go(sum_ref, place, home_sem, r, orb_peer((me + r) % 8))) for r in order]
    lasts.append(go(sum_ref, place, last_sem, 0, partner))
    out_ref[rows(ORB_PIECE * me, ORB_PIECE, mine_base), :] = sum_ref[...]
    for r, copy in homes1:
        copy.wait_recv()
        place = out_ref.at[rows(ORB_PIECE * ((me + 8 - r) % 8), ORB_PIECE, mine_base)]
        lasts.append(go(place, place, last_sem, r, partner))
    for r, copy in homes2:
        copy.wait_recv()
        place = out_ref.at[rows(SITE_PIECE * ((here + 16 - r) % 16), SITE_PIECE, mine_base + FORTH)]
        lasts.append(go(place, place, last2_sem, r, partner))
    for copy in lasts:
        copy.wait_recv()
    return every


def product(x, y):
    xh, xl = split(x)
    yh, yl = split(y)
    right = jnp.concatenate([yh, yl], axis=1)
    both = jnp.dot(
        jnp.concatenate([xh, xl], axis=1), jnp.concatenate([right, right], axis=0),
        preferred_element_type=jnp.float32,
    )
    return both[:, :128] + both[:, 128:]


def twice(y):
    yh, yl = split(y)
    return jnp.concatenate(
        [jnp.concatenate([yh, yh], axis=1), jnp.concatenate([yl, yl], axis=1)], axis=0
    )


def against(pair, right):
    both = lax.dot_general(pair, right, (((1,), (1,)), ((), ())), preferred_element_type=jnp.float32)
    return both[:, :128] + both[:, 128:]


def pair_of(x):
    return jnp.concatenate(split(x), axis=1)


def place_owned(owner_ref, sums_ref, owned_ref):
    here = lax.axis_index("xl") * 16 + lax.axis_index("z") * 2 + lax.axis_index("core")
    owned_ref[...] = jnp.zeros_like(owned_ref)

    def place(atom, count):
        held = owner_ref[atom] == here

        @pl.when(held)
        def _():
            owned_ref[jnp.minimum(count, OWN_CAP - 1)] = sums_ref[atom // ATOM_DEV, atom % ATOM_DEV]

        return count + jnp.where(held, 1, 0)

    lax.fori_loop(0, owner_ref.shape[0], place, 0)


def solve_kernel(
    scale, owner_ref, m_ref, t_ref, sums_ref, ray_ref, out_ref, owned_ref, rayleigh_ref,
    panel_ref, left_ref, inv_ref, work_ref, unit_ref,
):
    rayleigh_ref[...] = ray_ref[...]
    place_owned(owner_ref, sums_ref, owned_ref)
    row = lax.broadcasted_iota(jnp.int32, (128, 128), 0)
    col = lax.broadcasted_iota(jnp.int32, (128, 128), 1)
    eye = (row == col).astype(jnp.float32)
    half = (row > col).astype(jnp.float32) + 0.5 * eye
    down, across = [], []
    for k in range(8):
        diagonal = m_ref[k * (k + 1) // 2 + k] * eye
        down.append(lax.rsqrt(jnp.sum(diagonal, axis=1, keepdims=True) * scale))
        across.append(lax.rsqrt(jnp.sum(diagonal, axis=0, keepdims=True) * scale))
    for j in range(8):
        for i in range(j, 8):
            block = m_ref[i * (i + 1) // 2 + j] * scale
            panel_ref[j, 128 * i:128 * (i + 1), :] = block * down[i] * across[j]
        panel_ref[j, 1024:1024 + ROWS, :] = t_ref[j] * across[j]
    bottom = 1024 + ROWS
    for k in range(8):
        block = panel_ref[k, 128 * k:128 * (k + 1), :]
        x = eye - half * (block - eye)
        for step in range(2):
            error = against(pair_of(product(x, block)), twice(x)) - eye
            x = x - product(half * error, x)
        inv_ref[...] = x

        def unfinished(state):
            return (state[0] < 12) & jnp.logical_not(state[1] < 3e-5)

        def improve(state):
            x = inv_ref[...]
            block = panel_ref[k, 128 * k:128 * (k + 1), :]
            error = against(pair_of(product(x, block)), twice(x)) - eye
            inv_ref[...] = x - product(half * error, x)
            return state[0] + 1, jnp.sum(error * error)

        left = lax.while_loop(unfinished, improve, (0, jnp.sum(error * error)))[1]

        @pl.when(jnp.logical_not(left < 3e-5))
        def _():
            work_ref[...] = panel_ref[k, 128 * k:128 * (k + 1), :]
            unit_ref[...] = eye

            def eliminate(j, carry):
                lane = (col == j).astype(jnp.float32)
                mine = work_ref[pl.ds(j, 1), :]
                unit = unit_ref[pl.ds(j, 1), :]
                pivot = jnp.sum(jnp.where(col[0:1] == j, mine, 0.0), axis=1, keepdims=True)
                whole = work_ref[...]
                column = jnp.sum(jnp.where(col == j, whole, 0.0), axis=1, keepdims=True)
                factor = jnp.where(row > j, column / pivot, 0.0)
                work_ref[...] = whole - factor * mine
                unit_ref[...] = unit_ref[...] - factor * unit
                inv_ref[pl.ds(j, 1), :] = unit * lax.rsqrt(pivot)
                return carry

            lax.fori_loop(0, 128, eliminate, 0)

        right = twice(inv_ref[...])
        starts = list(range(128 * (k + 1), 1024, 128)) + [1024, 1024 + ROWS // 2]
        for start in starts:
            size = 128 if start < 1024 else ROWS // 2
            value = against(pair_of(panel_ref[k, start:start + size, :]), right)
            if start < 1024:
                left_ref[start:start + size, :] = pair_of(value)
            else:
                out_ref[k, start - 1024:start - 1024 + size, :] = value
                if k < 7:
                    left_ref[start:start + size, :] = pair_of(value)
        for j in range(k + 1, 8):
            pair = left_ref[128 * j:128 * (j + 1), :]
            high, low = pair[:, :128], pair[:, 128:]
            right = jnp.concatenate(
                [jnp.concatenate([high, high], axis=1), jnp.concatenate([low, low], axis=1)], axis=0
            )
            for start in list(range(128 * j, 1024, 128)) + [1024, 1024 + ROWS // 2]:
                size = 128 if start < 1024 else ROWS // 2
                panel_ref[j, start:start + size, :] = panel_ref[j, start:start + size, :] - against(
                    left_ref[start:start + size, :], right
                )


def solve_rows(blocks, rows, scale, atom_owner, sums, rayleigh):
    return pl.pallas_call(
        functools.partial(solve_kernel, scale),
        out_shape=(
            jax.ShapeDtypeStruct((8, ROWS, 128), jnp.float32),
            jax.ShapeDtypeStruct((OWN_CAP, PROJ, 128), jnp.float32),
            jax.ShapeDtypeStruct((1, 128), jnp.float32),
        ),
        in_specs=[pl.BlockSpec(memory_space=pltpu.SMEM)] + [WHOLE] * 4,
        out_specs=(WHOLE,) * 3,
        scratch_shapes=[
            pltpu.VMEM((8, 1024 + ROWS, 128), jnp.float32),
            pltpu.VMEM((1024 + ROWS, 256), jnp.bfloat16),
            pltpu.VMEM((128, 128), jnp.float32),
            pltpu.VMEM((128, 128), jnp.float32),
            pltpu.VMEM((128, 128), jnp.float32),
        ],
        compiler_params=pltpu.CompilerParams(vmem_limit_bytes=62 * 1024 * 1024),
    )(atom_owner, blocks, rows, sums, rayleigh)


WINDOW = 2 * REACH + 1
TILE = 8
LINES = SIDE * DEG + 1
PLANE = LINES * LINES
HALO = 368
PADDED = EDGE * EDGE * TILE


def cell_peer(index):
    return {"xl": index // 16, "z": (index // 2) % 8, "core": index % 2}


def thrice(left, right, dims):
    lh, ll = left
    rh, rl = right
    dot = functools.partial(
        lax.dot_general, dimension_numbers=(dims, ((), ())), preferred_element_type=jnp.float32
    )
    return dot(lh, rh) + dot(ll, rh) + dot(lh, rl)


def cube_root(x):
    root = jnp.exp(jnp.log(x) * (1.0 / 3.0))
    for _ in range(2):
        root = root - (root * root * root - x) / (3.0 * root * root)
    return root


def trial_kernel(
    scale_ref, atom_ref, cell_ref,
    c_in, occ_in, ext_in, core_in, stiff_in, proj_in, coup_in,
    rows_ref, ray_ref, sums_ref, total_ref,
    hot_ref, c_ref, occ_ref, ext_ref, core_ref, stiff_ref, proj_ref, coup_ref, pick_ref, load_sem,
    halo_ref, tile_ref, value_ref, image_ref, top_ref, under_ref, proj24_ref,
    give_ref, take_ref, used_ref, window_ref, dens_ref, ray_all_ref, pot_ref,
    halo_sem, dens_send, dens_recv, give_send, give_recv, used_send, used_recv,
    top_sem, ray_send, ray_recv, sums_send, sums_recv,
    pad_ref, now_ref, move_ref, rays_ref, early_sem, body_sem, edge_sem, share_sem,
    gram_ref, left_ref, right_ref, *total_scratch,
):
    nodes = c_ref.shape[0]
    here = lax.axis_index("xl") * 16 + lax.axis_index("z") * 2 + lax.axis_index("core")
    me = my_orb()
    barrier = pltpu.get_barrier_semaphore()
    peers = [cell_peer((here + r) % 32) for r in range(1, 32)]
    peers += [orb_peer((me + r) % 8) for r in range(1, 8)]
    for peer in peers:
        pl.semaphore_signal(barrier, inc=1, device_id=peer, device_id_type=MESH_ID)
    loads = [
        pltpu.make_async_copy(source, target, load_sem.at[i])
        for i, (source, target) in enumerate(
            (
                (stiff_in, stiff_ref), (proj_in, proj_ref), (coup_in, coup_ref), (c_in, c_ref),
                (occ_in, occ_ref), (ext_in, ext_ref), (core_in, core_ref),
            )
        )
    ]
    for load in loads:
        load.start()
    for load in loads[3:]:
        load.wait()
    current = c_ref[...]
    pad_ref[0:nodes, :] = current
    pad_ref[nodes:8 * ROWS, :] = jnp.zeros((8 * ROWS - nodes, 128), jnp.float32)
    pl.semaphore_wait(barrier, len(peers))
    halo = remote(
        c_ref.at[pl.ds(0, HALO)], halo_ref, halo_sem.at[0], halo_sem.at[1], cell_peer((here + 31) % 32)
    )
    halo.start()
    square = current * current
    density = thrice(split(jnp.broadcast_to(occ_ref[...].reshape(1, 128), (TILE, 128))), split(square), ((1,), (1,)))
    dens_ref[0] = density[0:1, :]
    dens_copies = []
    for r in range(1, 8):
        peer = (me + r) % 8
        copy = remote(dens_ref.at[0], dens_ref.at[r], dens_send.at[r], dens_recv.at[r], orb_peer(peer))
        copy.start()
        dens_copies.append(copy)

    order = (6, 2, 5, 3, 7, 1, 4)

    def edge(index):
        return pl.ds(pl.multiple_of(EDGE_ROWS * index, 8), EDGE_ROWS)

    def body(index):
        return pl.ds(pl.multiple_of(8 * EDGE_ROWS + BODY_ROWS * index, 8), BODY_ROWS)

    early = []
    for r in order:
        peer = (me + r) % 8
        for source, target, i in (
            (body(peer), pl.ds(EDGE_ROWS, BODY_ROWS), 0), (edge(peer), pl.ds(0, EDGE_ROWS), 2)
        ):
            copy = remote(
                pad_ref.at[source], now_ref.at[me, target], early_sem.at[i, r], early_sem.at[i + 1, r],
                orb_peer(peer),
            )
            copy.start()
            early.append(copy)
    now_ref[me, 0:EDGE_ROWS, :] = pad_ref[edge(me), :]
    now_ref[me, EDGE_ROWS:ROWS, :] = pad_ref[body(me), :]

    node = lax.broadcasted_iota(jnp.int32, (CELL_NODES, PADDED), 0)
    place = lax.broadcasted_iota(jnp.int32, (CELL_NODES, PADDED), 1)
    inside = (place & 7) < EDGE
    match = node == EDGE * (place >> 3) + (place & 7)
    spot = jnp.where(inside & match, 1.0, 0.0).astype(jnp.bfloat16)
    dot = functools.partial(lax.dot_general, preferred_element_type=jnp.float32)

    def both_sides(part):
        wide = dot(part, spot, (((1,), (0,)), ((), ()))).astype(jnp.bfloat16)
        return dot(spot, wide, (((0,), (0,)), ((), ()))).astype(jnp.bfloat16)

    loads[0].wait()
    stiff = tuple(both_sides(part) for part in split(stiff_ref[...]))
    loads[1].wait()
    proj24_ref[...] = jnp.zeros_like(proj24_ref)
    for t in range(TOUCH_DEV):
        proj24_ref[24 * t:24 * t + PROJ, :] = proj_ref[t, :, 0, :]
    parts = split(proj24_ref[...])
    proj_rows = tuple(dot(p, spot, (((1,), (0,)), ((), ()))).astype(jnp.bfloat16) for p in parts)
    proj_cols = tuple(dot(spot, p, (((0,), (1,)), ((), ()))).astype(jnp.bfloat16) for p in parts)

    loads[2].wait()
    lane = lax.broadcasted_iota(jnp.int32, (PROJ, 64), 1)
    for m in range(ATOM_DEV):
        for p in range(PROJ):
            column = jnp.sum(jnp.where(lane == 2 * here + m, coup_ref[p], 0.0), axis=1, keepdims=True)
            pick_ref[m, p] = jnp.broadcast_to(column, (PROJ, 128))
    for t in range(TOUCH_DEV):
        for w in range(WINDOW * ATOM_DEV):
            atom = (2 * (here + w // ATOM_DEV + 32 - REACH) + w % ATOM_DEV) % 64
            gap = atom_ref[here * TOUCH_DEV + t] - atom
            hot_ref[w, t] = (1 - jnp.minimum(gap * gap, 1)).astype(jnp.float32)
        for c in range(SIDE * SIDE):
            gap = cell_ref[t] - c
            hot_ref[10 + c, t] = (1 - jnp.minimum(gap * gap, 1)).astype(jnp.float32)

    for a in range(DEG):
        for y in range(LINES):
            for s in range(SIDE):
                start = PLANE * a + LINES * y + DEG * s
                if start + TILE > nodes:
                    piece = jnp.concatenate(
                        [c_ref[start:nodes, :], jnp.zeros((start + TILE - nodes, 128), jnp.float32)], axis=0
                    )
                else:
                    piece = c_ref[start:start + TILE, :]
                tile_ref[s, a, TILE * y:TILE * (y + 1), :] = piece
    halo.wait_recv()
    for y in range(LINES):
        for s in range(SIDE):
            start = LINES * y + DEG * s
            tile_ref[s, DEG, TILE * y:TILE * (y + 1), :] = halo_ref[start:start + TILE, :]

    def cell_values(r):
        span = slice(DEG * TILE * r, DEG * TILE * r + EDGE * TILE)
        return [
            jnp.concatenate([tile_ref[s, a, span, :] for a in range(EDGE)], axis=0)
            for s in range(SIDE)
        ]

    contrib = [jnp.zeros((24, 128), jnp.float32) for _ in range(TOUCH_DEV)]
    for r in range(SIDE):
        wide = thrice(proj_rows, split(jnp.concatenate(cell_values(r), axis=1)), ((1,), (0,)))
        for t in range(TOUCH_DEV):
            for s in range(SIDE):
                part = wide[24 * t:24 * t + 24, 128 * s:128 * (s + 1)]
                contrib[t] = contrib[t] + hot_ref[10 + SIDE * r + s, t] * part
    for k in range(WINDOW):
        for m in range(ATOM_DEV):
            total = hot_ref[ATOM_DEV * k + m, 0] * contrib[0]
            for t in range(1, TOUCH_DEV):
                total = total + hot_ref[ATOM_DEV * k + m, t] * contrib[t]
            give_ref[k, m] = total[:PROJ]
    gives = {}
    for k in (0, 4, 1, 3):
        copy = remote(
            give_ref.at[k], take_ref.at[k], give_send.at[k], give_recv.at[k],
            cell_peer((here + k + 32 - REACH) % 32),
        )
        copy.start()
        gives[k] = copy

    value_ref[...] = jnp.zeros_like(value_ref)

    def add_value(r, wide):
        for s in range(SIDE):
            for a in range(EDGE):
                span = slice(DEG * TILE * r, DEG * TILE * r + EDGE * TILE)
                value_ref[s, a, span, :] = (
                    value_ref[s, a, span, :]
                    + wide[EDGE * TILE * a:EDGE * TILE * (a + 1), 128 * s:128 * (s + 1)]
                )

    for r in range(SIDE):
        wide = jnp.concatenate(
            [value * scale_ref[SIDE * r + s] for s, value in enumerate(cell_values(r))], axis=1
        )
        add_value(r, thrice(stiff, split(wide), ((1,), (0,))))

    for k in (0, 4, 1, 3):
        gives[k].wait_recv()
    useds = {}
    for m in range(ATOM_DEV):
        total = give_ref[REACH, m]
        for k in (0, 1, 3, 4):
            total = total + take_ref[k, m]
        sums_ref[here, m] = total
        for p in range(PROJ):
            used_ref[m, p:p + 1, :] = jnp.sum(pick_ref[m, p] * total, axis=0, keepdims=True)
        window_ref[REACH, m] = used_ref[m]
    for q in (0, 4, 1, 3):
        copy = remote(
            used_ref, window_ref.at[4 - q], used_send.at[4 - q], used_recv.at[4 - q],
            cell_peer((here + q + 32 - REACH) % 32),
        )
        copy.start()
        useds[4 - q] = copy

    for copy in dens_copies:
        copy.wait_recv()
    density = dens_ref[0]
    for r in range(1, 8):
        density = density + dens_ref[r]
    potential = ext_ref[...].reshape(1, nodes) - exchange_coef * cube_root(
        density + core_ref[...].reshape(1, nodes)
    )
    pot_ref[...] = dot(
        jnp.broadcast_to(potential, (TILE, nodes)),
        (lax.broadcasted_iota(jnp.int32, (TILE, 128), 0) == 0).astype(jnp.float32),
        (((0,), (0,)), ((), ())), precision=highest,
    )

    for k in (0, 4, 1, 3):
        useds[k].wait_recv()
    back = []
    for t in range(TOUCH_DEV):
        total = jnp.zeros((PROJ, 128), jnp.float32)
        for k in range(WINDOW):
            for m in range(ATOM_DEV):
                total = total + hot_ref[ATOM_DEV * k + m, t] * window_ref[k, m]
        back.append(jnp.concatenate([total, jnp.zeros((24 - PROJ, 128), jnp.float32)], axis=0))
    for r in range(SIDE):
        wide = jnp.concatenate(
            [
                jnp.concatenate(
                    [
                        hot_ref[10 + SIDE * r + s, t] * back[t]
                        for t in range(TOUCH_DEV)
                    ],
                    axis=0,
                )
                for s in range(SIDE)
            ],
            axis=1,
        )
        add_value(r, thrice(proj_cols, split(wide), ((1,), (0,))))

    top_ref[...] = jnp.zeros_like(top_ref)
    for y in range(LINES):
        for s in range(SIDE):
            start = LINES * y + DEG * s
            top_ref[start:start + TILE, :] = (
                top_ref[start:start + TILE, :] + value_ref[s, DEG, TILE * y:TILE * (y + 1), :]
            )
    top = remote(top_ref, under_ref, top_sem.at[0], top_sem.at[1], cell_peer((here + 1) % 32))
    top.start()

    current = c_ref[...]
    square = current * current
    numerator = jnp.sum(pot_ref[...] * square, axis=0, keepdims=True)
    for s in range(SIDE):
        for a in range(EDGE):
            numerator = numerator + jnp.sum(tile_ref[s, a] * value_ref[s, a], axis=0, keepdims=True)
    ray_all_ref[here, 0:1, :] = numerator
    ray_all_ref[here, 1:2, :] = jnp.sum(square, axis=0, keepdims=True)
    rays = []
    for r in range(1, 32):
        copy = remote(
            ray_all_ref.at[here], ray_all_ref.at[here], ray_send.at[r], ray_recv.at[r],
            cell_peer((here + r) % 32),
        )
        copy.start()
        rays.append(copy)

    image_ref[...] = jnp.zeros_like(image_ref)
    image_ref[0:nodes, :] = pot_ref[...] * current
    for a in range(DEG):
        for y in range(LINES):
            for s in range(SIDE):
                start = PLANE * a + LINES * y + DEG * s
                image_ref[start:start + TILE, :] = (
                    image_ref[start:start + TILE, :] + value_ref[s, a, TILE * y:TILE * (y + 1), :]
                )
    bodies = []
    for r in order:
        peer = (me + r) % 8
        copy = remote(
            image_ref.at[body(peer)], move_ref.at[me, pl.ds(EDGE_ROWS, BODY_ROWS)],
            body_sem.at[0, r], body_sem.at[1, r], orb_peer(peer),
        )
        copy.start()
        bodies.append(copy)
    move_ref[me, EDGE_ROWS:ROWS, :] = image_ref[body(me), :]
    top.wait_recv()
    image_ref[0:PLANE, :] = image_ref[0:PLANE, :] + under_ref[0:PLANE, :]
    edges = []
    for r in order:
        peer = (me + r) % 8
        copy = remote(
            image_ref.at[edge(peer)], move_ref.at[me, pl.ds(0, EDGE_ROWS)],
            edge_sem.at[0, r], edge_sem.at[1, r], orb_peer(peer),
        )
        copy.start()
        edges.append(copy)
    move_ref[me, 0:EDGE_ROWS, :] = image_ref[edge(me), :]
    for copy in rays:
        copy.wait_recv()
    total = jnp.sum(ray_all_ref[...], axis=0)
    rayleigh = total[0:1, :] / (total[1:2, :] + tiny)
    ray_ref[...] = rayleigh
    rays_ref[me] = rayleigh
    shares = []
    for r in order:
        copy = remote(
            rays_ref.at[me], rays_ref.at[me], share_sem.at[0, r], share_sem.at[1, r],
            orb_peer((me + r) % 8),
        )
        copy.start()
        shares.append(copy)
    sums = []
    for r in range(1, 16):
        copy = remote(
            sums_ref.at[here], sums_ref.at[here], sums_send.at[r], sums_recv.at[r],
            site_peer((my_site() + r) % 16),
        )
        copy.start()
        sums.append(copy)
    for copy in early + shares + bodies + edges:
        copy.wait_recv()
    for j in range(8):
        now = now_ref[j]
        rows_ref[j] = now - step_size * (move_ref[j] - rays_ref[j] * now)
    gram(rows_ref, gram_ref, left_ref, right_ref)
    core = lax.axis_index("core")
    passed = []
    for r in range(16):
        if r:
            sums[r - 1].wait_recv()
        held = sums_ref.at[2 * ((my_site() + 16 - r) % 16) + core]
        copy = remote(held, held, sums_send.at[16 + r], sums_recv.at[16 + r], {"core": 1 - core})
        copy.start()
        passed.append(copy)
    everything = total_over_all(gram_ref, total_ref, *total_scratch)
    for copy in passed:
        copy.wait_recv()
    everything += passed
    everything += [halo, top] + dens_copies + list(gives.values()) + list(useds.values()) + rays
    for copy in everything + early + shares + bodies + edges + sums:
        copy.wait_send()


def trial_rows(
    orbitals, occupations, external, core_density, cell_scale, stiffness,
    touched_atom, touched_cells, projectors, coupling, collective_id,
):
    nodes = orbitals.shape[0]
    scalars = pl.BlockSpec(memory_space=pltpu.SMEM)
    dma = lambda *n: pltpu.SemaphoreType.DMA(n)
    vmem = lambda *shape: pltpu.VMEM(shape, jnp.float32)
    return pl.pallas_call(
        trial_kernel,
        out_shape=(
            jax.ShapeDtypeStruct((8, ROWS, 128), jnp.float32),
            jax.ShapeDtypeStruct((1, 128), jnp.float32),
            jax.ShapeDtypeStruct((32, ATOM_DEV, PROJ, 128), jnp.float32),
            jax.ShapeDtypeStruct((36 * 128, 128), jnp.float32),
        ),
        in_specs=[scalars] * 3 + [pl.BlockSpec(memory_space=pltpu.HBM)] * 7,
        out_specs=(WHOLE,) * 4,
        scratch_shapes=[
            pltpu.SMEM((19, TOUCH_DEV), jnp.float32),
            vmem(nodes, 128), vmem(128), vmem(nodes), vmem(nodes), vmem(CELL_NODES, CELL_NODES),
            vmem(TOUCH_DEV, PROJ, 1, CELL_NODES), vmem(PROJ, PROJ, 64), vmem(ATOM_DEV, PROJ, PROJ, 128),
            dma(7),
            vmem(HALO, 128),
            vmem(SIDE, EDGE, LINES * TILE, 128),
            vmem(SIDE, EDGE, LINES * TILE, 128),
            vmem(8 * ROWS, 128),
            vmem(HALO, 128),
            vmem(HALO, 128),
            vmem(24 * TOUCH_DEV, CELL_NODES),
            vmem(WINDOW, ATOM_DEV, PROJ, 128),
            vmem(WINDOW, ATOM_DEV, PROJ, 128),
            vmem(ATOM_DEV, PROJ, 128),
            vmem(WINDOW, ATOM_DEV, PROJ, 128),
            vmem(8, 1, nodes),
            vmem(32, 2, 128),
            vmem(nodes, 128),
            dma(2), dma(8), dma(8), dma(5), dma(5), dma(5), dma(5),
            dma(2), dma(32), dma(32), dma(32), dma(32),
            vmem(8 * ROWS, 128), vmem(8, ROWS, 128), vmem(8, ROWS, 128), vmem(8, 1, 128),
            dma(4, 8), dma(2, 8), dma(2, 8), dma(2, 8),
            vmem(36 * 128, 128),
            pltpu.VMEM((3 * ROWS, 1024), jnp.bfloat16),
            pltpu.VMEM((3 * ROWS, 1024), jnp.bfloat16),
            vmem(18 * 128, 128), vmem(18 * 128, 128),
            vmem(8, ORB_PIECE, 128), vmem(ORB_PIECE, 128), vmem(16, ORB_SLOT, 128),
            vmem(16, ORB_SLOT, 128), vmem(16, ORB_SLOT, 128),
            vmem(8, SITE_SLOT, 128), vmem(SITE_PIECE, 128), vmem(8, SITE_SLOT, 128),
            vmem(16, SITE_PIECE, 128), vmem(8, SITE_SLOT, 128),
            dma(2, 9), dma(2, 8), dma(2, 16), dma(2, 16), dma(2, 8), dma(2, 8),
            dma(2, 8), dma(2, 16), dma(2, 8), dma(2, 16), dma(2, 16),
        ],
        compiler_params=pltpu.CompilerParams(
            collective_id=collective_id, has_side_effects=True, vmem_limit_bytes=62 * 1024 * 1024
        ),
    )(
        cell_scale, touched_atom, touched_cells.reshape(-1), orbitals, occupations,
        external, core_density, stiffness, projectors.transpose(0, 2, 1, 3), coupling.transpose(1, 2, 0),
    )


def per_device(
    orbitals,
    occupations,
    external,
    core_density,
    cell_scale,
    stiffness,
    touched_atom,
    touched_cells,
    projectors,
    coupling,
    atom_owner,
):
    nodes = orbitals.shape[0]
    rows, rayleigh, sums, blocks = trial_rows(
        orbitals, occupations, external, core_density, cell_scale, stiffness,
        touched_atom, touched_cells, projectors, coupling, 1,
    )
    solved, owned, rayleigh = solve_rows(
        blocks.reshape(36, 128, 128), rows, 1.0 / (nodes * 32), atom_owner.reshape(-1), sums, rayleigh
    )
    return (rows_back(solved, nodes, 2), rayleigh.reshape(-1), owned)


def solution(mesh):
    finer = Mesh(mesh.devices.reshape(2, 8, 2, 2, 4), ("xl", "z", "core", "xh", "y"))
    return jax.shard_map(
        per_device,
        mesh=finer,
        in_specs=(
            P(CELLS, ORBS),
            P(ORBS),
            P(CELLS),
            P(CELLS),
            P(CELLS),
            P(),
            P(),
            P(CELLS, None),
            P(CELLS, None, None, None),
            P(),
            P(),
        ),
        out_specs=(P(CELLS, ORBS), P(ORBS), P(CELLS, None, ORBS)),
        check_vma=False,
    )
```

```python
import functools
import math

import jax
import jax.numpy as jnp
from jax import lax
from jax.experimental import pallas as pl
from jax.experimental.pallas import tpu as pltpu
from jax.sharding import Mesh
from jax.sharding import PartitionSpec as P

DEG = 6
EDGE = 7
CELL_NODES = 343
SIDE = 3
PROJ = 18
ATOM_DEV = 2
REACH = 2
TOUCH_DEV = 6
OWN_CAP = 5
CELLS = ("xl", "z", "core")
ORBS = ("xh", "y")

highest = lax.Precision.HIGHEST
step_size = 0.1
exchange_coef = (3.0 / math.pi) ** (1.0 / 3.0)
tiny = 1e-06


ROWS = 272
EDGE_ROWS = 48
BODY_ROWS = 224
FORTH = 1536
ORB_PIECE, ORB_SLOT = 192, 12
SITE_PIECE, SITE_SLOT = 48, 6
MESH_ID = pl.DeviceIdType.MESH
WHOLE = pl.BlockSpec(memory_space=pltpu.VMEM)


def split(x):
    high = x.astype(jnp.bfloat16)
    low = (x - high.astype(jnp.float32)).astype(jnp.bfloat16)
    return high, low


def orb_peer(index):
    return {"xh": index // 4, "y": index % 4}


def site_peer(index):
    return {"xl": index // 8, "z": index % 8}


def my_orb():
    return lax.axis_index("xh") * 4 + lax.axis_index("y")


def my_site():
    return lax.axis_index("xl") * 8 + lax.axis_index("z")


def greet(peers):
    barrier = pltpu.get_barrier_semaphore()
    for peer in peers:
        pl.semaphore_signal(barrier, inc=1, device_id=peer, device_id_type=MESH_ID)
    pl.semaphore_wait(barrier, len(peers))


def remote(src, dst, send, recv, peer):
    return pltpu.make_async_remote_copy(
        src_ref=src, dst_ref=dst, send_sem=send, recv_sem=recv,
        device_id=peer, device_id_type=MESH_ID,
    )


def rows_back_kernel(t_ref, out_ref, full_ref, edge_sem, body_sem, own):
    me = my_orb()
    greet([orb_peer((me + r) % 8) for r in range(1, 8)])
    edge = pl.ds(pl.multiple_of(EDGE_ROWS * me, 8), EDGE_ROWS)
    body = pl.ds(pl.multiple_of(8 * EDGE_ROWS + BODY_ROWS * me, 8), BODY_ROWS)
    copies = []
    for r in (6, 2, 5, 3, 7, 1, 4):
        peer = (me + r) % 8
        for source, target, sems in (
            (pl.ds(EDGE_ROWS, BODY_ROWS), body, body_sem), (pl.ds(0, EDGE_ROWS), edge, edge_sem)
        ):
            copy = remote(
                t_ref.at[peer, source], full_ref.at[target], sems.at[0, r], sems.at[1, r], orb_peer(peer)
            )
            copy.start()
            copies.append(copy)
    locals_ = [
        pltpu.make_async_copy(t_ref.at[me, pl.ds(EDGE_ROWS, BODY_ROWS)], full_ref.at[body], own.at[0]),
        pltpu.make_async_copy(t_ref.at[me, pl.ds(0, EDGE_ROWS)], full_ref.at[edge], own.at[1]),
    ]
    for copy in locals_:
        copy.start()
    for copy in locals_ + copies:
        copy.wait()
    out_ref[...] = full_ref[0:out_ref.shape[0], :]


def rows_back(value, nodes, collective_id):
    return pl.pallas_call(
        rows_back_kernel,
        out_shape=jax.ShapeDtypeStruct((nodes, 128), jnp.float32),
        in_specs=[pl.BlockSpec(memory_space=pltpu.HBM)],
        out_specs=WHOLE,
        scratch_shapes=[
            pltpu.VMEM((8 * ROWS, 128), jnp.float32),
            pltpu.SemaphoreType.DMA((2, 8)), pltpu.SemaphoreType.DMA((2, 8)), pltpu.SemaphoreType.DMA((2,)),
        ],
        compiler_params=pltpu.CompilerParams(
            collective_id=collective_id, has_side_effects=True, vmem_limit_bytes=36 * 1024 * 1024
        ),
    )(value)


def gram(x_ref, out_ref, left_ref, right_ref):
    for j in range(8):
        high, low = split(x_ref[j])
        lanes = pl.ds(128 * j, 128)
        left_ref[0:ROWS, lanes] = high
        left_ref[ROWS:2 * ROWS, lanes] = low
        left_ref[2 * ROWS:3 * ROWS, lanes] = high
        right_ref[0:ROWS, lanes] = high
        right_ref[ROWS:2 * ROWS, lanes] = high
        right_ref[2 * ROWS:3 * ROWS, lanes] = low
    for i in range(8):
        product = lax.dot_general(
            left_ref[:, pl.ds(128 * i, 128)], right_ref[:, pl.ds(0, 128 * (i + 1))],
            (((0,), (0,)), ((), ())), preferred_element_type=jnp.float32,
        )
        for j in range(i + 1):
            block = i * (i + 1) // 2 + j
            out_ref[128 * block:128 * (block + 1), :] = product[:, 128 * j:128 * (j + 1)]


def total_over_all(
    m_ref, out_ref, pair_ref, mine_ref,
    orb_ref, sum_ref, cut_ref, site_ref, done_ref,
    orb2_ref, sum2_ref, cut2_ref, site2_ref, done2_ref,
    pair_sem, orb_sem, site_sem, back_sem, home_sem, last_sem,
    orb2_sem, site2_sem, back2_sem, home2_sem, last2_sem,
):
    core = lax.axis_index("core")
    me = my_orb()
    here = my_site()
    partner = {"core": 1 - core}
    order = (6, 2, 5, 3, 7, 1, 4)
    sites = (4, 12, 5, 3, 13, 11, 6, 2, 14, 10, 7, 1, 15, 9, 8)
    half = m_ref.shape[0] // 2
    every = []

    def rows(start, size, base=0):
        return pl.ds(pl.multiple_of(base + start, 8), size)

    def go(source, target, sems, index, peer):
        copy = remote(source, target, sems.at[0, index], sems.at[1, index], peer)
        copy.start()
        every.append(copy)
        return copy

    mine_base = core * half
    other_base = (1 - core) * half
    first = go(
        m_ref.at[rows(FORTH, half - FORTH, other_base)], pair_ref.at[pl.ds(FORTH, half - FORTH)],
        pair_sem, 8, partner,
    )
    arrivals = {}
    for r in order + (0,):
        start = ORB_PIECE * ((me + r) % 8)
        arrivals[r] = go(
            m_ref.at[rows(start, ORB_PIECE, other_base)], pair_ref.at[rows(start, ORB_PIECE)],
            pair_sem, r, partner,
        )
    first.wait_recv()
    mine_ref[FORTH:half, :] = m_ref[rows(FORTH, half - FORTH, mine_base), :] + pair_ref[FORTH:half, :]
    spread2 = {}
    for r in sites:
        peer = (here + r) % 16
        spread2[r] = go(
            mine_ref.at[rows(SITE_PIECE * peer, SITE_PIECE, FORTH)], site2_ref.at[r], site2_sem, r,
            site_peer(peer),
        )
    spread1 = {}
    for r in order + (0,):
        peer = (me + r) % 8
        start = ORB_PIECE * peer
        arrivals[r].wait_recv()
        mine_ref[rows(start, ORB_PIECE), :] = (
            m_ref[rows(start, ORB_PIECE, mine_base), :] + pair_ref[rows(start, ORB_PIECE), :]
        )
        if r:
            spread1[r] = go(
                mine_ref.at[rows(start, ORB_PIECE)], orb_ref.at[r], orb_sem, r, orb_peer(peer)
            )
    total = mine_ref[rows(SITE_PIECE * here, SITE_PIECE, FORTH), :]
    for r in sites:
        spread2[r].wait_recv()
        total = total + site2_ref[r]
    sum2_ref[...] = total
    for i in range(8):
        cut2_ref[i] = sum2_ref[SITE_SLOT * i:SITE_SLOT * (i + 1), :]
    inner2 = {}
    for r in order:
        peer = (me + r) % 8
        inner2[r] = go(cut2_ref.at[peer], orb2_ref.at[r], orb2_sem, r, orb_peer(peer))
    total = mine_ref[rows(ORB_PIECE * me, ORB_PIECE), :]
    for r in order:
        spread1[r].wait_recv()
        total = total + orb_ref[r]
    sum_ref[...] = total
    for i in range(16):
        cut_ref[i] = sum_ref[ORB_SLOT * i:ORB_SLOT * (i + 1), :]
    inner1 = {}
    for r in sites:
        peer = (here + r) % 16
        inner1[r] = go(cut_ref.at[peer], site_ref.at[r], site_sem, r, site_peer(peer))
    slot = cut2_ref[me]
    for r in order:
        inner2[r].wait_recv()
        slot = slot + orb2_ref[r]
    done2_ref[me] = slot
    outer2 = [
        go(done2_ref.at[me], done2_ref.at[me], back2_sem, r, orb_peer((me + r) % 8)) for r in order
    ]
    slot = cut_ref[here]
    for r in sites:
        inner1[r].wait_recv()
        slot = slot + site_ref[r]
    done_ref[here] = slot
    outer1 = [
        go(done_ref.at[here], done_ref.at[here], back_sem, r, site_peer((here + r) % 16)) for r in sites
    ]
    for copy in outer2:
        copy.wait_recv()
    for i in range(8):
        sum2_ref[SITE_SLOT * i:SITE_SLOT * (i + 1), :] = done2_ref[i]
    place2 = out_ref.at[rows(SITE_PIECE * here, SITE_PIECE, mine_base + FORTH)]
    homes2 = [
        (r, go(sum2_ref, place2, home2_sem, r, site_peer((here + r) % 16))) for r in sites
    ]
    lasts = [go(sum2_ref, place2, last2_sem, 0, partner)]
    out_ref[rows(SITE_PIECE * here, SITE_PIECE, mine_base + FORTH), :] = sum2_ref[...]
    for copy in outer1:
        copy.wait_recv()
    for i in range(16):
        sum_ref[ORB_SLOT * i:ORB_SLOT * (i + 1), :] = done_ref[i]
    place = out_ref.at[rows(ORB_PIECE * me, ORB_PIECE, mine_base)]
    homes1 = [(r, go(sum_ref, place, home_sem, r, orb_peer((me + r) % 8))) for r in order]
    lasts.append(go(sum_ref, place, last_sem, 0, partner))
    out_ref[rows(ORB_PIECE * me, ORB_PIECE, mine_base), :] = sum_ref[...]
    for r, copy in homes1:
        copy.wait_recv()
        place = out_ref.at[rows(ORB_PIECE * ((me + 8 - r) % 8), ORB_PIECE, mine_base)]
        lasts.append(go(place, place, last_sem, r, partner))
    for r, copy in homes2:
        copy.wait_recv()
        place = out_ref.at[rows(SITE_PIECE * ((here + 16 - r) % 16), SITE_PIECE, mine_base + FORTH)]
        lasts.append(go(place, place, last2_sem, r, partner))
    for copy in lasts:
        copy.wait_recv()
    return every


def product(x, y):
    xh, xl = split(x)
    yh, yl = split(y)
    right = jnp.concatenate([yh, yl], axis=1)
    both = jnp.dot(
        jnp.concatenate([xh, xl], axis=1), jnp.concatenate([right, right], axis=0),
        preferred_element_type=jnp.float32,
    )
    return both[:, :128] + both[:, 128:]


def twice(y):
    yh, yl = split(y)
    return jnp.concatenate(
        [jnp.concatenate([yh, yh], axis=1), jnp.concatenate([yl, yl], axis=1)], axis=0
    )


def against(pair, right):
    both = lax.dot_general(pair, right, (((1,), (1,)), ((), ())), preferred_element_type=jnp.float32)
    return both[:, :128] + both[:, 128:]


def pair_of(x):
    return jnp.concatenate(split(x), axis=1)


def place_owned(owner_ref, sums_ref, owned_ref):
    here = lax.axis_index("xl") * 16 + lax.axis_index("z") * 2 + lax.axis_index("core")
    owned_ref[...] = jnp.zeros_like(owned_ref)

    def place(atom, count):
        held = owner_ref[atom] == here

        @pl.when(held)
        def _():
            owned_ref[jnp.minimum(count, OWN_CAP - 1)] = sums_ref[atom // ATOM_DEV, atom % ATOM_DEV]

        return count + jnp.where(held, 1, 0)

    lax.fori_loop(0, owner_ref.shape[0], place, 0)


def solve_kernel(
    scale, owner_ref, m_ref, t_ref, sums_ref, ray_ref, out_ref, owned_ref, rayleigh_ref,
    panel_ref, left_ref, inv_ref, work_ref, unit_ref,
):
    rayleigh_ref[...] = ray_ref[...]
    place_owned(owner_ref, sums_ref, owned_ref)
    row = lax.broadcasted_iota(jnp.int32, (128, 128), 0)
    col = lax.broadcasted_iota(jnp.int32, (128, 128), 1)
    eye = (row == col).astype(jnp.float32)
    half = (row > col).astype(jnp.float32) + 0.5 * eye
    down, across = [], []
    for k in range(8):
        diagonal = m_ref[k * (k + 1) // 2 + k] * eye
        down.append(lax.rsqrt(jnp.sum(diagonal, axis=1, keepdims=True) * scale))
        across.append(lax.rsqrt(jnp.sum(diagonal, axis=0, keepdims=True) * scale))
    for j in range(8):
        for i in range(j, 8):
            block = m_ref[i * (i + 1) // 2 + j] * scale
            panel_ref[j, 128 * i:128 * (i + 1), :] = block * down[i] * across[j]
        panel_ref[j, 1024:1024 + ROWS, :] = t_ref[j] * across[j]
    bottom = 1024 + ROWS
    for k in range(8):
        block = panel_ref[k, 128 * k:128 * (k + 1), :]
        x = eye - half * (block - eye)
        for step in range(2):
            error = against(pair_of(product(x, block)), twice(x)) - eye
            x = x - product(half * error, x)
        inv_ref[...] = x

        def unfinished(state):
            return (state[0] < 12) & jnp.logical_not(state[1] < 3e-5)

        def improve(state):
            x = inv_ref[...]
            block = panel_ref[k, 128 * k:128 * (k + 1), :]
            error = against(pair_of(product(x, block)), twice(x)) - eye
            inv_ref[...] = x - product(half * error, x)
            return state[0] + 1, jnp.sum(error * error)

        left = lax.while_loop(unfinished, improve, (0, jnp.sum(error * error)))[1]

        @pl.when(jnp.logical_not(left < 3e-5))
        def _():
            work_ref[...] = panel_ref[k, 128 * k:128 * (k + 1), :]
            unit_ref[...] = eye

            def eliminate(j, carry):
                lane = (col == j).astype(jnp.float32)
                mine = work_ref[pl.ds(j, 1), :]
                unit = unit_ref[pl.ds(j, 1), :]
                pivot = jnp.sum(jnp.where(col[0:1] == j, mine, 0.0), axis=1, keepdims=True)
                whole = work_ref[...]
                column = jnp.sum(jnp.where(col == j, whole, 0.0), axis=1, keepdims=True)
                factor = jnp.where(row > j, column / pivot, 0.0)
                work_ref[...] = whole - factor * mine
                unit_ref[...] = unit_ref[...] - factor * unit
                inv_ref[pl.ds(j, 1), :] = unit * lax.rsqrt(pivot)
                return carry

            lax.fori_loop(0, 128, eliminate, 0)

        right = twice(inv_ref[...])
        starts = list(range(128 * (k + 1), 1024, 128)) + [1024, 1024 + ROWS // 2]
        for start in starts:
            size = 128 if start < 1024 else ROWS // 2
            value = against(pair_of(panel_ref[k, start:start + size, :]), right)
            if start < 1024:
                left_ref[start:start + size, :] = pair_of(value)
            else:
                out_ref[k, start - 1024:start - 1024 + size, :] = value
                if k < 7:
                    left_ref[start:start + size, :] = pair_of(value)
        for j in range(k + 1, 8):
            pair = left_ref[128 * j:128 * (j + 1), :]
            high, low = pair[:, :128], pair[:, 128:]
            right = jnp.concatenate(
                [jnp.concatenate([high, high], axis=1), jnp.concatenate([low, low], axis=1)], axis=0
            )
            for start in list(range(128 * j, 1024, 128)) + [1024, 1024 + ROWS // 2]:
                size = 128 if start < 1024 else ROWS // 2
                panel_ref[j, start:start + size, :] = panel_ref[j, start:start + size, :] - against(
                    left_ref[start:start + size, :], right
                )


def solve_rows(blocks, rows, scale, atom_owner, sums, rayleigh):
    return pl.pallas_call(
        functools.partial(solve_kernel, scale),
        out_shape=(
            jax.ShapeDtypeStruct((8, ROWS, 128), jnp.float32),
            jax.ShapeDtypeStruct((OWN_CAP, PROJ, 128), jnp.float32),
            jax.ShapeDtypeStruct((1, 128), jnp.float32),
        ),
        in_specs=[pl.BlockSpec(memory_space=pltpu.SMEM)] + [WHOLE] * 4,
        out_specs=(WHOLE,) * 3,
        scratch_shapes=[
            pltpu.VMEM((8, 1024 + ROWS, 128), jnp.float32),
            pltpu.VMEM((1024 + ROWS, 256), jnp.bfloat16),
            pltpu.VMEM((128, 128), jnp.float32),
            pltpu.VMEM((128, 128), jnp.float32),
            pltpu.VMEM((128, 128), jnp.float32),
        ],
        compiler_params=pltpu.CompilerParams(vmem_limit_bytes=62 * 1024 * 1024),
    )(atom_owner, blocks, rows, sums, rayleigh)


WINDOW = 2 * REACH + 1
TILE = 8
LINES = SIDE * DEG + 1
PLANE = LINES * LINES
HALO = 368
PADDED = EDGE * EDGE * TILE


def cell_peer(index):
    return {"xl": index // 16, "z": (index // 2) % 8, "core": index % 2}


def thrice(left, right, dims):
    lh, ll = left
    rh, rl = right
    dot = functools.partial(
        lax.dot_general, dimension_numbers=(dims, ((), ())), preferred_element_type=jnp.float32
    )
    return dot(lh, rh) + dot(ll, rh) + dot(lh, rl)


def cube_root(x):
    root = jnp.exp(jnp.log(x) * (1.0 / 3.0))
    for _ in range(2):
        root = root - (root * root * root - x) / (3.0 * root * root)
    return root


def trial_kernel(
    scale_ref, atom_ref, cell_ref,
    c_in, occ_in, ext_in, core_in, stiff_in, proj_in, coup_in,
    rows_ref, ray_ref, sums_ref, total_ref,
    hot_ref, c_ref, occ_ref, ext_ref, core_ref, stiff_ref, proj_ref, coup_ref, pick_ref, load_sem,
    halo_ref, tile_ref, value_ref, image_ref, top_ref, under_ref, proj24_ref,
    give_ref, take_ref, used_ref, window_ref, dens_ref, ray_all_ref, pot_ref,
    halo_sem, dens_send, dens_recv, give_send, give_recv, used_send, used_recv,
    top_sem, ray_send, ray_recv, sums_send, sums_recv,
    pad_ref, now_ref, move_ref, rays_ref, early_sem, body_sem, edge_sem, share_sem,
    gram_ref, left_ref, right_ref, *total_scratch,
):
    nodes = c_ref.shape[0]
    here = lax.axis_index("xl") * 16 + lax.axis_index("z") * 2 + lax.axis_index("core")
    me = my_orb()
    barrier = pltpu.get_barrier_semaphore()
    peers = [cell_peer((here + r) % 32) for r in range(1, 32)]
    peers += [orb_peer((me + r) % 8) for r in range(1, 8)]
    for peer in peers:
        pl.semaphore_signal(barrier, inc=1, device_id=peer, device_id_type=MESH_ID)
    loads = [
        pltpu.make_async_copy(source, target, load_sem.at[i])
        for i, (source, target) in enumerate(
            (
                (stiff_in, stiff_ref), (proj_in, proj_ref), (coup_in, coup_ref), (c_in, c_ref),
                (occ_in, occ_ref), (ext_in, ext_ref), (core_in, core_ref),
            )
        )
    ]
    for load in loads:
        load.start()
    for load in loads[3:]:
        load.wait()
    current = c_ref[...]
    pad_ref[0:nodes, :] = current
    pad_ref[nodes:8 * ROWS, :] = jnp.zeros((8 * ROWS - nodes, 128), jnp.float32)
    pl.semaphore_wait(barrier, len(peers))
    halo = remote(
        c_ref.at[pl.ds(0, HALO)], halo_ref, halo_sem.at[0], halo_sem.at[1], cell_peer((here + 31) % 32)
    )
    halo.start()
    square = current * current
    density = thrice(split(jnp.broadcast_to(occ_ref[...].reshape(1, 128), (TILE, 128))), split(square), ((1,), (1,)))
    dens_ref[0] = density[0:1, :]
    dens_copies = []
    for r in range(1, 8):
        peer = (me + r) % 8
        copy = remote(dens_ref.at[0], dens_ref.at[r], dens_send.at[r], dens_recv.at[r], orb_peer(peer))
        copy.start()
        dens_copies.append(copy)

    order = (6, 2, 5, 3, 7, 1, 4)

    def edge(index):
        return pl.ds(pl.multiple_of(EDGE_ROWS * index, 8), EDGE_ROWS)

    def body(index):
        return pl.ds(pl.multiple_of(8 * EDGE_ROWS + BODY_ROWS * index, 8), BODY_ROWS)

    early = []
    for r in order:
        peer = (me + r) % 8
        for source, target, i in (
            (body(peer), pl.ds(EDGE_ROWS, BODY_ROWS), 0), (edge(peer), pl.ds(0, EDGE_ROWS), 2)
        ):
            copy = remote(
                pad_ref.at[source], now_ref.at[me, target], early_sem.at[i, r], early_sem.at[i + 1, r],
                orb_peer(peer),
            )
            copy.start()
            early.append(copy)
    now_ref[me, 0:EDGE_ROWS, :] = pad_ref[edge(me), :]
    now_ref[me, EDGE_ROWS:ROWS, :] = pad_ref[body(me), :]

    node = lax.broadcasted_iota(jnp.int32, (CELL_NODES, PADDED), 0)
    place = lax.broadcasted_iota(jnp.int32, (CELL_NODES, PADDED), 1)
    inside = (place & 7) < EDGE
    match = node == EDGE * (place >> 3) + (place & 7)
    spot = jnp.where(inside & match, 1.0, 0.0).astype(jnp.bfloat16)
    dot = functools.partial(lax.dot_general, preferred_element_type=jnp.float32)

    def both_sides(part):
        wide = dot(part, spot, (((1,), (0,)), ((), ()))).astype(jnp.bfloat16)
        return dot(spot, wide, (((0,), (0,)), ((), ()))).astype(jnp.bfloat16)

    loads[0].wait()
    stiff = tuple(both_sides(part) for part in split(stiff_ref[...]))
    loads[1].wait()
    proj24_ref[...] = jnp.zeros_like(proj24_ref)
    for t in range(TOUCH_DEV):
        proj24_ref[24 * t:24 * t + PROJ, :] = proj_ref[t, :, 0, :]
    parts = split(proj24_ref[...])
    proj_rows = tuple(dot(p, spot, (((1,), (0,)), ((), ()))).astype(jnp.bfloat16) for p in parts)
    proj_cols = tuple(dot(spot, p, (((0,), (1,)), ((), ()))).astype(jnp.bfloat16) for p in parts)

    loads[2].wait()
    lane = lax.broadcasted_iota(jnp.int32, (PROJ, 64), 1)
    for m in range(ATOM_DEV):
        for p in range(PROJ):
            column = jnp.sum(jnp.where(lane == 2 * here + m, coup_ref[p], 0.0), axis=1, keepdims=True)
            pick_ref[m, p] = jnp.broadcast_to(column, (PROJ, 128))
    for t in range(TOUCH_DEV):
        for w in range(WINDOW * ATOM_DEV):
            atom = (2 * (here + w // ATOM_DEV + 32 - REACH) + w % ATOM_DEV) % 64
            gap = atom_ref[here * TOUCH_DEV + t] - atom
            hot_ref[w, t] = (1 - jnp.minimum(gap * gap, 1)).astype(jnp.float32)
        for c in range(SIDE * SIDE):
            gap = cell_ref[t] - c
            hot_ref[10 + c, t] = (1 - jnp.minimum(gap * gap, 1)).astype(jnp.float32)

    for a in range(DEG):
        for y in range(LINES):
            for s in range(SIDE):
                start = PLANE * a + LINES * y + DEG * s
                if start + TILE > nodes:
                    piece = jnp.concatenate(
                        [c_ref[start:nodes, :], jnp.zeros((start + TILE - nodes, 128), jnp.float32)], axis=0
                    )
                else:
                    piece = c_ref[start:start + TILE, :]
                tile_ref[s, a, TILE * y:TILE * (y + 1), :] = piece
    halo.wait_recv()
    for y in range(LINES):
        for s in range(SIDE):
            start = LINES * y + DEG * s
            tile_ref[s, DEG, TILE * y:TILE * (y + 1), :] = halo_ref[start:start + TILE, :]

    def cell_values(r):
        span = slice(DEG * TILE * r, DEG * TILE * r + EDGE * TILE)
        return [
            jnp.concatenate([tile_ref[s, a, span, :] for a in range(EDGE)], axis=0)
            for s in range(SIDE)
        ]

    contrib = [jnp.zeros((24, 128), jnp.float32) for _ in range(TOUCH_DEV)]
    for r in range(SIDE):
        wide = thrice(proj_rows, split(jnp.concatenate(cell_values(r), axis=1)), ((1,), (0,)))
        for t in range(TOUCH_DEV):
            for s in range(SIDE):
                part = wide[24 * t:24 * t + 24, 128 * s:128 * (s + 1)]
                contrib[t] = contrib[t] + hot_ref[10 + SIDE * r + s, t] * part
    for k in range(WINDOW):
        for m in range(ATOM_DEV):
            total = hot_ref[ATOM_DEV * k + m, 0] * contrib[0]
            for t in range(1, TOUCH_DEV):
                total = total + hot_ref[ATOM_DEV * k + m, t] * contrib[t]
            give_ref[k, m] = total[:PROJ]
    gives = {}
    for k in (0, 4, 1, 3):
        copy = remote(
            give_ref.at[k], take_ref.at[k], give_send.at[k], give_recv.at[k],
            cell_peer((here + k + 32 - REACH) % 32),
        )
        copy.start()
        gives[k] = copy

    value_ref[...] = jnp.zeros_like(value_ref)

    def add_value(r, wide):
        for s in range(SIDE):
            for a in range(EDGE):
                span = slice(DEG * TILE * r, DEG * TILE * r + EDGE * TILE)
                value_ref[s, a, span, :] = (
                    value_ref[s, a, span, :]
                    + wide[EDGE * TILE * a:EDGE * TILE * (a + 1), 128 * s:128 * (s + 1)]
                )

    for r in range(SIDE):
        wide = jnp.concatenate(
            [value * scale_ref[SIDE * r + s] for s, value in enumerate(cell_values(r))], axis=1
        )
        add_value(r, thrice(stiff, split(wide), ((1,), (0,))))

    for k in (0, 4, 1, 3):
        gives[k].wait_recv()
    useds = {}
    for m in range(ATOM_DEV):
        total = give_ref[REACH, m]
        for k in (0, 1, 3, 4):
            total = total + take_ref[k, m]
        sums_ref[here, m] = total
        for p in range(PROJ):
            used_ref[m, p:p + 1, :] = jnp.sum(pick_ref[m, p] * total, axis=0, keepdims=True)
        window_ref[REACH, m] = used_ref[m]
    for q in (0, 4, 1, 3):
        copy = remote(
            used_ref, window_ref.at[4 - q], used_send.at[4 - q], used_recv.at[4 - q],
            cell_peer((here + q + 32 - REACH) % 32),
        )
        copy.start()
        useds[4 - q] = copy

    for copy in dens_copies:
        copy.wait_recv()
    density = dens_ref[0]
    for r in range(1, 8):
        density = density + dens_ref[r]
    potential = ext_ref[...].reshape(1, nodes) - exchange_coef * cube_root(
        density + core_ref[...].reshape(1, nodes)
    )
    pot_ref[...] = dot(
        jnp.broadcast_to(potential, (TILE, nodes)),
        (lax.broadcasted_iota(jnp.int32, (TILE, 128), 0) == 0).astype(jnp.float32),
        (((0,), (0,)), ((), ())), precision=highest,
    )

    for k in (0, 4, 1, 3):
        useds[k].wait_recv()
    back = []
    for t in range(TOUCH_DEV):
        total = jnp.zeros((PROJ, 128), jnp.float32)
        for k in range(WINDOW):
            for m in range(ATOM_DEV):
                total = total + hot_ref[ATOM_DEV * k + m, t] * window_ref[k, m]
        back.append(jnp.concatenate([total, jnp.zeros((24 - PROJ, 128), jnp.float32)], axis=0))
    for r in range(SIDE):
        wide = jnp.concatenate(
            [
                jnp.concatenate(
                    [
                        hot_ref[10 + SIDE * r + s, t] * back[t]
                        for t in range(TOUCH_DEV)
                    ],
                    axis=0,
                )
                for s in range(SIDE)
            ],
            axis=1,
        )
        add_value(r, thrice(proj_cols, split(wide), ((1,), (0,))))

    top_ref[...] = jnp.zeros_like(top_ref)
    for y in range(LINES):
        for s in range(SIDE):
            start = LINES * y + DEG * s
            top_ref[start:start + TILE, :] = (
                top_ref[start:start + TILE, :] + value_ref[s, DEG, TILE * y:TILE * (y + 1), :]
            )
    top = remote(top_ref, under_ref, top_sem.at[0], top_sem.at[1], cell_peer((here + 1) % 32))
    top.start()

    current = c_ref[...]
    square = current * current
    numerator = jnp.sum(pot_ref[...] * square, axis=0, keepdims=True)
    for s in range(SIDE):
        for a in range(EDGE):
            numerator = numerator + jnp.sum(tile_ref[s, a] * value_ref[s, a], axis=0, keepdims=True)
    ray_all_ref[here, 0:1, :] = numerator
    ray_all_ref[here, 1:2, :] = jnp.sum(square, axis=0, keepdims=True)
    rays = []
    for r in range(1, 32):
        copy = remote(
            ray_all_ref.at[here], ray_all_ref.at[here], ray_send.at[r], ray_recv.at[r],
            cell_peer((here + r) % 32),
        )
        copy.start()
        rays.append(copy)

    image_ref[...] = jnp.zeros_like(image_ref)
    image_ref[0:nodes, :] = pot_ref[...] * current
    for a in range(DEG):
        for y in range(LINES):
            for s in range(SIDE):
                start = PLANE * a + LINES * y + DEG * s
                image_ref[start:start + TILE, :] = (
                    image_ref[start:start + TILE, :] + value_ref[s, a, TILE * y:TILE * (y + 1), :]
                )
    bodies = []
    for r in order:
        peer = (me + r) % 8
        copy = remote(
            image_ref.at[body(peer)], move_ref.at[me, pl.ds(EDGE_ROWS, BODY_ROWS)],
            body_sem.at[0, r], body_sem.at[1, r], orb_peer(peer),
        )
        copy.start()
        bodies.append(copy)
    move_ref[me, EDGE_ROWS:ROWS, :] = image_ref[body(me), :]
    top.wait_recv()
    image_ref[0:PLANE, :] = image_ref[0:PLANE, :] + under_ref[0:PLANE, :]
    edges = []
    for r in order:
        peer = (me + r) % 8
        copy = remote(
            image_ref.at[edge(peer)], move_ref.at[me, pl.ds(0, EDGE_ROWS)],
            edge_sem.at[0, r], edge_sem.at[1, r], orb_peer(peer),
        )
        copy.start()
        edges.append(copy)
    move_ref[me, 0:EDGE_ROWS, :] = image_ref[edge(me), :]
    for copy in rays:
        copy.wait_recv()
    total = jnp.sum(ray_all_ref[...], axis=0)
    rayleigh = total[0:1, :] / (total[1:2, :] + tiny)
    ray_ref[...] = rayleigh
    rays_ref[me] = rayleigh
    shares = []
    for r in order:
        copy = remote(
            rays_ref.at[me], rays_ref.at[me], share_sem.at[0, r], share_sem.at[1, r],
            orb_peer((me + r) % 8),
        )
        copy.start()
        shares.append(copy)
    sums = []
    for r in range(1, 16):
        copy = remote(
            sums_ref.at[here], sums_ref.at[here], sums_send.at[r], sums_recv.at[r],
            site_peer((my_site() + r) % 16),
        )
        copy.start()
        sums.append(copy)
    for copy in early + shares + bodies + edges:
        copy.wait_recv()
    for j in range(8):
        now = now_ref[j]
        rows_ref[j] = now - step_size * (move_ref[j] - rays_ref[j] * now)
    gram(rows_ref, gram_ref, left_ref, right_ref)
    core = lax.axis_index("core")
    passed = []
    for r in range(16):
        if r:
            sums[r - 1].wait_recv()
        held = sums_ref.at[2 * ((my_site() + 16 - r) % 16) + core]
        copy = remote(held, held, sums_send.at[16 + r], sums_recv.at[16 + r], {"core": 1 - core})
        copy.start()
        passed.append(copy)
    everything = total_over_all(gram_ref, total_ref, *total_scratch)
    for copy in passed:
        copy.wait_recv()
    everything += passed
    everything += [halo, top] + dens_copies + list(gives.values()) + list(useds.values()) + rays
    for copy in everything + early + shares + bodies + edges + sums:
        copy.wait_send()


def trial_rows(
    orbitals, occupations, external, core_density, cell_scale, stiffness,
    touched_atom, touched_cells, projectors, coupling, collective_id,
):
    nodes = orbitals.shape[0]
    scalars = pl.BlockSpec(memory_space=pltpu.SMEM)
    dma = lambda *n: pltpu.SemaphoreType.DMA(n)
    vmem = lambda *shape: pltpu.VMEM(shape, jnp.float32)
    return pl.pallas_call(
        trial_kernel,
        out_shape=(
            jax.ShapeDtypeStruct((8, ROWS, 128), jnp.float32),
            jax.ShapeDtypeStruct((1, 128), jnp.float32),
            jax.ShapeDtypeStruct((32, ATOM_DEV, PROJ, 128), jnp.float32),
            jax.ShapeDtypeStruct((36 * 128, 128), jnp.float32),
        ),
        in_specs=[scalars] * 3 + [pl.BlockSpec(memory_space=pltpu.HBM)] * 7,
        out_specs=(WHOLE,) * 4,
        scratch_shapes=[
            pltpu.SMEM((19, TOUCH_DEV), jnp.float32),
            vmem(nodes, 128), vmem(128), vmem(nodes), vmem(nodes), vmem(CELL_NODES, CELL_NODES),
            vmem(TOUCH_DEV, PROJ, 1, CELL_NODES), vmem(PROJ, PROJ, 64), vmem(ATOM_DEV, PROJ, PROJ, 128),
            dma(7),
            vmem(HALO, 128),
            vmem(SIDE, EDGE, LINES * TILE, 128),
            vmem(SIDE, EDGE, LINES * TILE, 128),
            vmem(8 * ROWS, 128),
            vmem(HALO, 128),
            vmem(HALO, 128),
            vmem(24 * TOUCH_DEV, CELL_NODES),
            vmem(WINDOW, ATOM_DEV, PROJ, 128),
            vmem(WINDOW, ATOM_DEV, PROJ, 128),
            vmem(ATOM_DEV, PROJ, 128),
            vmem(WINDOW, ATOM_DEV, PROJ, 128),
            vmem(8, 1, nodes),
            vmem(32, 2, 128),
            vmem(nodes, 128),
            dma(2), dma(8), dma(8), dma(5), dma(5), dma(5), dma(5),
            dma(2), dma(32), dma(32), dma(32), dma(32),
            vmem(8 * ROWS, 128), vmem(8, ROWS, 128), vmem(8, ROWS, 128), vmem(8, 1, 128),
            dma(4, 8), dma(2, 8), dma(2, 8), dma(2, 8),
            vmem(36 * 128, 128),
            pltpu.VMEM((3 * ROWS, 1024), jnp.bfloat16),
            pltpu.VMEM((3 * ROWS, 1024), jnp.bfloat16),
            vmem(18 * 128, 128), vmem(18 * 128, 128),
            vmem(8, ORB_PIECE, 128), vmem(ORB_PIECE, 128), vmem(16, ORB_SLOT, 128),
            vmem(16, ORB_SLOT, 128), vmem(16, ORB_SLOT, 128),
            vmem(8, SITE_SLOT, 128), vmem(SITE_PIECE, 128), vmem(8, SITE_SLOT, 128),
            vmem(16, SITE_PIECE, 128), vmem(8, SITE_SLOT, 128),
            dma(2, 9), dma(2, 8), dma(2, 16), dma(2, 16), dma(2, 8), dma(2, 8),
            dma(2, 8), dma(2, 16), dma(2, 8), dma(2, 16), dma(2, 16),
        ],
        compiler_params=pltpu.CompilerParams(
            collective_id=collective_id, has_side_effects=True, vmem_limit_bytes=62 * 1024 * 1024
        ),
    )(
        cell_scale, touched_atom, touched_cells.reshape(-1), orbitals, occupations,
        external, core_density, stiffness, projectors.transpose(0, 2, 1, 3), coupling.transpose(1, 2, 0),
    )


def per_device(
    orbitals,
    occupations,
    external,
    core_density,
    cell_scale,
    stiffness,
    touched_atom,
    touched_cells,
    projectors,
    coupling,
    atom_owner,
):
    nodes = orbitals.shape[0]
    rows, rayleigh, sums, blocks = trial_rows(
        orbitals, occupations, external, core_density, cell_scale, stiffness,
        touched_atom, touched_cells, projectors, coupling, 1,
    )
    solved, owned, rayleigh = solve_rows(
        blocks.reshape(36, 128, 128), rows, 1.0 / (nodes * 32), atom_owner.reshape(-1), sums, rayleigh
    )
    return (rows_back(solved, nodes, 2), rayleigh.reshape(-1), owned)


def solution(mesh):
    finer = Mesh(mesh.devices.reshape(2, 8, 2, 2, 4), ("xl", "z", "core", "xh", "y"))
    return jax.shard_map(
        per_device,
        mesh=finer,
        in_specs=(
            P(CELLS, ORBS),
            P(ORBS),
            P(CELLS),
            P(CELLS),
            P(CELLS),
            P(),
            P(),
            P(CELLS, None),
            P(CELLS, None, None, None),
            P(),
            P(),
        ),
        out_specs=(P(CELLS, ORBS), P(ORBS), P(CELLS, None, ORBS)),
        check_vma=False,
    )
```
